256 devices in a mesh: tm: 128 (over z, x, y_hi, core), sec: 2 (over y_lo).
Axes of the slice: x: 4, y: 4 (y_hi: 2, y_lo: 2; y = y_hi * 2 + y_lo), z: 8, core: 2. Of those that a mesh axis runs over, the one named last changes fastest.
Arguments:
- state: float32 [512, 6, 4, 32, 128], P('tm', None, None, 'sec'), may hold values from 0.05 to 1
- adjoint: float32 [512, 6, 4, 32, 128], P('tm', None, None, 'sec'), may hold values from -6 to 6
- plan: int32 [512, 4], P('tm'), may hold values from 1 to 3
- valve: int32 [512, 4], P('tm'), may hold values 0 or 1
Outputs:
- residual: float32 [512, 6, 4, 32, 128], P('tm', None, None, 'sec')
- adjoint_out: float32 [512, 6, 4, 32, 128], P('tm', None, None, 'sec')
The draws below stay inside these ranges and needn't reach their ends.
Inputs may be any that keep to these rules, and one draw needn't show every extreme that they name: Bed b at instance t takes purge gas from bed (b + plan) mod 4, never from itself.
All inputs are finite; a program needn't handle non-finite values. No bound on the sum of `valve` on one device may be relied on, other than what follows from the above.
Results may differ from the reference program's by a relative error of at most 0.0003.
Values sent between devices are 32-bit elements; how exact they have to be, the bound alone decides.
A program may use at most 64 MiB of HBM per device.

```python
import jax
import jax.numpy as jnp
from jax import lax

I_DEV = 4
NR = 128
BEDS = 4
COMP = 6
NT = 512
NZ = 32


def with_ends(values, key, low, largest):
    shape = values.shape
    place = [jax.random.randint(jax.random.fold_in(key, axis), (), 0, shape[axis]) for axis in range(len(shape))]
    values = values.at[tuple(place)].set(low)
    longest = shape.index(max(shape))
    place[longest] = (place[longest] + 1) % shape[longest]
    return values.at[tuple(place)].set(largest)


def steps_of(rng, extent, cuts, low, high):
    def one(axis_at, parts):
        draws = jax.random.uniform(jax.random.fold_in(jax.random.fold_in(rng, 6), axis_at), (parts,), jnp.float32, low / len(cuts), high / len(cuts))
        return jnp.repeat(jnp.exp(draws), extent[axis_at] // parts).reshape((-1,) + (1,) * (len(extent) - axis_at - 1))

    factor_of = one(*cuts[0])
    for cut in cuts[1:]:
        factor_of = factor_of * one(*cut)
    return factor_of


def bell_draw(own_key, dims, scale, bound, shards=(), kind=jnp.bfloat16):
    factor_of = steps_of(own_key, dims, shards, -0.22, 0.18) if shards else 1.0
    array = jax.random.normal(own_key, dims, jnp.float32) * scale * factor_of
    return jnp.minimum(jnp.maximum(array, -bound), bound).astype(kind)


def setup_inputs(seed: int = 0) -> dict:
    key_of = jax.random.split(jax.random.key(seed), 5)
    state = jnp.clip(0.05 + 0.95 * jax.random.uniform(key_of[0], (NT, COMP, BEDS, NZ, NR), jnp.float32) ** steps_of(key_of[0], (NT, COMP, BEDS, NZ, NR), ((0, 128), (3, 2)), -0.2, 0.2), 0.05, 1.0)
    adjoint = bell_draw(key_of[1], (NT, COMP, BEDS, NZ, NR), 1.0, 6.0, ((0, 128), (3, 2)), jnp.float32)
    plan = with_ends(jax.random.randint(key_of[2], (NT, BEDS), 1, BEDS), jax.random.fold_in(key_of[2], 1), 1, BEDS - 1).astype(jnp.int32)
    valve = with_ends((jax.random.randint(key_of[3], (NT, BEDS), 0, 2) < 1).astype(jnp.int32), jax.random.fold_in(key_of[3], 1), 0, 1)
    return dict(state=state, adjoint=adjoint, plan=plan, valve=valve)


STENCIL = (0.8, -0.2, 4.0 / 105.0, -1.0 / 280.0)
TIME_SCALE = 4.0
FLOW_VELOCITY = 1.0
AXIAL_DISPERSION = 0.3
RADIAL_SPREADING = 0.2
BINDING_STRENGTH = (1.5, 0.6)
HEAT_EXPONENT = (0.5, 0.3)
KINETIC = (1.2, 0.7)
CAPACITY = (2.0, 1.0)
SORPTION_HEAT = (0.4, 0.25)
PURGE_GAIN = 1.5

def radial_diffusion_term(field):
    zero_edge = jnp.zeros_like(field[..., :1])
    upper = jnp.concatenate([field[..., 1:], zero_edge], axis=-1)
    lower = jnp.concatenate([zero_edge, field[..., :-1]], axis=-1)
    return upper - 2.0 * field + lower

def time_derivative(extended, instances):
    total_sum = jnp.zeros_like(extended[4:4 + instances])
    for offset, weight in enumerate(STENCIL):
        shift_by = offset + 1
        total_sum = total_sum + weight * (extended[4 + shift_by:4 + shift_by + instances] - extended[4 - shift_by:4 - shift_by + instances])
    return TIME_SCALE * total_sum

def spatial_residual(padded, offsets, valves, purge_mask):
    middle_cell = padded[:, :, :, 1:-1]
    cell_underneath = padded[:, :, :, :-2]
    cell_overhead = padded[:, :, :, 2:]
    gas_part = middle_cell[:, 0:3]
    transport = FLOW_VELOCITY * (gas_part - cell_underneath[:, 0:3]) - AXIAL_DISPERSION * (cell_overhead[:, 0:3] - 2.0 * gas_part + cell_underneath[:, 0:3])
    gas_res = transport - RADIAL_SPREADING * radial_diffusion_term(gas_part)
    thermal_field = middle_cell[:, 5]
    binding_first = BINDING_STRENGTH[0] * jnp.exp(HEAT_EXPONENT[0] * thermal_field)
    binding_second = BINDING_STRENGTH[1] * jnp.exp(HEAT_EXPONENT[1] * thermal_field)
    denominator = 1.0 + binding_first * middle_cell[:, 0] + binding_second * middle_cell[:, 1]
    uptake_first = KINETIC[0] * (CAPACITY[0] * binding_first * middle_cell[:, 0] / denominator - middle_cell[:, 3])
    uptake_second = KINETIC[1] * (CAPACITY[1] * binding_second * middle_cell[:, 1] / denominator - middle_cell[:, 4])
    bed_count = padded.shape[2]
    bed_ids = jnp.arange(bed_count, dtype=jnp.int32)
    product = lax.optimization_barrier(jnp.sum(gas_part * purge_mask[None, None, None, :, None], axis=3))
    source = (bed_ids[None, :] + offsets) % bed_count
    lookup_table = (source[:, :, None] == bed_ids[None, None, :]).astype(jnp.float32)
    incoming = lax.optimization_barrier(jnp.sum(lookup_table[:, None, :, :, None] * product[:, :, None, :, :], axis=3))
    purge_term = PURGE_GAIN * valves.astype(jnp.float32)[:, None, :, None] * (product - incoming)
    gas_res = gas_res + purge_term[:, :, :, None, :] * purge_mask[None, None, None, :, None]
    energy_residual = FLOW_VELOCITY * (thermal_field - cell_underneath[:, 5]) - AXIAL_DISPERSION * (cell_overhead[:, 5] - 2.0 * thermal_field + cell_underneath[:, 5])
    energy_residual = energy_residual - RADIAL_SPREADING * radial_diffusion_term(thermal_field) - (SORPTION_HEAT[0] * uptake_first + SORPTION_HEAT[1] * uptake_second)
    rows = [gas_res[:, 0] + uptake_first, gas_res[:, 1] + uptake_second, gas_res[:, 2], -uptake_first, -uptake_second, energy_residual]
    return jnp.stack(rows, axis=1)

def reference(state, adjoint, plan, valve):
    instance_total = state.shape[0]
    state_ext = jnp.concatenate([state[-4:], state, state[:4]], axis=0)
    adjoint_ext = jnp.concatenate([adjoint[-4:], adjoint, adjoint[:4]], axis=0)
    purge_mask = (jnp.arange(NZ, dtype=jnp.int32) == NZ - 1).astype(jnp.float32)
    block_count = instance_total // I_DEV

    def per_block(block_index):
        first_row = block_index * I_DEV
        state_block = lax.dynamic_slice_in_dim(state_ext, first_row, I_DEV + 8, 0)
        adjoint_block = lax.dynamic_slice_in_dim(adjoint_ext, first_row, I_DEV + 8, 0)
        offsets = lax.dynamic_slice_in_dim(plan, first_row, I_DEV, 0)
        valves = lax.dynamic_slice_in_dim(valve, first_row, I_DEV, 0)
        middle_cell = state_block[4:4 + I_DEV]
        multiplier = adjoint_block[4:4 + I_DEV]
        padded = jnp.pad(middle_cell, ((0, 0), (0, 0), (0, 0), (1, 1), (0, 0)))
        forward, pullback = jax.vjp(lambda field: spatial_residual(field, offsets, valves, purge_mask), padded)
        pulled = pullback(multiplier)[0][:, :, :, 1:-1]
        return (time_derivative(state_block, I_DEV) + forward, pulled - time_derivative(adjoint_block, I_DEV))
    residual_out, adjoint_res = lax.map(per_block, jnp.arange(block_count, dtype=jnp.int32))
    return (residual_out.reshape(state.shape), adjoint_res.reshape(state.shape))
```

```python
import jax
import jax.numpy as jnp
from jax import lax
from jax.experimental import pallas as pl
from jax.experimental.pallas import tpu as pltpu
from jax.sharding import PartitionSpec as P

STENCIL = (0.8, -0.2, 4.0 / 105.0, -1.0 / 280.0)
TIME_SCALE = 4.0
FLOW_VELOCITY = 1.0
AXIAL_DISPERSION = 0.3
RADIAL_SPREADING = 0.2
BINDING_STRENGTH = (1.5, 0.6)
HEAT_EXPONENT = (0.5, 0.3)
KINETIC = (1.2, 0.7)
CAPACITY = (2.0, 1.0)
SORPTION_HEAT = (0.4, 0.25)
PURGE_GAIN = 1.5

MESH = pl.DeviceIdType.MESH


def _kernel(n_tm, tbl, st, ad, res, adj, rl_st, rr_st, rl_ad, rr_ad, h_st, h_ad, send, recv):
    inst, comp, beds, nz, nr = st.shape
    me = lax.axis_index("tm")
    sec = lax.axis_index("sec")
    right = lax.rem(me + 1, n_tm)
    left = lax.rem(me + n_tm - 1, n_tm)
    partner = 1 - sec

    barrier = pltpu.get_barrier_semaphore()
    for dev in ((left, sec), (right, sec), (me, partner)):
        pl.semaphore_signal(barrier, inc=1, device_id=dev, device_id_type=MESH)
    pl.semaphore_wait(barrier, 3)

    row_src = (nz - 1) * (1 - sec)
    halo_copies = []
    for i, (src, dst) in enumerate(((st, h_st), (ad, h_ad))):
        cp = pltpu.make_async_remote_copy(
            src_ref=src.at[:, :, :, pl.ds(row_src, 1), :],
            dst_ref=dst.at[:, :, :, pl.ds(0, 1), :],
            send_sem=send.at[4 + i],
            recv_sem=recv.at[4 + i],
            device_id=(me, partner),
            device_id_type=MESH,
        )
        cp.start()
        halo_copies.append(cp)
    big = []
    for i, (src, dst, dev) in enumerate(
        ((st, rl_st, right), (st, rr_st, left), (ad, rl_ad, right), (ad, rr_ad, left))
    ):
        cp = pltpu.make_async_remote_copy(
            src_ref=src,
            dst_ref=dst,
            send_sem=send.at[i],
            recv_sem=recv.at[i],
            device_id=(dev, sec),
            device_id_type=MESH,
        )
        cp.start()
        big.append(cp)

    for cp in halo_copies:
        cp.wait()

    sec_f = sec.astype(jnp.float32)
    row = lax.broadcasted_iota(jnp.int32, (nz, nr), 0)
    lane = lax.broadcasted_iota(jnp.int32, (nz, nr), 1)
    first_row = row == 0
    last_row = row == nz - 1
    first_lane = lane == 0
    last_lane = lane == nr - 1

    def radial(x):
        lower = jnp.where(first_lane, 0.0, pltpu.roll(x, 1, 1))
        upper = jnp.where(last_lane, 0.0, pltpu.roll(x, nr - 1, 1))
        return upper - 2.0 * x + lower

    def axial(x, below, above):
        zm = jnp.where(first_row, below, pltpu.roll(x, 1, 0))
        zp = jnp.where(last_row, above, pltpu.roll(x, nz - 1, 0))
        return zm, zp

    def transport(x, below, above):
        zm, zp = axial(x, below, above)
        out = FLOW_VELOCITY * (x - zm) - AXIAL_DISPERSION * (zp - 2.0 * x + zm)
        return out - RADIAL_SPREADING * radial(x)

    def transport_t(lam, below, above):
        lm, lp = axial(lam, below, above)
        out = FLOW_VELOCITY * (lam - lp) - AXIAL_DISPERSION * (lm - 2.0 * lam + lp)
        return out - RADIAL_SPREADING * radial(lam)

    def spatial_body(t, carry):
        for b in range(beds):
            x = [st[t, c, b] for c in range(comp)]
            lam = [ad[t, c, b] for c in range(comp)]
            hs = [h_st[t, c, b, 0:1, :] for c in range(comp)]
            ha = [h_ad[t, c, b, 0:1, :] for c in range(comp)]
            y1, y2, y3, q1, q2, temp = x
            b1 = BINDING_STRENGTH[0] * jnp.exp(HEAT_EXPONENT[0] * temp)
            b2 = BINDING_STRENGTH[1] * jnp.exp(HEAT_EXPONENT[1] * temp)
            den = 1.0 + b1 * y1 + b2 * y2
            p1 = b1 * y1 / den
            p2 = b2 * y2 / den
            rate1 = KINETIC[0] * (CAPACITY[0] * p1 - q1)
            rate2 = KINETIC[1] * (CAPACITY[1] * p2 - q2)
            tr = {}
            trt = {}
            for c in (0, 1, 2, 5):
                below = hs[c] * sec_f
                above = hs[c] * (1.0 - sec_f)
                tr[c] = transport(x[c], below, above)
                lbelow = ha[c] * sec_f
                labove = ha[c] * (1.0 - sec_f)
                trt[c] = transport_t(lam[c], lbelow, labove)
            res[t, 0, b] = tr[0] + rate1
            res[t, 1, b] = tr[1] + rate2
            res[t, 2, b] = tr[2]
            res[t, 3, b] = -rate1
            res[t, 4, b] = -rate2
            res[t, 5, b] = tr[5] - (SORPTION_HEAT[0] * rate1 + SORPTION_HEAT[1] * rate2)
            mu1 = lam[0] - lam[3] - SORPTION_HEAT[0] * lam[5]
            mu2 = lam[1] - lam[4] - SORPTION_HEAT[1] * lam[5]
            n1 = (KINETIC[0] * CAPACITY[0]) * mu1
            n2 = (KINETIC[1] * CAPACITY[1]) * mu2
            cden = -(n1 * p1 + n2 * p2) / den
            cu1 = n1 / den + cden
            cu2 = n2 / den + cden
            adj[t, 0, b] = trt[0] + b1 * cu1
            adj[t, 1, b] = trt[1] + b2 * cu2
            adj[t, 2, b] = trt[2]
            adj[t, 3, b] = -KINETIC[0] * mu1
            adj[t, 4, b] = -KINETIC[1] * mu2
            adj[t, 5, b] = trt[5] + (HEAT_EXPONENT[0] * y1 * b1 * cu1 + HEAT_EXPONENT[1] * y2 * b2 * cu2)
        return carry

    lax.fori_loop(0, inst, spatial_body, 0)

    @pl.when(sec == 1)
    def _():
        def purge_body(t, carry):
            base = t * (beds * beds)
            for c in range(3):
                ys = [st[t, c, b, nz - 1 : nz, :] for b in range(beds)]
                ls = [ad[t, c, b, nz - 1 : nz, :] for b in range(beds)]
                for b in range(beds):
                    gain = tbl[beds * beds * inst + t * beds + b]
                    inc = tbl[base + b * beds] * ys[0]
                    for bp in range(1, beds):
                        inc = inc + tbl[base + b * beds + bp] * ys[bp]
                    res[t, c, b, nz - 1 : nz, :] = res[t, c, b, nz - 1 : nz, :] + gain * (ys[b] - inc)
                    back = gain * ls[b]
                    for bb in range(beds):
                        w = tbl[base + bb * beds + b] * tbl[beds * beds * inst + t * beds + bb]
                        back = back - w * ls[bb]
                    adj[t, c, b, nz - 1 : nz, :] = adj[t, c, b, nz - 1 : nz, :] + back
            return carry

        lax.fori_loop(0, inst, purge_body, 0)

    for cp in big:
        cp.wait()

    def pick(own, lft, rgt, j, c):
        if j < 0:
            return lft[j + inst, c]
        if j >= inst:
            return rgt[j - inst, c]
        return own[j, c]

    def time_body(c, carry):
        for t in range(inst):
            acc_s = None
            acc_a = None
            for k, w in enumerate(STENCIL):
                s = k + 1
                ds = w * (pick(st, rl_st, rr_st, t + s, c) - pick(st, rl_st, rr_st, t - s, c))
                da = w * (pick(ad, rl_ad, rr_ad, t + s, c) - pick(ad, rl_ad, rr_ad, t - s, c))
                acc_s = ds if acc_s is None else acc_s + ds
                acc_a = da if acc_a is None else acc_a + da
            res[t, c] = TIME_SCALE * acc_s + res[t, c]
            adj[t, c] = adj[t, c] - TIME_SCALE * acc_a
        return carry

    lax.fori_loop(0, comp, time_body, 0)


def local(state, adjoint, plan, valve):
    n_tm = lax.axis_size("tm")
    inst, comp, beds, nz, nr = state.shape
    bed_ids = jnp.arange(beds, dtype=jnp.int32)
    source = (bed_ids[None, :] + plan) % beds
    onehot = (source[:, :, None] == bed_ids[None, None, :]).astype(jnp.float32)
    gain = PURGE_GAIN * valve.astype(jnp.float32)
    tbl = jnp.concatenate([onehot.reshape(-1), gain.reshape(-1)])
    block = jax.ShapeDtypeStruct(state.shape, jnp.float32)
    vmem = pl.BlockSpec(memory_space=pltpu.VMEM)
    halo_shape = (inst, comp, beds, 8, nr)

    def kern(*refs):
        _kernel(n_tm, *refs)

    res, adj = pl.pallas_call(
        kern,
        out_shape=(block, block),
        in_specs=[pl.BlockSpec(memory_space=pltpu.SMEM), vmem, vmem],
        out_specs=(vmem, vmem),
        scratch_shapes=[pltpu.VMEM(state.shape, jnp.float32)] * 4
        + [pltpu.VMEM(halo_shape, jnp.float32)] * 2
        + [pltpu.SemaphoreType.DMA((6,)), pltpu.SemaphoreType.DMA((6,))],
        compiler_params=pltpu.CompilerParams(collective_id=0, has_side_effects=True),
    )(tbl, state, adjoint)
    return res, adj


def solution(mesh):
    return jax.shard_map(
        local,
        mesh=mesh,
        in_specs=(
            P("tm", None, None, "sec", None),
            P("tm", None, None, "sec", None),
            P("tm", None),
            P("tm", None),
        ),
        out_specs=(P("tm", None, None, "sec", None), P("tm", None, None, "sec", None)),
        check_vma=False,
    )
```

```python
import jax
import jax.numpy as jnp
from jax import lax
from jax.experimental import pallas as pl
from jax.experimental.pallas import tpu as pltpu
from jax.sharding import PartitionSpec as P

STENCIL = (0.8, -0.2, 4.0 / 105.0, -1.0 / 280.0)
TIME_SCALE = 4.0
FLOW_VELOCITY = 1.0
AXIAL_DISPERSION = 0.3
RADIAL_SPREADING = 0.2
BINDING_STRENGTH = (1.5, 0.6)
HEAT_EXPONENT = (0.5, 0.3)
KINETIC = (1.2, 0.7)
CAPACITY = (2.0, 1.0)
SORPTION_HEAT = (0.4, 0.25)
PURGE_GAIN = 1.5

MESH = pl.DeviceIdType.MESH


def _kernel(n_tm, tbl, st, ad, res, adj, rv_st, rv_ad, ry_st, ry_ad, h_st, h_ad, send, recv):
    inst, comp, beds, nz, nr = st.shape
    me = lax.axis_index("tm")
    sec = lax.axis_index("sec")
    core = lax.rem(me, 2)
    ring = lax.div(me, 4)
    y = lax.rem(lax.div(me, 2), 2) * 2 + sec

    def at(yy, cc):
        return (ring * 4 + lax.div(yy, 2) * 2 + cc, lax.rem(yy, 2))

    def up_of(dev):
        t, s = dev
        yy = lax.rem(lax.div(t, 2), 2) * 2 + s
        yy = lax.rem(yy + 1, 4)
        return (lax.div(t, 4) * 4 + lax.div(yy, 2) * 2 + lax.rem(t, 2), lax.rem(yy, 2))

    def dn_of(dev):
        t, s = dev
        yy = lax.rem(lax.div(t, 2), 2) * 2 + s
        yy = lax.rem(yy + 3, 4)
        return (lax.div(t, 4) * 4 + lax.div(yy, 2) * 2 + lax.rem(t, 2), lax.rem(yy, 2))

    def cross_of(dev):
        t, s = dev
        return (lax.rem(t + 2 * lax.rem(t, 2) - 1 + n_tm, n_tm), s)

    mine = (me, sec)
    pair = (me + 1 - 2 * core, sec)
    up = at(lax.rem(y + 1, 4), core)
    dn = at(lax.rem(y + 3, 4), core)
    fwd_st = cross_of(dn)
    fwd_ad = cross_of(up)
    cross = cross_of(mine)
    from_st = up_of(cross)
    from_ad = dn_of(cross)
    partner = (me, 1 - sec)

    barrier = pltpu.get_barrier_semaphore()
    for dev in (pair, up, dn, fwd_st, fwd_ad, from_st, from_ad):
        pl.semaphore_signal(barrier, inc=1, device_id=dev, device_id_type=MESH)
    pl.semaphore_wait(barrier, 7)

    def rcopy(src, dst, i, dev):
        cp = pltpu.make_async_remote_copy(
            src_ref=src, dst_ref=dst, send_sem=send.at[i], recv_sem=recv.at[i],
            device_id=dev, device_id_type=MESH,
        )
        cp.start()
        return cp

    row_src = (nz - 1) * (1 - sec)
    halo_copies = [
        rcopy(src.at[:, :, :, pl.ds(row_src, 1), :], dst.at[:, :, :, pl.ds(0, 1), :], 4 + i, partner)
        for i, (src, dst) in enumerate(((st, h_st), (ad, h_ad)))
    ]
    leg_st = rcopy(st, ry_st, 0, up)
    leg_ad = rcopy(ad, ry_ad, 1, dn)
    near_st = rcopy(st, rv_st.at[core], 2, pair)
    near_ad = rcopy(ad, rv_ad.at[core], 3, pair)

    for cp in halo_copies:
        cp.wait()

    sec_f = sec.astype(jnp.float32)
    row = lax.broadcasted_iota(jnp.int32, (nz, nr), 0)
    lane = lax.broadcasted_iota(jnp.int32, (nz, nr), 1)
    first_row = row == 0
    last_row = row == nz - 1
    first_lane = lane == 0
    last_lane = lane == nr - 1

    def radial(x):
        lower = jnp.where(first_lane, 0.0, pltpu.roll(x, 1, 1))
        upper = jnp.where(last_lane, 0.0, pltpu.roll(x, nr - 1, 1))
        return upper - 2.0 * x + lower

    def axial(x, below, above):
        zm = jnp.where(first_row, below, pltpu.roll(x, 1, 0))
        zp = jnp.where(last_row, above, pltpu.roll(x, nz - 1, 0))
        return zm, zp

    def transport(x, below, above):
        zm, zp = axial(x, below, above)
        out = FLOW_VELOCITY * (x - zm) - AXIAL_DISPERSION * (zp - 2.0 * x + zm)
        return out - RADIAL_SPREADING * radial(x)

    def transport_t(lam, below, above):
        lm, lp = axial(lam, below, above)
        out = FLOW_VELOCITY * (lam - lp) - AXIAL_DISPERSION * (lm - 2.0 * lam + lp)
        return out - RADIAL_SPREADING * radial(lam)

    def spatial_body(t, carry):
        for b in range(beds):
            x = [st[t, c, b] for c in range(comp)]
            lam = [ad[t, c, b] for c in range(comp)]
            hs = [h_st[t, c, b, 0:1, :] for c in range(comp)]
            ha = [h_ad[t, c, b, 0:1, :] for c in range(comp)]
            y1, y2, y3, q1, q2, temp = x
            b1 = BINDING_STRENGTH[0] * jnp.exp(HEAT_EXPONENT[0] * temp)
            b2 = BINDING_STRENGTH[1] * jnp.exp(HEAT_EXPONENT[1] * temp)
            den = 1.0 + b1 * y1 + b2 * y2
            p1 = b1 * y1 / den
            p2 = b2 * y2 / den
            rate1 = KINETIC[0] * (CAPACITY[0] * p1 - q1)
            rate2 = KINETIC[1] * (CAPACITY[1] * p2 - q2)
            tr = {}
            trt = {}
            for c in (0, 1, 2, 5):
                below = hs[c] * sec_f
                above = hs[c] * (1.0 - sec_f)
                tr[c] = transport(x[c], below, above)
                lbelow = ha[c] * sec_f
                labove = ha[c] * (1.0 - sec_f)
                trt[c] = transport_t(lam[c], lbelow, labove)
            res[t, 0, b] = tr[0] + rate1
            res[t, 1, b] = tr[1] + rate2
            res[t, 2, b] = tr[2]
            res[t, 3, b] = -rate1
            res[t, 4, b] = -rate2
            res[t, 5, b] = tr[5] - (SORPTION_HEAT[0] * rate1 + SORPTION_HEAT[1] * rate2)
            mu1 = lam[0] - lam[3] - SORPTION_HEAT[0] * lam[5]
            mu2 = lam[1] - lam[4] - SORPTION_HEAT[1] * lam[5]
            n1 = (KINETIC[0] * CAPACITY[0]) * mu1
            n2 = (KINETIC[1] * CAPACITY[1]) * mu2
            cden = -(n1 * p1 + n2 * p2) / den
            cu1 = n1 / den + cden
            cu2 = n2 / den + cden
            adj[t, 0, b] = trt[0] + b1 * cu1
            adj[t, 1, b] = trt[1] + b2 * cu2
            adj[t, 2, b] = trt[2]
            adj[t, 3, b] = -KINETIC[0] * mu1
            adj[t, 4, b] = -KINETIC[1] * mu2
            adj[t, 5, b] = trt[5] + (HEAT_EXPONENT[0] * y1 * b1 * cu1 + HEAT_EXPONENT[1] * y2 * b2 * cu2)
        return carry

    lax.fori_loop(0, inst, spatial_body, 0)

    @pl.when(sec == 1)
    def _():
        def purge_body(t, carry):
            base = t * (beds * beds)
            for c in range(3):
                ys = [st[t, c, b, nz - 1 : nz, :] for b in range(beds)]
                ls = [ad[t, c, b, nz - 1 : nz, :] for b in range(beds)]
                for b in range(beds):
                    gain = tbl[beds * beds * inst + t * beds + b]
                    inc = tbl[base + b * beds] * ys[0]
                    for bp in range(1, beds):
                        inc = inc + tbl[base + b * beds + bp] * ys[bp]
                    res[t, c, b, nz - 1 : nz, :] = res[t, c, b, nz - 1 : nz, :] + gain * (ys[b] - inc)
                    back = gain * ls[b]
                    for bb in range(beds):
                        w = tbl[base + bb * beds + b] * tbl[beds * beds * inst + t * beds + bb]
                        back = back - w * ls[bb]
                    adj[t, c, b, nz - 1 : nz, :] = adj[t, c, b, nz - 1 : nz, :] + back
            return carry

        lax.fori_loop(0, inst, purge_body, 0)

    leg_st.wait_recv()
    on_st = rcopy(ry_st, rv_st.at[1 - core], 6, fwd_st)
    leg_ad.wait_recv()
    on_ad = rcopy(ry_ad, rv_ad.at[1 - core], 7, fwd_ad)
    for cp in (near_st, near_ad, on_st, on_ad):
        cp.wait_recv()

    def pick(own, recvd, j, c):
        if j < 0:
            return recvd[0, j + inst, c]
        if j >= inst:
            return recvd[1, j - inst, c]
        return own[j, c]

    def time_body(c, carry):
        for t in range(inst):
            acc_s = None
            acc_a = None
            for k, w in enumerate(STENCIL):
                s = k + 1
                ds = w * (pick(st, rv_st, t + s, c) - pick(st, rv_st, t - s, c))
                da = w * (pick(ad, rv_ad, t + s, c) - pick(ad, rv_ad, t - s, c))
                acc_s = ds if acc_s is None else acc_s + ds
                acc_a = da if acc_a is None else acc_a + da
            res[t, c] = TIME_SCALE * acc_s + res[t, c]
            adj[t, c] = adj[t, c] - TIME_SCALE * acc_a
        return carry

    lax.fori_loop(0, comp, time_body, 0)
    for cp in (leg_st, leg_ad, near_st, near_ad, on_st, on_ad):
        cp.wait_send()


def local(state, adjoint, plan, valve):
    n_tm = lax.axis_size("tm")
    inst, comp, beds, nz, nr = state.shape
    bed_ids = jnp.arange(beds, dtype=jnp.int32)
    source = (bed_ids[None, :] + plan) % beds
    onehot = (source[:, :, None] == bed_ids[None, None, :]).astype(jnp.float32)
    gain = PURGE_GAIN * valve.astype(jnp.float32)
    tbl = jnp.concatenate([onehot.reshape(-1), gain.reshape(-1)])
    block = jax.ShapeDtypeStruct(state.shape, jnp.float32)
    vmem = pl.BlockSpec(memory_space=pltpu.VMEM)
    halo_shape = (inst, comp, beds, 8, nr)

    def kern(*refs):
        _kernel(n_tm, *refs)

    res, adj = pl.pallas_call(
        kern,
        out_shape=(block, block),
        in_specs=[pl.BlockSpec(memory_space=pltpu.SMEM), vmem, vmem],
        out_specs=(vmem, vmem),
        scratch_shapes=[pltpu.VMEM((2,) + state.shape, jnp.float32)] * 2
        + [pltpu.VMEM(state.shape, jnp.float32)] * 2
        + [pltpu.VMEM(halo_shape, jnp.float32)] * 2
        + [pltpu.SemaphoreType.DMA((8,)), pltpu.SemaphoreType.DMA((8,))],
        compiler_params=pltpu.CompilerParams(collective_id=0, has_side_effects=True),
    )(tbl, state, adjoint)
    return res, adj


def solution(mesh):
    return jax.shard_map(
        local,
        mesh=mesh,
        in_specs=(
            P("tm", None, None, "sec", None),
            P("tm", None, None, "sec", None),
            P("tm", None),
            P("tm", None),
        ),
        out_specs=(P("tm", None, None, "sec", None), P("tm", None, None, "sec", None)),
        check_vma=False,
    )
```

```python
import jax
import jax.numpy as jnp
from jax import lax
from jax.experimental import pallas as pl
from jax.experimental.pallas import tpu as pltpu
from jax.sharding import PartitionSpec as P

STENCIL = (0.8, -0.2, 4.0 / 105.0, -1.0 / 280.0)
TIME_SCALE = 4.0
FLOW_VELOCITY = 1.0
AXIAL_DISPERSION = 0.3
RADIAL_SPREADING = 0.2
BINDING_STRENGTH = (1.5, 0.6)
HEAT_EXPONENT = (0.5, 0.3)
KINETIC = (1.2, 0.7)
CAPACITY = (2.0, 1.0)
SORPTION_HEAT = (0.4, 0.25)
PURGE_GAIN = 1.5

MESH = pl.DeviceIdType.MESH


def _kernel(n_tm, plan, valve, st, ad, res, adj, rv_st, rv_ad, h_st, h_ad, send, recv):
    inst, comp, beds, nz, nr = st.shape
    me = lax.axis_index("tm")
    sec = lax.axis_index("sec")
    core = lax.rem(me, 2)
    pair = (me + 1 - 2 * core, sec)
    cross = (lax.rem(me + 2 * core - 1 + n_tm, n_tm), sec)
    partner = (me, 1 - sec)

    barrier = pltpu.get_barrier_semaphore()
    for dev in (pair, cross, partner):
        pl.semaphore_signal(barrier, inc=1, device_id=dev, device_id_type=MESH)
    pl.semaphore_wait(barrier, 3)

    def rcopy(src, dst, i, dev):
        cp = pltpu.make_async_remote_copy(
            src_ref=src, dst_ref=dst, send_sem=send.at[i], recv_sem=recv.at[i],
            device_id=dev, device_id_type=MESH,
        )
        cp.start()
        return cp

    row_src = (nz - 1) * (1 - sec)
    halo_copies = [
        rcopy(src.at[:, :, :, pl.ds(row_src, 1), :], dst.at[:, :, :, pl.ds(0, 1), :], 4 + i, partner)
        for i, (src, dst) in enumerate(((st, h_st), (ad, h_ad)))
    ]
    far_st = rcopy(st, rv_st.at[1 - core], 0, cross)
    far_ad = rcopy(ad, rv_ad.at[1 - core], 1, cross)
    near_st = rcopy(st, rv_st.at[core], 2, pair)
    near_ad = rcopy(ad, rv_ad.at[core], 3, pair)

    for cp in halo_copies:
        cp.wait_recv()

    sec_f = sec.astype(jnp.float32)
    row = lax.broadcasted_iota(jnp.int32, (nz, nr), 0)
    lane = lax.broadcasted_iota(jnp.int32, (nz, nr), 1)
    first_row = row == 0
    last_row = row == nz - 1
    first_lane = lane == 0
    last_lane = lane == nr - 1

    def radial(x):
        lower = jnp.where(first_lane, 0.0, pltpu.roll(x, 1, 1))
        upper = jnp.where(last_lane, 0.0, pltpu.roll(x, nr - 1, 1))
        return upper - 2.0 * x + lower

    def axial(x, below, above):
        zm = jnp.where(first_row, below, pltpu.roll(x, 1, 0))
        zp = jnp.where(last_row, above, pltpu.roll(x, nz - 1, 0))
        return zm, zp

    def transport(x, below, above):
        zm, zp = axial(x, below, above)
        out = FLOW_VELOCITY * (x - zm) - AXIAL_DISPERSION * (zp - 2.0 * x + zm)
        return out - RADIAL_SPREADING * radial(x)

    def transport_t(lam, below, above):
        lm, lp = axial(lam, below, above)
        out = FLOW_VELOCITY * (lam - lp) - AXIAL_DISPERSION * (lm - 2.0 * lam + lp)
        return out - RADIAL_SPREADING * radial(lam)

    def spatial_body(t, carry):
        for b in range(beds):
            x = [st[t, c, b] for c in range(comp)]
            lam = [ad[t, c, b] for c in range(comp)]
            hs = [h_st[t, c, b, 0:1, :] for c in range(comp)]
            ha = [h_ad[t, c, b, 0:1, :] for c in range(comp)]
            y1, y2, y3, q1, q2, temp = x
            b1 = BINDING_STRENGTH[0] * jnp.exp(HEAT_EXPONENT[0] * temp)
            b2 = BINDING_STRENGTH[1] * jnp.exp(HEAT_EXPONENT[1] * temp)
            den = 1.0 + b1 * y1 + b2 * y2
            p1 = b1 * y1 / den
            p2 = b2 * y2 / den
            rate1 = KINETIC[0] * (CAPACITY[0] * p1 - q1)
            rate2 = KINETIC[1] * (CAPACITY[1] * p2 - q2)
            tr = {}
            trt = {}
            for c in (0, 1, 2, 5):
                below = hs[c] * sec_f
                above = hs[c] * (1.0 - sec_f)
                tr[c] = transport(x[c], below, above)
                lbelow = ha[c] * sec_f
                labove = ha[c] * (1.0 - sec_f)
                trt[c] = transport_t(lam[c], lbelow, labove)
            res[t, 0, b] = tr[0] + rate1
            res[t, 1, b] = tr[1] + rate2
            res[t, 2, b] = tr[2]
            res[t, 3, b] = -rate1
            res[t, 4, b] = -rate2
            res[t, 5, b] = tr[5] - (SORPTION_HEAT[0] * rate1 + SORPTION_HEAT[1] * rate2)
            mu1 = lam[0] - lam[3] - SORPTION_HEAT[0] * lam[5]
            mu2 = lam[1] - lam[4] - SORPTION_HEAT[1] * lam[5]
            n1 = (KINETIC[0] * CAPACITY[0]) * mu1
            n2 = (KINETIC[1] * CAPACITY[1]) * mu2
            cden = -(n1 * p1 + n2 * p2) / den
            cu1 = n1 / den + cden
            cu2 = n2 / den + cden
            adj[t, 0, b] = trt[0] + b1 * cu1
            adj[t, 1, b] = trt[1] + b2 * cu2
            adj[t, 2, b] = trt[2]
            adj[t, 3, b] = -KINETIC[0] * mu1
            adj[t, 4, b] = -KINETIC[1] * mu2
            adj[t, 5, b] = trt[5] + (HEAT_EXPONENT[0] * y1 * b1 * cu1 + HEAT_EXPONENT[1] * y2 * b2 * cu2)
        return carry

    lax.fori_loop(0, inst, spatial_body, 0)

    @pl.when(sec == 1)
    def _():
        def purge_body(t, carry):
            srcs = [lax.rem(b + plan[t, b], beds) for b in range(beds)]
            opens = [jnp.full((1, nr), valve[t, b], jnp.int32) != 0 for b in range(beds)]
            for c in range(3):
                ys = [st[t, c, b, nz - 1 : nz, :] for b in range(beds)]
                ls = [ad[t, c, b, nz - 1 : nz, :] for b in range(beds)]
                for b in range(beds):
                    inc = jnp.zeros((1, nr), jnp.float32)
                    for bp in range(beds):
                        inc = inc + jnp.where(srcs[b] == bp, ys[bp], 0.0)
                    term = jnp.where(opens[b], PURGE_GAIN * (ys[b] - inc), 0.0)
                    res[t, c, b, nz - 1 : nz, :] = res[t, c, b, nz - 1 : nz, :] + term
                    back = jnp.where(opens[b], PURGE_GAIN * ls[b], 0.0)
                    for bb in range(beds):
                        hit = jnp.logical_and(opens[bb], srcs[bb] == b)
                        back = back - jnp.where(hit, PURGE_GAIN * ls[bb], 0.0)
                    adj[t, c, b, nz - 1 : nz, :] = adj[t, c, b, nz - 1 : nz, :] + back
            return carry

        lax.fori_loop(0, inst, purge_body, 0)

    def time_pass(cross_right, use_far):
        def body(c, carry):
            for t in range(inst):
                acc_s = None
                acc_a = None
                for k, w in enumerate(STENCIL):
                    s = k + 1
                    d_s = None
                    d_a = None
                    for j, sign in ((t + s, 1.0), (t - s, -1.0)):
                        if j >= inst:
                            far = cross_right
                            xs, xa = rv_st[1, j - inst, c], rv_ad[1, j - inst, c]
                        elif j < 0:
                            far = not cross_right
                            xs, xa = rv_st[0, j + inst, c], rv_ad[0, j + inst, c]
                        else:
                            far = False
                            xs, xa = st[j, c], ad[j, c]
                        if far != use_far:
                            continue
                        if sign < 0:
                            xs, xa = -xs, -xa
                        d_s = xs if d_s is None else d_s + xs
                        d_a = xa if d_a is None else d_a + xa
                    if d_s is None:
                        continue
                    acc_s = w * d_s if acc_s is None else acc_s + w * d_s
                    acc_a = w * d_a if acc_a is None else acc_a + w * d_a
                if acc_s is None:
                    continue
                res[t, c] = TIME_SCALE * acc_s + res[t, c]
                adj[t, c] = adj[t, c] - TIME_SCALE * acc_a
            return carry

        lax.fori_loop(0, comp, body, 0)

    near_st.wait_recv()
    near_ad.wait_recv()

    @pl.when(core == 0)
    def _():
        time_pass(False, False)

    @pl.when(core == 1)
    def _():
        time_pass(True, False)

    far_st.wait_recv()
    far_ad.wait_recv()

    @pl.when(core == 0)
    def _():
        time_pass(False, True)

    @pl.when(core == 1)
    def _():
        time_pass(True, True)

    for cp in halo_copies + [far_st, far_ad, near_st, near_ad]:
        cp.wait_send()


def local(state, adjoint, plan, valve):
    n_tm = lax.axis_size("tm")
    inst, comp, beds, nz, nr = state.shape
    block = jax.ShapeDtypeStruct(state.shape, jnp.float32)
    vmem = pl.BlockSpec(memory_space=pltpu.VMEM)
    halo_shape = (inst, comp, beds, 8, nr)

    def kern(*refs):
        _kernel(n_tm, *refs)

    res, adj = pl.pallas_call(
        kern,
        out_shape=(block, block),
        in_specs=[pl.BlockSpec(memory_space=pltpu.SMEM)] * 2 + [vmem, vmem],
        out_specs=(vmem, vmem),
        scratch_shapes=[pltpu.VMEM((2,) + state.shape, jnp.float32)] * 2
        + [pltpu.VMEM(halo_shape, jnp.float32)] * 2
        + [pltpu.SemaphoreType.DMA((6,)), pltpu.SemaphoreType.DMA((6,))],
        compiler_params=pltpu.CompilerParams(collective_id=0, has_side_effects=True),
    )(plan, valve, state, adjoint)
    return res, adj


def solution(mesh):
    return jax.shard_map(
        local,
        mesh=mesh,
        in_specs=(
            P("tm", None, None, "sec", None),
            P("tm", None, None, "sec", None),
            P("tm", None),
            P("tm", None),
        ),
        out_specs=(P("tm", None, None, "sec", None), P("tm", None, None, "sec", None)),
        check_vma=False,
    )
```

```python
import jax
import jax.numpy as jnp
from jax import lax
from jax.experimental import pallas as pl
from jax.experimental.pallas import tpu as pltpu
from jax.sharding import PartitionSpec as P

STENCIL = (0.8, -0.2, 4.0 / 105.0, -1.0 / 280.0)
TIME_SCALE = 4.0
FLOW_VELOCITY = 1.0
AXIAL_DISPERSION = 0.3
RADIAL_SPREADING = 0.2
BINDING_STRENGTH = (1.5, 0.6)
HEAT_EXPONENT = (0.5, 0.3)
KINETIC = (1.2, 0.7)
CAPACITY = (2.0, 1.0)
SORPTION_HEAT = (0.4, 0.25)
PURGE_GAIN = 1.5

MESH = pl.DeviceIdType.MESH


def _kernel(n_tm, plan, valve, st, ad, res, adj, rv_st, rv_ad, h_st, h_ad, ry_st, ry_ad, send, recv):
    inst, comp, beds, nz, nr = st.shape
    me = lax.axis_index("tm")
    sec = lax.axis_index("sec")
    core = lax.rem(me, 2)
    ring = lax.div(me, 4)
    y = lax.rem(lax.div(me, 2), 2) * 2 + sec
    pair = (me + 1 - 2 * core, sec)
    cross = (lax.rem(me + 2 * core - 1 + n_tm, n_tm), sec)
    partner = (me, 1 - sec)

    def at(yy, cc):
        yy = lax.rem(yy, 4)
        return (ring * 4 + lax.div(yy, 2) * 2 + cc, lax.rem(yy, 2))

    is_pure = (core + lax.div(y, 2)) == 1
    is_relay = (core + lax.div(lax.rem(y + 1, 4), 2)) == 1
    relay_of_me = at(y + 3, core)
    relay_to_me = at(y + 1, 1 - core)
    source = at(y + 1, core)
    dest = at(y + 3, 1 - core)

    barrier = pltpu.get_barrier_semaphore()
    for dev in (pair, cross, partner):
        pl.semaphore_signal(barrier, inc=1, device_id=dev, device_id_type=MESH)

    @pl.when(is_pure)
    def _():
        for dev in (relay_of_me, relay_to_me):
            pl.semaphore_signal(barrier, inc=1, device_id=dev, device_id_type=MESH)

    @pl.when(is_relay)
    def _():
        for dev in (source, dest):
            pl.semaphore_signal(barrier, inc=1, device_id=dev, device_id_type=MESH)

    pl.semaphore_wait(barrier, 3 + 2 * is_pure.astype(jnp.int32) + 2 * is_relay.astype(jnp.int32))

    def desc(src, dst, i, dev):
        return pltpu.make_async_remote_copy(
            src_ref=src, dst_ref=dst, send_sem=send.at[i], recv_sem=recv.at[i],
            device_id=dev, device_id_type=MESH,
        )

    def rcopy(src, dst, i, dev):
        cp = desc(src, dst, i, dev)
        cp.start()
        return cp

    split = inst - 1

    def far_descs(n):
        return [
            desc(st.at[0:n], rv_st.at[1 - core, 0:n], 0, cross),
            desc(ad.at[0:n], rv_ad.at[1 - core, 0:n], 1, cross),
        ]

    def leg_descs():
        return [
            desc(st.at[split:inst], ry_st, 6, relay_of_me),
            desc(ad.at[split:inst], ry_ad, 7, relay_of_me),
        ]

    def fwd_descs():
        return [
            desc(ry_st, rv_st.at[1 - core, split:inst], 8, dest),
            desc(ry_ad, rv_ad.at[1 - core, split:inst], 9, dest),
        ]

    row_src = (nz - 1) * (1 - sec)
    halo_copies = [
        rcopy(src.at[:, :, :, pl.ds(row_src, 1), :], dst.at[:, :, :, pl.ds(0, 1), :], 4 + i, partner)
        for i, (src, dst) in enumerate(((st, h_st), (ad, h_ad)))
    ]

    @pl.when(is_pure)
    def _():
        for cp in far_descs(split) + leg_descs():
            cp.start()

    @pl.when(jnp.logical_not(is_pure))
    def _():
        for cp in far_descs(inst):
            cp.start()

    near_st = rcopy(st, rv_st.at[core], 2, pair)
    near_ad = rcopy(ad, rv_ad.at[core], 3, pair)

    for cp in halo_copies:
        cp.wait_recv()

    sec_f = sec.astype(jnp.float32)
    row = lax.broadcasted_iota(jnp.int32, (nz, nr), 0)
    lane = lax.broadcasted_iota(jnp.int32, (nz, nr), 1)
    first_row = row == 0
    last_row = row == nz - 1
    first_lane = lane == 0
    last_lane = lane == nr - 1

    def radial(x):
        lower = jnp.where(first_lane, 0.0, pltpu.roll(x, 1, 1))
        upper = jnp.where(last_lane, 0.0, pltpu.roll(x, nr - 1, 1))
        return upper - 2.0 * x + lower

    def axial(x, below, above):
        zm = jnp.where(first_row, below, pltpu.roll(x, 1, 0))
        zp = jnp.where(last_row, above, pltpu.roll(x, nz - 1, 0))
        return zm, zp

    def transport(x, below, above):
        zm, zp = axial(x, below, above)
        out = FLOW_VELOCITY * (x - zm) - AXIAL_DISPERSION * (zp - 2.0 * x + zm)
        return out - RADIAL_SPREADING * radial(x)

    def transport_t(lam, below, above):
        lm, lp = axial(lam, below, above)
        out = FLOW_VELOCITY * (lam - lp) - AXIAL_DISPERSION * (lm - 2.0 * lam + lp)
        return out - RADIAL_SPREADING * radial(lam)

    def spatial_body(t, carry):
        for b in range(beds):
            x = [st[t, c, b] for c in range(comp)]
            lam = [ad[t, c, b] for c in range(comp)]
            hs = [h_st[t, c, b, 0:1, :] for c in range(comp)]
            ha = [h_ad[t, c, b, 0:1, :] for c in range(comp)]
            y1, y2, y3, q1, q2, temp = x
            b1 = BINDING_STRENGTH[0] * jnp.exp(HEAT_EXPONENT[0] * temp)
            b2 = BINDING_STRENGTH[1] * jnp.exp(HEAT_EXPONENT[1] * temp)
            den = 1.0 + b1 * y1 + b2 * y2
            p1 = b1 * y1 / den
            p2 = b2 * y2 / den
            rate1 = KINETIC[0] * (CAPACITY[0] * p1 - q1)
            rate2 = KINETIC[1] * (CAPACITY[1] * p2 - q2)
            tr = {}
            trt = {}
            for c in (0, 1, 2, 5):
                below = hs[c] * sec_f
                above = hs[c] * (1.0 - sec_f)
                tr[c] = transport(x[c], below, above)
                lbelow = ha[c] * sec_f
                labove = ha[c] * (1.0 - sec_f)
                trt[c] = transport_t(lam[c], lbelow, labove)
            res[t, 0, b] = tr[0] + rate1
            res[t, 1, b] = tr[1] + rate2
            res[t, 2, b] = tr[2]
            res[t, 3, b] = -rate1
            res[t, 4, b] = -rate2
            res[t, 5, b] = tr[5] - (SORPTION_HEAT[0] * rate1 + SORPTION_HEAT[1] * rate2)
            mu1 = lam[0] - lam[3] - SORPTION_HEAT[0] * lam[5]
            mu2 = lam[1] - lam[4] - SORPTION_HEAT[1] * lam[5]
            n1 = (KINETIC[0] * CAPACITY[0]) * mu1
            n2 = (KINETIC[1] * CAPACITY[1]) * mu2
            cden = -(n1 * p1 + n2 * p2) / den
            cu1 = n1 / den + cden
            cu2 = n2 / den + cden
            adj[t, 0, b] = trt[0] + b1 * cu1
            adj[t, 1, b] = trt[1] + b2 * cu2
            adj[t, 2, b] = trt[2]
            adj[t, 3, b] = -KINETIC[0] * mu1
            adj[t, 4, b] = -KINETIC[1] * mu2
            adj[t, 5, b] = trt[5] + (HEAT_EXPONENT[0] * y1 * b1 * cu1 + HEAT_EXPONENT[1] * y2 * b2 * cu2)
        return carry

    lax.fori_loop(0, inst, spatial_body, 0)

    @pl.when(sec == 1)
    def _():
        def purge_body(t, carry):
            srcs = [lax.rem(b + plan[t, b], beds) for b in range(beds)]
            opens = [jnp.full((1, nr), valve[t, b], jnp.int32) != 0 for b in range(beds)]
            for c in range(3):
                ys = [st[t, c, b, nz - 1 : nz, :] for b in range(beds)]
                ls = [ad[t, c, b, nz - 1 : nz, :] for b in range(beds)]
                for b in range(beds):
                    inc = jnp.zeros((1, nr), jnp.float32)
                    for bp in range(beds):
                        inc = inc + jnp.where(srcs[b] == bp, ys[bp], 0.0)
                    term = jnp.where(opens[b], PURGE_GAIN * (ys[b] - inc), 0.0)
                    res[t, c, b, nz - 1 : nz, :] = res[t, c, b, nz - 1 : nz, :] + term
                    back = jnp.where(opens[b], PURGE_GAIN * ls[b], 0.0)
                    for bb in range(beds):
                        hit = jnp.logical_and(opens[bb], srcs[bb] == b)
                        back = back - jnp.where(hit, PURGE_GAIN * ls[bb], 0.0)
                    adj[t, c, b, nz - 1 : nz, :] = adj[t, c, b, nz - 1 : nz, :] + back
            return carry

        lax.fori_loop(0, inst, purge_body, 0)

    def time_pass(cross_right, use_far):
        def body(c, carry):
            for t in range(inst):
                acc_s = None
                acc_a = None
                for k, w in enumerate(STENCIL):
                    s = k + 1
                    d_s = None
                    d_a = None
                    for j, sign in ((t + s, 1.0), (t - s, -1.0)):
                        if j >= inst:
                            far = cross_right
                            xs, xa = rv_st[1, j - inst, c], rv_ad[1, j - inst, c]
                        elif j < 0:
                            far = not cross_right
                            xs, xa = rv_st[0, j + inst, c], rv_ad[0, j + inst, c]
                        else:
                            far = False
                            xs, xa = st[j, c], ad[j, c]
                        if far != use_far:
                            continue
                        if sign < 0:
                            xs, xa = -xs, -xa
                        d_s = xs if d_s is None else d_s + xs
                        d_a = xa if d_a is None else d_a + xa
                    if d_s is None:
                        continue
                    acc_s = w * d_s if acc_s is None else acc_s + w * d_s
                    acc_a = w * d_a if acc_a is None else acc_a + w * d_a
                if acc_s is None:
                    continue
                res[t, c] = TIME_SCALE * acc_s + res[t, c]
                adj[t, c] = adj[t, c] - TIME_SCALE * acc_a
            return carry

        lax.fori_loop(0, comp, body, 0)

    @pl.when(is_relay)
    def _():
        for leg, fwd in zip(leg_descs(), fwd_descs()):
            leg.wait_recv()
            fwd.start()

    near_st.wait_recv()
    near_ad.wait_recv()

    @pl.when(core == 0)
    def _():
        time_pass(False, False)

    @pl.when(core == 1)
    def _():
        time_pass(True, False)

    @pl.when(is_pure)
    def _():
        for cp in far_descs(split) + fwd_descs():
            cp.wait_recv()

    @pl.when(jnp.logical_not(is_pure))
    def _():
        for cp in far_descs(inst):
            cp.wait_recv()

    @pl.when(core == 0)
    def _():
        time_pass(False, True)

    @pl.when(core == 1)
    def _():
        time_pass(True, True)

    for cp in halo_copies + [near_st, near_ad]:
        cp.wait_send()

    @pl.when(is_pure)
    def _():
        for cp in far_descs(split) + leg_descs():
            cp.wait_send()

    @pl.when(jnp.logical_not(is_pure))
    def _():
        for cp in far_descs(inst):
            cp.wait_send()

    @pl.when(is_relay)
    def _():
        for cp in fwd_descs():
            cp.wait_send()


def local(state, adjoint, plan, valve):
    n_tm = lax.axis_size("tm")
    inst, comp, beds, nz, nr = state.shape
    block = jax.ShapeDtypeStruct(state.shape, jnp.float32)
    vmem = pl.BlockSpec(memory_space=pltpu.VMEM)
    halo_shape = (inst, comp, beds, 8, nr)

    def kern(*refs):
        _kernel(n_tm, *refs)

    res, adj = pl.pallas_call(
        kern,
        out_shape=(block, block),
        in_specs=[pl.BlockSpec(memory_space=pltpu.SMEM)] * 2 + [vmem, vmem],
        out_specs=(vmem, vmem),
        scratch_shapes=[pltpu.VMEM((2,) + state.shape, jnp.float32)] * 2
        + [pltpu.VMEM(halo_shape, jnp.float32)] * 2
        + [pltpu.VMEM((1,) + state.shape[1:], jnp.float32)] * 2
        + [pltpu.SemaphoreType.DMA((10,)), pltpu.SemaphoreType.DMA((10,))],
        compiler_params=pltpu.CompilerParams(collective_id=0, has_side_effects=True),
    )(plan, valve, state, adjoint)
    return res, adj


def solution(mesh):
    return jax.shard_map(
        local,
        mesh=mesh,
        in_specs=(
            P("tm", None, None, "sec", None),
            P("tm", None, None, "sec", None),
            P("tm", None),
            P("tm", None),
        ),
        out_specs=(P("tm", None, None, "sec", None), P("tm", None, None, "sec", None)),
        check_vma=False,
    )
```

```python
import jax
import jax.numpy as jnp
from jax import lax
from jax.experimental import pallas as pl
from jax.experimental.pallas import tpu as pltpu
from jax.sharding import PartitionSpec as P

STENCIL = (0.8, -0.2, 4.0 / 105.0, -1.0 / 280.0)
TIME_SCALE = 4.0
FLOW_VELOCITY = 1.0
AXIAL_DISPERSION = 0.3
RADIAL_SPREADING = 0.2
BINDING_STRENGTH = (1.5, 0.6)
HEAT_EXPONENT = (0.5, 0.3)
KINETIC = (1.2, 0.7)
CAPACITY = (2.0, 1.0)
SORPTION_HEAT = (0.4, 0.25)
PURGE_GAIN = 1.5

MESH = pl.DeviceIdType.MESH


def _kernel(n_tm, plan, valve, st, ad, res, adj, rv_st, rv_ad, h_st, h_ad, ry_st, ry_ad, send, recv):
    inst, comp, beds, nz, nr = st.shape
    me = lax.axis_index("tm")
    sec = lax.axis_index("sec")
    core = lax.rem(me, 2)
    ring = lax.div(me, 4)
    y = lax.rem(lax.div(me, 2), 2) * 2 + sec
    pair = (me + 1 - 2 * core, sec)
    cross = (lax.rem(me + 2 * core - 1 + n_tm, n_tm), sec)
    partner = (me, 1 - sec)

    def at(yy, cc):
        yy = lax.rem(yy, 4)
        return (ring * 4 + lax.div(yy, 2) * 2 + cc, lax.rem(yy, 2))

    is_pure = (core + lax.div(y, 2)) == 1
    is_relay = (core + lax.div(lax.rem(y + 3, 4), 2)) == 1
    relay_of_me = at(y + 1, core)
    relay_to_me = at(y + 3, 1 - core)
    source = at(y + 3, core)
    dest = at(y + 1, 1 - core)

    barrier = pltpu.get_barrier_semaphore()
    for dev in (pair, cross, partner):
        pl.semaphore_signal(barrier, inc=1, device_id=dev, device_id_type=MESH)

    @pl.when(is_pure)
    def _():
        for dev in (relay_of_me, relay_to_me):
            pl.semaphore_signal(barrier, inc=1, device_id=dev, device_id_type=MESH)

    @pl.when(is_relay)
    def _():
        for dev in (source, dest):
            pl.semaphore_signal(barrier, inc=1, device_id=dev, device_id_type=MESH)

    pl.semaphore_wait(barrier, 3 + 2 * is_pure.astype(jnp.int32) + 2 * is_relay.astype(jnp.int32))

    def desc(src, dst, i, dev):
        return pltpu.make_async_remote_copy(
            src_ref=src, dst_ref=dst, send_sem=send.at[i], recv_sem=recv.at[i],
            device_id=dev, device_id_type=MESH,
        )

    def rcopy(src, dst, i, dev):
        cp = desc(src, dst, i, dev)
        cp.start()
        return cp

    split = inst - 1

    def far_descs(n):
        return [
            desc(st.at[0:n], rv_st.at[1 - core, 0:n], 0, cross),
            desc(ad.at[0:n], rv_ad.at[1 - core, 0:n], 1, cross),
        ]

    def leg_descs():
        return [
            desc(st.at[split:inst], ry_st, 6, relay_of_me),
            desc(ad.at[split:inst], ry_ad, 7, relay_of_me),
        ]

    def fwd_descs():
        return [
            desc(ry_st, rv_st.at[1 - core, split:inst], 8, dest),
            desc(ry_ad, rv_ad.at[1 - core, split:inst], 9, dest),
        ]

    row_src = (nz - 1) * (1 - sec)
    halo_copies = [
        rcopy(src.at[:, :, :, pl.ds(row_src, 1), :], dst.at[:, :, :, pl.ds(0, 1), :], 4 + i, partner)
        for i, (src, dst) in enumerate(((st, h_st), (ad, h_ad)))
    ]

    @pl.when(is_pure)
    def _():
        for cp in far_descs(split) + leg_descs():
            cp.start()

    @pl.when(jnp.logical_not(is_pure))
    def _():
        for cp in far_descs(inst):
            cp.start()

    near_st = rcopy(st, rv_st.at[core], 2, pair)
    near_ad = rcopy(ad, rv_ad.at[core], 3, pair)

    for cp in halo_copies:
        cp.wait_recv()

    sec_f = sec.astype(jnp.float32)
    row = lax.broadcasted_iota(jnp.int32, (nz, nr), 0)
    lane = lax.broadcasted_iota(jnp.int32, (nz, nr), 1)
    first_row = row == 0
    last_row = row == nz - 1
    first_lane = lane == 0
    last_lane = lane == nr - 1

    def radial(x):
        lower = jnp.where(first_lane, 0.0, pltpu.roll(x, 1, 1))
        upper = jnp.where(last_lane, 0.0, pltpu.roll(x, nr - 1, 1))
        return upper - 2.0 * x + lower

    def axial(x, below, above):
        zm = jnp.where(first_row, below, pltpu.roll(x, 1, 0))
        zp = jnp.where(last_row, above, pltpu.roll(x, nz - 1, 0))
        return zm, zp

    def transport(x, below, above):
        zm, zp = axial(x, below, above)
        out = FLOW_VELOCITY * (x - zm) - AXIAL_DISPERSION * (zp - 2.0 * x + zm)
        return out - RADIAL_SPREADING * radial(x)

    def transport_t(lam, below, above):
        lm, lp = axial(lam, below, above)
        out = FLOW_VELOCITY * (lam - lp) - AXIAL_DISPERSION * (lm - 2.0 * lam + lp)
        return out - RADIAL_SPREADING * radial(lam)

    def spatial_body(t, carry):
        for b in range(beds):
            x = [st[t, c, b] for c in range(comp)]
            lam = [ad[t, c, b] for c in range(comp)]
            hs = [h_st[t, c, b, 0:1, :] for c in range(comp)]
            ha = [h_ad[t, c, b, 0:1, :] for c in range(comp)]
            y1, y2, y3, q1, q2, temp = x
            b1 = BINDING_STRENGTH[0] * jnp.exp(HEAT_EXPONENT[0] * temp)
            b2 = BINDING_STRENGTH[1] * jnp.exp(HEAT_EXPONENT[1] * temp)
            den = 1.0 + b1 * y1 + b2 * y2
            p1 = b1 * y1 / den
            p2 = b2 * y2 / den
            rate1 = KINETIC[0] * (CAPACITY[0] * p1 - q1)
            rate2 = KINETIC[1] * (CAPACITY[1] * p2 - q2)
            tr = {}
            trt = {}
            for c in (0, 1, 2, 5):
                below = hs[c] * sec_f
                above = hs[c] * (1.0 - sec_f)
                tr[c] = transport(x[c], below, above)
                lbelow = ha[c] * sec_f
                labove = ha[c] * (1.0 - sec_f)
                trt[c] = transport_t(lam[c], lbelow, labove)
            res[t, 0, b] = tr[0] + rate1
            res[t, 1, b] = tr[1] + rate2
            res[t, 2, b] = tr[2]
            res[t, 3, b] = -rate1
            res[t, 4, b] = -rate2
            res[t, 5, b] = tr[5] - (SORPTION_HEAT[0] * rate1 + SORPTION_HEAT[1] * rate2)
            mu1 = lam[0] - lam[3] - SORPTION_HEAT[0] * lam[5]
            mu2 = lam[1] - lam[4] - SORPTION_HEAT[1] * lam[5]
            n1 = (KINETIC[0] * CAPACITY[0]) * mu1
            n2 = (KINETIC[1] * CAPACITY[1]) * mu2
            cden = -(n1 * p1 + n2 * p2) / den
            cu1 = n1 / den + cden
            cu2 = n2 / den + cden
            adj[t, 0, b] = trt[0] + b1 * cu1
            adj[t, 1, b] = trt[1] + b2 * cu2
            adj[t, 2, b] = trt[2]
            adj[t, 3, b] = -KINETIC[0] * mu1
            adj[t, 4, b] = -KINETIC[1] * mu2
            adj[t, 5, b] = trt[5] + (HEAT_EXPONENT[0] * y1 * b1 * cu1 + HEAT_EXPONENT[1] * y2 * b2 * cu2)
        return carry

    lax.fori_loop(0, inst, spatial_body, 0)

    @pl.when(sec == 1)
    def _():
        def purge_body(t, carry):
            srcs = [lax.rem(b + plan[t, b], beds) for b in range(beds)]
            opens = [jnp.full((1, nr), valve[t, b], jnp.int32) != 0 for b in range(beds)]
            for c in range(3):
                ys = [st[t, c, b, nz - 1 : nz, :] for b in range(beds)]
                ls = [ad[t, c, b, nz - 1 : nz, :] for b in range(beds)]
                for b in range(beds):
                    inc = jnp.zeros((1, nr), jnp.float32)
                    for bp in range(beds):
                        inc = inc + jnp.where(srcs[b] == bp, ys[bp], 0.0)
                    term = jnp.where(opens[b], PURGE_GAIN * (ys[b] - inc), 0.0)
                    res[t, c, b, nz - 1 : nz, :] = res[t, c, b, nz - 1 : nz, :] + term
                    back = jnp.where(opens[b], PURGE_GAIN * ls[b], 0.0)
                    for bb in range(beds):
                        hit = jnp.logical_and(opens[bb], srcs[bb] == b)
                        back = back - jnp.where(hit, PURGE_GAIN * ls[bb], 0.0)
                    adj[t, c, b, nz - 1 : nz, :] = adj[t, c, b, nz - 1 : nz, :] + back
            return carry

        lax.fori_loop(0, inst, purge_body, 0)

    def time_pass(cross_right, use_far):
        def body(c, carry):
            for t in range(inst):
                acc_s = None
                acc_a = None
                for k, w in enumerate(STENCIL):
                    s = k + 1
                    d_s = None
                    d_a = None
                    for j, sign in ((t + s, 1.0), (t - s, -1.0)):
                        if j >= inst:
                            far = cross_right
                            xs, xa = rv_st[1, j - inst, c], rv_ad[1, j - inst, c]
                        elif j < 0:
                            far = not cross_right
                            xs, xa = rv_st[0, j + inst, c], rv_ad[0, j + inst, c]
                        else:
                            far = False
                            xs, xa = st[j, c], ad[j, c]
                        if far != use_far:
                            continue
                        if sign < 0:
                            xs, xa = -xs, -xa
                        d_s = xs if d_s is None else d_s + xs
                        d_a = xa if d_a is None else d_a + xa
                    if d_s is None:
                        continue
                    acc_s = w * d_s if acc_s is None else acc_s + w * d_s
                    acc_a = w * d_a if acc_a is None else acc_a + w * d_a
                if acc_s is None:
                    continue
                res[t, c] = TIME_SCALE * acc_s + res[t, c]
                adj[t, c] = adj[t, c] - TIME_SCALE * acc_a
            return carry

        lax.fori_loop(0, comp, body, 0)

    @pl.when(is_relay)
    def _():
        for leg, fwd in zip(leg_descs(), fwd_descs()):
            leg.wait_recv()
            fwd.start()

    near_st.wait_recv()
    near_ad.wait_recv()

    @pl.when(core == 0)
    def _():
        time_pass(False, False)

    @pl.when(core == 1)
    def _():
        time_pass(True, False)

    @pl.when(is_pure)
    def _():
        for cp in far_descs(split) + fwd_descs():
            cp.wait_recv()

    @pl.when(jnp.logical_not(is_pure))
    def _():
        for cp in far_descs(inst):
            cp.wait_recv()

    @pl.when(core == 0)
    def _():
        time_pass(False, True)

    @pl.when(core == 1)
    def _():
        time_pass(True, True)

    for cp in halo_copies + [near_st, near_ad]:
        cp.wait_send()

    @pl.when(is_pure)
    def _():
        for cp in far_descs(split) + leg_descs():
            cp.wait_send()

    @pl.when(jnp.logical_not(is_pure))
    def _():
        for cp in far_descs(inst):
            cp.wait_send()

    @pl.when(is_relay)
    def _():
        for cp in fwd_descs():
            cp.wait_send()


def local(state, adjoint, plan, valve):
    n_tm = lax.axis_size("tm")
    inst, comp, beds, nz, nr = state.shape
    block = jax.ShapeDtypeStruct(state.shape, jnp.float32)
    vmem = pl.BlockSpec(memory_space=pltpu.VMEM)
    halo_shape = (inst, comp, beds, 8, nr)

    def kern(*refs):
        _kernel(n_tm, *refs)

    res, adj = pl.pallas_call(
        kern,
        out_shape=(block, block),
        in_specs=[pl.BlockSpec(memory_space=pltpu.SMEM)] * 2 + [vmem, vmem],
        out_specs=(vmem, vmem),
        scratch_shapes=[pltpu.VMEM((2,) + state.shape, jnp.float32)] * 2
        + [pltpu.VMEM(halo_shape, jnp.float32)] * 2
        + [pltpu.VMEM((1,) + state.shape[1:], jnp.float32)] * 2
        + [pltpu.SemaphoreType.DMA((10,)), pltpu.SemaphoreType.DMA((10,))],
        compiler_params=pltpu.CompilerParams(collective_id=0, has_side_effects=True),
    )(plan, valve, state, adjoint)
    return res, adj


def solution(mesh):
    return jax.shard_map(
        local,
        mesh=mesh,
        in_specs=(
            P("tm", None, None, "sec", None),
            P("tm", None, None, "sec", None),
            P("tm", None),
            P("tm", None),
        ),
        out_specs=(P("tm", None, None, "sec", None), P("tm", None, None, "sec", None)),
        check_vma=False,
    )
```

```python
import jax
import jax.numpy as jnp
from jax import lax
from jax.experimental import pallas as pl
from jax.experimental.pallas import tpu as pltpu
from jax.sharding import PartitionSpec as P

STENCIL = (0.8, -0.2, 4.0 / 105.0, -1.0 / 280.0)
TIME_SCALE = 4.0
FLOW_VELOCITY = 1.0
AXIAL_DISPERSION = 0.3
RADIAL_SPREADING = 0.2
BINDING_STRENGTH = (1.5, 0.6)
HEAT_EXPONENT = (0.5, 0.3)
KINETIC = (1.2, 0.7)
CAPACITY = (2.0, 1.0)
SORPTION_HEAT = (0.4, 0.25)
PURGE_GAIN = 1.5

MESH = pl.DeviceIdType.MESH


def _kernel(n_tm, plan, valve, st, ad, res, adj, rv_st, rv_ad, h_st, h_ad, send, recv):
    inst, comp, beds, nz, nr = st.shape
    me = lax.axis_index("tm")
    sec = lax.axis_index("sec")
    core = lax.rem(me, 2)
    pair = (me + 1 - 2 * core, sec)
    cross = (lax.rem(me + 2 * core - 1 + n_tm, n_tm), sec)
    partner = (me, 1 - sec)

    barrier = pltpu.get_barrier_semaphore()
    for dev in (pair, cross, partner):
        pl.semaphore_signal(barrier, inc=1, device_id=dev, device_id_type=MESH)
    pl.semaphore_wait(barrier, 3)

    def rcopy(src, dst, i, dev):
        cp = pltpu.make_async_remote_copy(
            src_ref=src, dst_ref=dst, send_sem=send.at[i], recv_sem=recv.at[i],
            device_id=dev, device_id_type=MESH,
        )
        cp.start()
        return cp

    row_src = (nz - 1) * (1 - sec)
    halo_copies = [
        rcopy(src.at[:, :, :, pl.ds(row_src, 1), :], dst.at[:, :, :, pl.ds(0, 1), :], 4 + i, partner)
        for i, (src, dst) in enumerate(((st, h_st), (ad, h_ad)))
    ]
    def desc(src, dst, i, dev):
        return pltpu.make_async_remote_copy(
            src_ref=src, dst_ref=dst, send_sem=send.at[i], recv_sem=recv.at[i],
            device_id=dev, device_id_type=MESH,
        )

    def chunked(src, dst, i, dev):
        for j in range(inst):
            desc(src.at[j : j + 1], dst.at[j : j + 1], i, dev).start()
        return desc(src, dst, i, dev)

    far_st = chunked(st, rv_st.at[1 - core], 0, cross)
    far_ad = chunked(ad, rv_ad.at[1 - core], 1, cross)
    near_st = rcopy(st, rv_st.at[core], 2, pair)
    near_ad = rcopy(ad, rv_ad.at[core], 3, pair)

    for cp in halo_copies:
        cp.wait_recv()

    sec_f = sec.astype(jnp.float32)
    row = lax.broadcasted_iota(jnp.int32, (nz, nr), 0)
    lane = lax.broadcasted_iota(jnp.int32, (nz, nr), 1)
    first_row = row == 0
    last_row = row == nz - 1
    first_lane = lane == 0
    last_lane = lane == nr - 1

    def radial(x):
        lower = jnp.where(first_lane, 0.0, pltpu.roll(x, 1, 1))
        upper = jnp.where(last_lane, 0.0, pltpu.roll(x, nr - 1, 1))
        return upper - 2.0 * x + lower

    def axial(x, below, above):
        zm = jnp.where(first_row, below, pltpu.roll(x, 1, 0))
        zp = jnp.where(last_row, above, pltpu.roll(x, nz - 1, 0))
        return zm, zp

    def transport(x, below, above):
        zm, zp = axial(x, below, above)
        out = FLOW_VELOCITY * (x - zm) - AXIAL_DISPERSION * (zp - 2.0 * x + zm)
        return out - RADIAL_SPREADING * radial(x)

    def transport_t(lam, below, above):
        lm, lp = axial(lam, below, above)
        out = FLOW_VELOCITY * (lam - lp) - AXIAL_DISPERSION * (lm - 2.0 * lam + lp)
        return out - RADIAL_SPREADING * radial(lam)

    def spatial_body(t, carry):
        for b in range(beds):
            x = [st[t, c, b] for c in range(comp)]
            lam = [ad[t, c, b] for c in range(comp)]
            hs = [h_st[t, c, b, 0:1, :] for c in range(comp)]
            ha = [h_ad[t, c, b, 0:1, :] for c in range(comp)]
            y1, y2, y3, q1, q2, temp = x
            b1 = BINDING_STRENGTH[0] * jnp.exp(HEAT_EXPONENT[0] * temp)
            b2 = BINDING_STRENGTH[1] * jnp.exp(HEAT_EXPONENT[1] * temp)
            den = 1.0 + b1 * y1 + b2 * y2
            p1 = b1 * y1 / den
            p2 = b2 * y2 / den
            rate1 = KINETIC[0] * (CAPACITY[0] * p1 - q1)
            rate2 = KINETIC[1] * (CAPACITY[1] * p2 - q2)
            tr = {}
            trt = {}
            for c in (0, 1, 2, 5):
                below = hs[c] * sec_f
                above = hs[c] * (1.0 - sec_f)
                tr[c] = transport(x[c], below, above)
                lbelow = ha[c] * sec_f
                labove = ha[c] * (1.0 - sec_f)
                trt[c] = transport_t(lam[c], lbelow, labove)
            res[t, 0, b] = tr[0] + rate1
            res[t, 1, b] = tr[1] + rate2
            res[t, 2, b] = tr[2]
            res[t, 3, b] = -rate1
            res[t, 4, b] = -rate2
            res[t, 5, b] = tr[5] - (SORPTION_HEAT[0] * rate1 + SORPTION_HEAT[1] * rate2)
            mu1 = lam[0] - lam[3] - SORPTION_HEAT[0] * lam[5]
            mu2 = lam[1] - lam[4] - SORPTION_HEAT[1] * lam[5]
            n1 = (KINETIC[0] * CAPACITY[0]) * mu1
            n2 = (KINETIC[1] * CAPACITY[1]) * mu2
            cden = -(n1 * p1 + n2 * p2) / den
            cu1 = n1 / den + cden
            cu2 = n2 / den + cden
            adj[t, 0, b] = trt[0] + b1 * cu1
            adj[t, 1, b] = trt[1] + b2 * cu2
            adj[t, 2, b] = trt[2]
            adj[t, 3, b] = -KINETIC[0] * mu1
            adj[t, 4, b] = -KINETIC[1] * mu2
            adj[t, 5, b] = trt[5] + (HEAT_EXPONENT[0] * y1 * b1 * cu1 + HEAT_EXPONENT[1] * y2 * b2 * cu2)
        return carry

    lax.fori_loop(0, inst, spatial_body, 0)

    @pl.when(sec == 1)
    def _():
        def purge_body(t, carry):
            srcs = [lax.rem(b + plan[t, b], beds) for b in range(beds)]
            opens = [jnp.full((1, nr), valve[t, b], jnp.int32) != 0 for b in range(beds)]
            for c in range(3):
                ys = [st[t, c, b, nz - 1 : nz, :] for b in range(beds)]
                ls = [ad[t, c, b, nz - 1 : nz, :] for b in range(beds)]
                for b in range(beds):
                    inc = jnp.zeros((1, nr), jnp.float32)
                    for bp in range(beds):
                        inc = inc + jnp.where(srcs[b] == bp, ys[bp], 0.0)
                    term = jnp.where(opens[b], PURGE_GAIN * (ys[b] - inc), 0.0)
                    res[t, c, b, nz - 1 : nz, :] = res[t, c, b, nz - 1 : nz, :] + term
                    back = jnp.where(opens[b], PURGE_GAIN * ls[b], 0.0)
                    for bb in range(beds):
                        hit = jnp.logical_and(opens[bb], srcs[bb] == b)
                        back = back - jnp.where(hit, PURGE_GAIN * ls[bb], 0.0)
                    adj[t, c, b, nz - 1 : nz, :] = adj[t, c, b, nz - 1 : nz, :] + back
            return carry

        lax.fori_loop(0, inst, purge_body, 0)

    def time_pass(cross_right, use_far):
        def body(c, carry):
            for t in range(inst):
                acc_s = None
                acc_a = None
                for k, w in enumerate(STENCIL):
                    s = k + 1
                    d_s = None
                    d_a = None
                    for j, sign in ((t + s, 1.0), (t - s, -1.0)):
                        if j >= inst:
                            far = cross_right
                            xs, xa = rv_st[1, j - inst, c], rv_ad[1, j - inst, c]
                        elif j < 0:
                            far = not cross_right
                            xs, xa = rv_st[0, j + inst, c], rv_ad[0, j + inst, c]
                        else:
                            far = False
                            xs, xa = st[j, c], ad[j, c]
                        if far != use_far:
                            continue
                        if sign < 0:
                            xs, xa = -xs, -xa
                        d_s = xs if d_s is None else d_s + xs
                        d_a = xa if d_a is None else d_a + xa
                    if d_s is None:
                        continue
                    acc_s = w * d_s if acc_s is None else acc_s + w * d_s
                    acc_a = w * d_a if acc_a is None else acc_a + w * d_a
                if acc_s is None:
                    continue
                res[t, c] = TIME_SCALE * acc_s + res[t, c]
                adj[t, c] = adj[t, c] - TIME_SCALE * acc_a
            return carry

        lax.fori_loop(0, comp, body, 0)

    near_st.wait_recv()
    near_ad.wait_recv()

    @pl.when(core == 0)
    def _():
        time_pass(False, False)

    @pl.when(core == 1)
    def _():
        time_pass(True, False)

    far_st.wait_recv()
    far_ad.wait_recv()

    @pl.when(core == 0)
    def _():
        time_pass(False, True)

    @pl.when(core == 1)
    def _():
        time_pass(True, True)

    for cp in halo_copies + [far_st, far_ad, near_st, near_ad]:
        cp.wait_send()


def local(state, adjoint, plan, valve):
    n_tm = lax.axis_size("tm")
    inst, comp, beds, nz, nr = state.shape
    block = jax.ShapeDtypeStruct(state.shape, jnp.float32)
    vmem = pl.BlockSpec(memory_space=pltpu.VMEM)
    halo_shape = (inst, comp, beds, 8, nr)

    def kern(*refs):
        _kernel(n_tm, *refs)

    res, adj = pl.pallas_call(
        kern,
        out_shape=(block, block),
        in_specs=[pl.BlockSpec(memory_space=pltpu.SMEM)] * 2 + [vmem, vmem],
        out_specs=(vmem, vmem),
        scratch_shapes=[pltpu.VMEM((2,) + state.shape, jnp.float32)] * 2
        + [pltpu.VMEM(halo_shape, jnp.float32)] * 2
        + [pltpu.SemaphoreType.DMA((6,)), pltpu.SemaphoreType.DMA((6,))],
        compiler_params=pltpu.CompilerParams(collective_id=0, has_side_effects=True),
    )(plan, valve, state, adjoint)
    return res, adj


def solution(mesh):
    return jax.shard_map(
        local,
        mesh=mesh,
        in_specs=(
            P("tm", None, None, "sec", None),
            P("tm", None, None, "sec", None),
            P("tm", None),
            P("tm", None),
        ),
        out_specs=(P("tm", None, None, "sec", None), P("tm", None, None, "sec", None)),
        check_vma=False,
    )
```

```python
import jax
import jax.numpy as jnp
from jax import lax
from jax.experimental import pallas as pl
from jax.experimental.pallas import tpu as pltpu
from jax.sharding import PartitionSpec as P

STENCIL = (0.8, -0.2, 4.0 / 105.0, -1.0 / 280.0)
TIME_SCALE = 4.0
FLOW_VELOCITY = 1.0
AXIAL_DISPERSION = 0.3
RADIAL_SPREADING = 0.2
BINDING_STRENGTH = (1.5, 0.6)
HEAT_EXPONENT = (0.5, 0.3)
KINETIC = (1.2, 0.7)
CAPACITY = (2.0, 1.0)
SORPTION_HEAT = (0.4, 0.25)
PURGE_GAIN = 1.5

MESH = pl.DeviceIdType.MESH


def _kernel(n_tm, plan, valve, st, ad, res, adj, x_st, x_ad, n_st, n_ad, h_st, h_ad, send, recv):
    inst, comp, beds, nz, nr = st.shape
    me = lax.axis_index("tm")
    sec = lax.axis_index("sec")
    core = lax.rem(me, 2)
    pair = (me + 1 - 2 * core, sec)
    cross = (lax.rem(me + 2 * core - 1 + n_tm, n_tm), sec)
    partner = (me, 1 - sec)

    barrier = pltpu.get_barrier_semaphore()
    for dev in (pair, cross, partner):
        pl.semaphore_signal(barrier, inc=1, device_id=dev, device_id_type=MESH)
    pl.semaphore_wait(barrier, 3)

    def rcopy(src, dst, i, dev):
        cp = pltpu.make_async_remote_copy(
            src_ref=src, dst_ref=dst, send_sem=send.at[i], recv_sem=recv.at[i],
            device_id=dev, device_id_type=MESH,
        )
        cp.start()
        return cp

    row_src = (nz - 1) * (1 - sec)
    halo_copies = [
        rcopy(src.at[:, :, :, pl.ds(row_src, 1), :], dst.at[:, :, :, pl.ds(0, 1), :], 4 + i, partner)
        for i, (src, dst) in enumerate(((st, h_st), (ad, h_ad)))
    ]
    far_st = rcopy(st, x_st, 0, cross)
    far_ad = rcopy(ad, x_ad, 1, cross)
    near_st = rcopy(st, n_st, 2, pair)
    near_ad = rcopy(ad, n_ad, 3, pair)

    for cp in halo_copies:
        cp.wait_recv()

    sec_f = sec.astype(jnp.float32)
    row = lax.broadcasted_iota(jnp.int32, (nz, nr), 0)
    lane = lax.broadcasted_iota(jnp.int32, (nz, nr), 1)
    first_row = row == 0
    last_row = row == nz - 1
    first_lane = lane == 0
    last_lane = lane == nr - 1

    def radial(x):
        lower = jnp.where(first_lane, 0.0, pltpu.roll(x, 1, 1))
        upper = jnp.where(last_lane, 0.0, pltpu.roll(x, nr - 1, 1))
        return upper - 2.0 * x + lower

    def axial(x, below, above):
        zm = jnp.where(first_row, below, pltpu.roll(x, 1, 0))
        zp = jnp.where(last_row, above, pltpu.roll(x, nz - 1, 0))
        return zm, zp

    def transport(x, below, above):
        zm, zp = axial(x, below, above)
        out = FLOW_VELOCITY * (x - zm) - AXIAL_DISPERSION * (zp - 2.0 * x + zm)
        return out - RADIAL_SPREADING * radial(x)

    def transport_t(lam, below, above):
        lm, lp = axial(lam, below, above)
        out = FLOW_VELOCITY * (lam - lp) - AXIAL_DISPERSION * (lm - 2.0 * lam + lp)
        return out - RADIAL_SPREADING * radial(lam)

    def spatial_body(t, carry):
        for b in range(beds):
            x = [st[t, c, b] for c in range(comp)]
            lam = [ad[t, c, b] for c in range(comp)]
            hs = [h_st[t, c, b, 0:1, :] for c in range(comp)]
            ha = [h_ad[t, c, b, 0:1, :] for c in range(comp)]
            y1, y2, y3, q1, q2, temp = x
            b1 = BINDING_STRENGTH[0] * jnp.exp(HEAT_EXPONENT[0] * temp)
            b2 = BINDING_STRENGTH[1] * jnp.exp(HEAT_EXPONENT[1] * temp)
            den = 1.0 + b1 * y1 + b2 * y2
            p1 = b1 * y1 / den
            p2 = b2 * y2 / den
            rate1 = KINETIC[0] * (CAPACITY[0] * p1 - q1)
            rate2 = KINETIC[1] * (CAPACITY[1] * p2 - q2)
            tr = {}
            trt = {}
            for c in (0, 1, 2, 5):
                below = hs[c] * sec_f
                above = hs[c] * (1.0 - sec_f)
                tr[c] = transport(x[c], below, above)
                lbelow = ha[c] * sec_f
                labove = ha[c] * (1.0 - sec_f)
                trt[c] = transport_t(lam[c], lbelow, labove)
            res[t, 0, b] = tr[0] + rate1
            res[t, 1, b] = tr[1] + rate2
            res[t, 2, b] = tr[2]
            res[t, 3, b] = -rate1
            res[t, 4, b] = -rate2
            res[t, 5, b] = tr[5] - (SORPTION_HEAT[0] * rate1 + SORPTION_HEAT[1] * rate2)
            mu1 = lam[0] - lam[3] - SORPTION_HEAT[0] * lam[5]
            mu2 = lam[1] - lam[4] - SORPTION_HEAT[1] * lam[5]
            n1 = (KINETIC[0] * CAPACITY[0]) * mu1
            n2 = (KINETIC[1] * CAPACITY[1]) * mu2
            cden = -(n1 * p1 + n2 * p2) / den
            cu1 = n1 / den + cden
            cu2 = n2 / den + cden
            adj[t, 0, b] = trt[0] + b1 * cu1
            adj[t, 1, b] = trt[1] + b2 * cu2
            adj[t, 2, b] = trt[2]
            adj[t, 3, b] = -KINETIC[0] * mu1
            adj[t, 4, b] = -KINETIC[1] * mu2
            adj[t, 5, b] = trt[5] + (HEAT_EXPONENT[0] * y1 * b1 * cu1 + HEAT_EXPONENT[1] * y2 * b2 * cu2)
        return carry

    lax.fori_loop(0, inst, spatial_body, 0)

    @pl.when(sec == 1)
    def _():
        def purge_body(t, carry):
            srcs = [lax.rem(b + plan[t, b], beds) for b in range(beds)]
            opens = [jnp.full((1, nr), valve[t, b], jnp.int32) != 0 for b in range(beds)]
            for c in range(3):
                ys = [st[t, c, b, nz - 1 : nz, :] for b in range(beds)]
                ls = [ad[t, c, b, nz - 1 : nz, :] for b in range(beds)]
                for b in range(beds):
                    inc = jnp.zeros((1, nr), jnp.float32)
                    for bp in range(beds):
                        inc = inc + jnp.where(srcs[b] == bp, ys[bp], 0.0)
                    term = jnp.where(opens[b], PURGE_GAIN * (ys[b] - inc), 0.0)
                    res[t, c, b, nz - 1 : nz, :] = res[t, c, b, nz - 1 : nz, :] + term
                    back = jnp.where(opens[b], PURGE_GAIN * ls[b], 0.0)
                    for bb in range(beds):
                        hit = jnp.logical_and(opens[bb], srcs[bb] == b)
                        back = back - jnp.where(hit, PURGE_GAIN * ls[bb], 0.0)
                    adj[t, c, b, nz - 1 : nz, :] = adj[t, c, b, nz - 1 : nz, :] + back
            return carry

        lax.fori_loop(0, inst, purge_body, 0)

    near_st.wait_recv()
    near_ad.wait_recv()

    @pl.when(core == 0)
    def _():
        _time_terms(res, adj, res, adj, st, ad, None, (n_st, n_ad), False, False)

    @pl.when(core == 1)
    def _():
        _time_terms(res, adj, res, adj, st, ad, (n_st, n_ad), None, True, False)

    far_st.wait_recv()
    far_ad.wait_recv()

    for cp in halo_copies + [far_st, far_ad, near_st, near_ad]:
        cp.wait_send()


def _time_terms(out_res, out_adj, in_res, in_adj, st, ad, lo, hi, cross_right, use_far):
    inst, comp = st.shape[0], st.shape[1]

    def body(c, carry):
        for t in range(inst):
            acc_s = None
            acc_a = None
            for k, w in enumerate(STENCIL):
                s = k + 1
                d_s = None
                d_a = None
                for j, sign in ((t + s, 1.0), (t - s, -1.0)):
                    if j >= inst:
                        far = cross_right
                    elif j < 0:
                        far = not cross_right
                    else:
                        far = False
                    if far != use_far:
                        continue
                    if j >= inst:
                        pair = (hi[0], hi[1], j - inst)
                    elif j < 0:
                        pair = (lo[0], lo[1], j + inst)
                    else:
                        pair = (st, ad, j)
                    xs, xa = pair[0][pair[2], c], pair[1][pair[2], c]
                    if sign < 0:
                        xs, xa = -xs, -xa
                    d_s = xs if d_s is None else d_s + xs
                    d_a = xa if d_a is None else d_a + xa
                if d_s is None:
                    continue
                acc_s = w * d_s if acc_s is None else acc_s + w * d_s
                acc_a = w * d_a if acc_a is None else acc_a + w * d_a
            if acc_s is None:
                continue
            out_res[t, c] = TIME_SCALE * acc_s + in_res[t, c]
            out_adj[t, c] = in_adj[t, c] - TIME_SCALE * acc_a
        return carry

    lax.fori_loop(0, comp, body, 0)


def _finish(x_st, x_ad, res_p, adj_p, res, adj):
    core = lax.rem(lax.axis_index("tm"), 2)

    @pl.when(core == 0)
    def _():
        _time_terms(res, adj, res_p, adj_p, x_st, x_ad, (x_st, x_ad), None, False, True)

    @pl.when(core == 1)
    def _():
        _time_terms(res, adj, res_p, adj_p, x_st, x_ad, None, (x_st, x_ad), True, True)


def local(state, adjoint, plan, valve):
    n_tm = lax.axis_size("tm")
    inst, comp, beds, nz, nr = state.shape
    block = jax.ShapeDtypeStruct(state.shape, jnp.float32)
    vmem = pl.BlockSpec(memory_space=pltpu.VMEM)
    halo_shape = (inst, comp, beds, 8, nr)

    def kern(*refs):
        _kernel(n_tm, *refs)

    res_p, adj_p, x_st, x_ad = pl.pallas_call(
        kern,
        out_shape=(block,) * 4,
        in_specs=[pl.BlockSpec(memory_space=pltpu.SMEM)] * 2 + [vmem, vmem],
        out_specs=(vmem,) * 4,
        scratch_shapes=[pltpu.VMEM(state.shape, jnp.float32)] * 2
        + [pltpu.VMEM(halo_shape, jnp.float32)] * 2
        + [pltpu.SemaphoreType.DMA((6,)), pltpu.SemaphoreType.DMA((6,))],
        compiler_params=pltpu.CompilerParams(collective_id=0, has_side_effects=True),
    )(plan, valve, state, adjoint)
    res, adj = pl.pallas_call(
        _finish,
        out_shape=(block, block),
        in_specs=[vmem] * 4,
        out_specs=(vmem, vmem),
    )(x_st, x_ad, res_p, adj_p)
    return res, adj


def solution(mesh):
    return jax.shard_map(
        local,
        mesh=mesh,
        in_specs=(
            P("tm", None, None, "sec", None),
            P("tm", None, None, "sec", None),
            P("tm", None),
            P("tm", None),
        ),
        out_specs=(P("tm", None, None, "sec", None), P("tm", None, None, "sec", None)),
        check_vma=False,
    )
```

```python
import jax
import jax.numpy as jnp
from jax import lax
from jax.experimental import pallas as pl
from jax.experimental.pallas import tpu as pltpu
from jax.sharding import PartitionSpec as P

STENCIL = (0.8, -0.2, 4.0 / 105.0, -1.0 / 280.0)
TIME_SCALE = 4.0
FLOW_VELOCITY = 1.0
AXIAL_DISPERSION = 0.3
RADIAL_SPREADING = 0.2
BINDING_STRENGTH = (1.5, 0.6)
HEAT_EXPONENT = (0.5, 0.3)
KINETIC = (1.2, 0.7)
CAPACITY = (2.0, 1.0)
SORPTION_HEAT = (0.4, 0.25)
PURGE_GAIN = 1.5

MESH = pl.DeviceIdType.MESH


def _kernel(n_tm, plan, valve, st, ad, res, adj, x_st, x_ad, n_st, n_ad, h_st, h_ad, send, recv):
    inst, comp, beds, nz, nr = st.shape
    me = lax.axis_index("tm")
    sec = lax.axis_index("sec")
    core = lax.rem(me, 2)
    pair = (me + 1 - 2 * core, sec)
    cross = (lax.rem(me + 2 * core - 1 + n_tm, n_tm), sec)
    partner = (me, 1 - sec)

    barrier = pltpu.get_barrier_semaphore()
    for dev in (pair, cross, partner):
        pl.semaphore_signal(barrier, inc=1, device_id=dev, device_id_type=MESH)
    pl.semaphore_wait(barrier, 3)

    def rcopy(src, dst, i, dev):
        cp = pltpu.make_async_remote_copy(
            src_ref=src, dst_ref=dst, send_sem=send.at[i], recv_sem=recv.at[i],
            device_id=dev, device_id_type=MESH,
        )
        cp.start()
        return cp

    row_src = (nz - 1) * (1 - sec)
    halo_copies = [
        rcopy(src.at[:, :, :, pl.ds(row_src, 1), :], dst.at[:, :, :, pl.ds(0, 1), :], 4 + i, partner)
        for i, (src, dst) in enumerate(((st, h_st), (ad, h_ad)))
    ]
    far_st = rcopy(st, x_st, 0, cross)
    far_ad = rcopy(ad, x_ad, 1, cross)
    near_st = rcopy(st, n_st, 2, pair)
    near_ad = rcopy(ad, n_ad, 3, pair)

    for cp in halo_copies:
        cp.wait_recv()

    sec_f = sec.astype(jnp.float32)
    row = lax.broadcasted_iota(jnp.int32, (nz, nr), 0)
    lane = lax.broadcasted_iota(jnp.int32, (nz, nr), 1)
    first_row = row == 0
    last_row = row == nz - 1
    first_lane = lane == 0
    last_lane = lane == nr - 1

    def radial(x):
        lower = jnp.where(first_lane, 0.0, pltpu.roll(x, 1, 1))
        upper = jnp.where(last_lane, 0.0, pltpu.roll(x, nr - 1, 1))
        return upper - 2.0 * x + lower

    def axial(x, below, above):
        zm = jnp.where(first_row, below, pltpu.roll(x, 1, 0))
        zp = jnp.where(last_row, above, pltpu.roll(x, nz - 1, 0))
        return zm, zp

    def transport(x, below, above):
        zm, zp = axial(x, below, above)
        out = FLOW_VELOCITY * (x - zm) - AXIAL_DISPERSION * (zp - 2.0 * x + zm)
        return out - RADIAL_SPREADING * radial(x)

    def transport_t(lam, below, above):
        lm, lp = axial(lam, below, above)
        out = FLOW_VELOCITY * (lam - lp) - AXIAL_DISPERSION * (lm - 2.0 * lam + lp)
        return out - RADIAL_SPREADING * radial(lam)

    def spatial_body(t, carry):
        for b in range(beds):
            x = [st[t, c, b] for c in range(comp)]
            lam = [ad[t, c, b] for c in range(comp)]
            hs = [h_st[t, c, b, 0:1, :] for c in range(comp)]
            ha = [h_ad[t, c, b, 0:1, :] for c in range(comp)]
            y1, y2, y3, q1, q2, temp = x
            b1 = BINDING_STRENGTH[0] * jnp.exp(HEAT_EXPONENT[0] * temp)
            b2 = BINDING_STRENGTH[1] * jnp.exp(HEAT_EXPONENT[1] * temp)
            den = 1.0 + b1 * y1 + b2 * y2
            p1 = b1 * y1 / den
            p2 = b2 * y2 / den
            rate1 = KINETIC[0] * (CAPACITY[0] * p1 - q1)
            rate2 = KINETIC[1] * (CAPACITY[1] * p2 - q2)
            tr = {}
            trt = {}
            for c in (0, 1, 2, 5):
                below = hs[c] * sec_f
                above = hs[c] * (1.0 - sec_f)
                tr[c] = transport(x[c], below, above)
                lbelow = ha[c] * sec_f
                labove = ha[c] * (1.0 - sec_f)
                trt[c] = transport_t(lam[c], lbelow, labove)
            res[t, 0, b] = tr[0] + rate1
            res[t, 1, b] = tr[1] + rate2
            res[t, 2, b] = tr[2]
            res[t, 3, b] = -rate1
            res[t, 4, b] = -rate2
            res[t, 5, b] = tr[5] - (SORPTION_HEAT[0] * rate1 + SORPTION_HEAT[1] * rate2)
            mu1 = lam[0] - lam[3] - SORPTION_HEAT[0] * lam[5]
            mu2 = lam[1] - lam[4] - SORPTION_HEAT[1] * lam[5]
            n1 = (KINETIC[0] * CAPACITY[0]) * mu1
            n2 = (KINETIC[1] * CAPACITY[1]) * mu2
            cden = -(n1 * p1 + n2 * p2) / den
            cu1 = n1 / den + cden
            cu2 = n2 / den + cden
            adj[t, 0, b] = trt[0] + b1 * cu1
            adj[t, 1, b] = trt[1] + b2 * cu2
            adj[t, 2, b] = trt[2]
            adj[t, 3, b] = -KINETIC[0] * mu1
            adj[t, 4, b] = -KINETIC[1] * mu2
            adj[t, 5, b] = trt[5] + (HEAT_EXPONENT[0] * y1 * b1 * cu1 + HEAT_EXPONENT[1] * y2 * b2 * cu2)
        return carry

    lax.fori_loop(0, inst, spatial_body, 0)

    @pl.when(sec == 1)
    def _():
        def purge_body(t, carry):
            srcs = [lax.rem(b + plan[t, b], beds) for b in range(beds)]
            opens = [jnp.full((1, nr), valve[t, b], jnp.int32) != 0 for b in range(beds)]
            for c in range(3):
                ys = [st[t, c, b, nz - 1 : nz, :] for b in range(beds)]
                ls = [ad[t, c, b, nz - 1 : nz, :] for b in range(beds)]
                for b in range(beds):
                    inc = jnp.zeros((1, nr), jnp.float32)
                    for bp in range(beds):
                        inc = inc + jnp.where(srcs[b] == bp, ys[bp], 0.0)
                    term = jnp.where(opens[b], PURGE_GAIN * (ys[b] - inc), 0.0)
                    res[t, c, b, nz - 1 : nz, :] = res[t, c, b, nz - 1 : nz, :] + term
                    back = jnp.where(opens[b], PURGE_GAIN * ls[b], 0.0)
                    for bb in range(beds):
                        hit = jnp.logical_and(opens[bb], srcs[bb] == b)
                        back = back - jnp.where(hit, PURGE_GAIN * ls[bb], 0.0)
                    adj[t, c, b, nz - 1 : nz, :] = adj[t, c, b, nz - 1 : nz, :] + back
            return carry

        lax.fori_loop(0, inst, purge_body, 0)

    near_st.wait_recv()
    near_ad.wait_recv()

    @pl.when(core == 0)
    def _():
        _time_terms(res, adj, res, adj, st, ad, None, (n_st, n_ad), False, False)

    @pl.when(core == 1)
    def _():
        _time_terms(res, adj, res, adj, st, ad, (n_st, n_ad), None, True, False)

    far_st.wait_recv()
    far_ad.wait_recv()

    for cp in halo_copies + [far_st, far_ad, near_st, near_ad]:
        cp.wait_send()


def _time_terms(out_res, out_adj, in_res, in_adj, st, ad, lo, hi, cross_right, use_far):
    inst, comp = st.shape[0], st.shape[1]

    def body(c, carry):
        for t in range(inst):
            acc_s = None
            acc_a = None
            for k, w in enumerate(STENCIL):
                s = k + 1
                d_s = None
                d_a = None
                for j, sign in ((t + s, 1.0), (t - s, -1.0)):
                    if j >= inst:
                        far = cross_right
                    elif j < 0:
                        far = not cross_right
                    else:
                        far = False
                    if far != use_far:
                        continue
                    if j >= inst:
                        pair = (hi[0], hi[1], j - inst)
                    elif j < 0:
                        pair = (lo[0], lo[1], j + inst)
                    else:
                        pair = (st, ad, j)
                    xs, xa = pair[0][pair[2], c], pair[1][pair[2], c]
                    if sign < 0:
                        xs, xa = -xs, -xa
                    d_s = xs if d_s is None else d_s + xs
                    d_a = xa if d_a is None else d_a + xa
                if d_s is None:
                    continue
                acc_s = w * d_s if acc_s is None else acc_s + w * d_s
                acc_a = w * d_a if acc_a is None else acc_a + w * d_a
            if acc_s is None:
                continue
            out_res[t, c] = TIME_SCALE * acc_s + in_res[t, c]
            out_adj[t, c] = in_adj[t, c] - TIME_SCALE * acc_a
        return carry

    lax.fori_loop(0, comp, body, 0)


def _finish(x_st, x_ad, res_p, adj_p, res, adj):
    core = lax.rem(lax.axis_index("tm"), 2)

    @pl.when(core == 0)
    def _():
        _time_terms(res, adj, res_p, adj_p, x_st, x_ad, (x_st, x_ad), None, False, True)

    @pl.when(core == 1)
    def _():
        _time_terms(res, adj, res_p, adj_p, x_st, x_ad, None, (x_st, x_ad), True, True)


def local(state, adjoint, plan, valve):
    n_tm = lax.axis_size("tm")
    inst, comp, beds, nz, nr = state.shape
    block = jax.ShapeDtypeStruct(state.shape, jnp.float32)
    vmem = pl.BlockSpec(memory_space=pltpu.VMEM)
    halo_shape = (inst, comp, beds, 8, nr)

    def kern(*refs):
        _kernel(n_tm, *refs)

    res_p, adj_p, x_st, x_ad = pl.pallas_call(
        kern,
        out_shape=(block,) * 4,
        in_specs=[pl.BlockSpec(memory_space=pltpu.SMEM)] * 2 + [vmem, vmem],
        out_specs=(vmem,) * 4,
        scratch_shapes=[pltpu.VMEM(state.shape, jnp.float32)] * 2
        + [pltpu.VMEM(halo_shape, jnp.float32)] * 2
        + [pltpu.SemaphoreType.DMA((6,)), pltpu.SemaphoreType.DMA((6,))],
        compiler_params=pltpu.CompilerParams(collective_id=0, has_side_effects=True),
    )(plan, valve, state, adjoint)
    per_comp = pl.BlockSpec((inst, 1, beds, nz, nr), lambda c: (0, c, 0, 0, 0))
    res, adj = pl.pallas_call(
        _finish,
        out_shape=(block, block),
        grid=(comp,),
        in_specs=[per_comp] * 4,
        out_specs=(per_comp, per_comp),
    )(x_st, x_ad, res_p, adj_p)
    return res, adj


def solution(mesh):
    return jax.shard_map(
        local,
        mesh=mesh,
        in_specs=(
            P("tm", None, None, "sec", None),
            P("tm", None, None, "sec", None),
            P("tm", None),
            P("tm", None),
        ),
        out_specs=(P("tm", None, None, "sec", None), P("tm", None, None, "sec", None)),
        check_vma=False,
    )
```

```python
import jax
import jax.numpy as jnp
from jax import lax
from jax.experimental import pallas as pl
from jax.experimental.pallas import tpu as pltpu
from jax.sharding import PartitionSpec as P

STENCIL = (0.8, -0.2, 4.0 / 105.0, -1.0 / 280.0)
TIME_SCALE = 4.0
FLOW_VELOCITY = 1.0
AXIAL_DISPERSION = 0.3
RADIAL_SPREADING = 0.2
BINDING_STRENGTH = (1.5, 0.6)
HEAT_EXPONENT = (0.5, 0.3)
KINETIC = (1.2, 0.7)
CAPACITY = (2.0, 1.0)
SORPTION_HEAT = (0.4, 0.25)
PURGE_GAIN = 1.5

MESH = pl.DeviceIdType.MESH


def _kernel(n_tm, plan, valve, st, ad, res, adj, x_st, x_ad, n_st, n_ad, h_st, h_ad, send, recv):
    inst, comp, beds, nz, nr = st.shape
    me = lax.axis_index("tm")
    sec = lax.axis_index("sec")
    core = lax.rem(me, 2)
    pair = (me + 1 - 2 * core, sec)
    cross = (lax.rem(me + 2 * core - 1 + n_tm, n_tm), sec)
    partner = (me, 1 - sec)

    barrier = pltpu.get_barrier_semaphore()
    for dev in (pair, cross, partner):
        pl.semaphore_signal(barrier, inc=1, device_id=dev, device_id_type=MESH)
    pl.semaphore_wait(barrier, 3)

    def rcopy(src, dst, i, dev):
        cp = pltpu.make_async_remote_copy(
            src_ref=src, dst_ref=dst, send_sem=send.at[i], recv_sem=recv.at[i],
            device_id=dev, device_id_type=MESH,
        )
        cp.start()
        return cp

    row_src = (nz - 1) * (1 - sec)
    halo_copies = [
        rcopy(src.at[:, :, :, pl.ds(row_src, 1), :], dst.at[:, :, :, pl.ds(0, 1), :], 4 + i, partner)
        for i, (src, dst) in enumerate(((st, h_st), (ad, h_ad)))
    ]
    far_st = rcopy(st, x_st, 0, cross)
    far_ad = rcopy(ad, x_ad, 1, cross)
    near_st = rcopy(st, n_st, 2, pair)
    near_ad = rcopy(ad, n_ad, 3, pair)

    for cp in halo_copies:
        cp.wait_recv()

    sec_f = sec.astype(jnp.float32)
    row = lax.broadcasted_iota(jnp.int32, (nz, nr), 0)
    lane = lax.broadcasted_iota(jnp.int32, (nz, nr), 1)
    first_row = row == 0
    last_row = row == nz - 1
    first_lane = lane == 0
    last_lane = lane == nr - 1

    def radial(x):
        lower = jnp.where(first_lane, 0.0, pltpu.roll(x, 1, 1))
        upper = jnp.where(last_lane, 0.0, pltpu.roll(x, nr - 1, 1))
        return upper - 2.0 * x + lower

    def axial(x, below, above):
        zm = jnp.where(first_row, below, pltpu.roll(x, 1, 0))
        zp = jnp.where(last_row, above, pltpu.roll(x, nz - 1, 0))
        return zm, zp

    def transport(x, below, above):
        zm, zp = axial(x, below, above)
        out = FLOW_VELOCITY * (x - zm) - AXIAL_DISPERSION * (zp - 2.0 * x + zm)
        return out - RADIAL_SPREADING * radial(x)

    def transport_t(lam, below, above):
        lm, lp = axial(lam, below, above)
        out = FLOW_VELOCITY * (lam - lp) - AXIAL_DISPERSION * (lm - 2.0 * lam + lp)
        return out - RADIAL_SPREADING * radial(lam)

    def spatial_body(t, carry):
        for b in range(beds):
            x = [st[t, c, b] for c in range(comp)]
            lam = [ad[t, c, b] for c in range(comp)]
            hs = [h_st[t, c, b, 0:1, :] for c in range(comp)]
            ha = [h_ad[t, c, b, 0:1, :] for c in range(comp)]
            y1, y2, y3, q1, q2, temp = x
            b1 = BINDING_STRENGTH[0] * jnp.exp(HEAT_EXPONENT[0] * temp)
            b2 = BINDING_STRENGTH[1] * jnp.exp(HEAT_EXPONENT[1] * temp)
            den = 1.0 + b1 * y1 + b2 * y2
            p1 = b1 * y1 / den
            p2 = b2 * y2 / den
            rate1 = KINETIC[0] * (CAPACITY[0] * p1 - q1)
            rate2 = KINETIC[1] * (CAPACITY[1] * p2 - q2)
            tr = {}
            trt = {}
            for c in (0, 1, 2, 5):
                below = hs[c] * sec_f
                above = hs[c] * (1.0 - sec_f)
                tr[c] = transport(x[c], below, above)
                lbelow = ha[c] * sec_f
                labove = ha[c] * (1.0 - sec_f)
                trt[c] = transport_t(lam[c], lbelow, labove)
            res[t, 0, b] = tr[0] + rate1
            res[t, 1, b] = tr[1] + rate2
            res[t, 2, b] = tr[2]
            res[t, 3, b] = -rate1
            res[t, 4, b] = -rate2
            res[t, 5, b] = tr[5] - (SORPTION_HEAT[0] * rate1 + SORPTION_HEAT[1] * rate2)
            mu1 = lam[0] - lam[3] - SORPTION_HEAT[0] * lam[5]
            mu2 = lam[1] - lam[4] - SORPTION_HEAT[1] * lam[5]
            n1 = (KINETIC[0] * CAPACITY[0]) * mu1
            n2 = (KINETIC[1] * CAPACITY[1]) * mu2
            cden = -(n1 * p1 + n2 * p2) / den
            cu1 = n1 / den + cden
            cu2 = n2 / den + cden
            adj[t, 0, b] = trt[0] + b1 * cu1
            adj[t, 1, b] = trt[1] + b2 * cu2
            adj[t, 2, b] = trt[2]
            adj[t, 3, b] = -KINETIC[0] * mu1
            adj[t, 4, b] = -KINETIC[1] * mu2
            adj[t, 5, b] = trt[5] + (HEAT_EXPONENT[0] * y1 * b1 * cu1 + HEAT_EXPONENT[1] * y2 * b2 * cu2)
        return carry

    lax.fori_loop(0, inst, spatial_body, 0)

    @pl.when(sec == 1)
    def _():
        def purge_body(t, carry):
            srcs = [lax.rem(b + plan[t, b], beds) for b in range(beds)]
            opens = [jnp.full((1, nr), valve[t, b], jnp.int32) != 0 for b in range(beds)]
            for c in range(3):
                ys = [st[t, c, b, nz - 1 : nz, :] for b in range(beds)]
                ls = [ad[t, c, b, nz - 1 : nz, :] for b in range(beds)]
                for b in range(beds):
                    inc = jnp.zeros((1, nr), jnp.float32)
                    for bp in range(beds):
                        inc = inc + jnp.where(srcs[b] == bp, ys[bp], 0.0)
                    term = jnp.where(opens[b], PURGE_GAIN * (ys[b] - inc), 0.0)
                    res[t, c, b, nz - 1 : nz, :] = res[t, c, b, nz - 1 : nz, :] + term
                    back = jnp.where(opens[b], PURGE_GAIN * ls[b], 0.0)
                    for bb in range(beds):
                        hit = jnp.logical_and(opens[bb], srcs[bb] == b)
                        back = back - jnp.where(hit, PURGE_GAIN * ls[bb], 0.0)
                    adj[t, c, b, nz - 1 : nz, :] = adj[t, c, b, nz - 1 : nz, :] + back
            return carry

        lax.fori_loop(0, inst, purge_body, 0)

    near_st.wait_recv()
    near_ad.wait_recv()

    @pl.when(core == 0)
    def _():
        _time_terms(res, adj, res, adj, st, ad, None, (n_st, n_ad), False, False)

    @pl.when(core == 1)
    def _():
        _time_terms(res, adj, res, adj, st, ad, (n_st, n_ad), None, True, False)

    far_st.wait_recv()
    far_ad.wait_recv()

    for cp in halo_copies + [far_st, far_ad, near_st, near_ad]:
        cp.wait_send()


def _time_terms(out_res, out_adj, in_res, in_adj, st, ad, lo, hi, cross_right, use_far):
    inst, comp = st.shape[0], st.shape[1]

    def body(c, carry):
        for t in range(inst):
            acc_s = None
            acc_a = None
            for k, w in enumerate(STENCIL):
                s = k + 1
                d_s = None
                d_a = None
                for j, sign in ((t + s, 1.0), (t - s, -1.0)):
                    if j >= inst:
                        far = cross_right
                    elif j < 0:
                        far = not cross_right
                    else:
                        far = False
                    if far != use_far:
                        continue
                    if j >= inst:
                        pair = (hi[0], hi[1], j - inst)
                    elif j < 0:
                        pair = (lo[0], lo[1], j + inst)
                    else:
                        pair = (st, ad, j)
                    xs, xa = pair[0][pair[2], c], pair[1][pair[2], c]
                    if sign < 0:
                        xs, xa = -xs, -xa
                    d_s = xs if d_s is None else d_s + xs
                    d_a = xa if d_a is None else d_a + xa
                if d_s is None:
                    continue
                acc_s = w * d_s if acc_s is None else acc_s + w * d_s
                acc_a = w * d_a if acc_a is None else acc_a + w * d_a
            if acc_s is None:
                continue
            out_res[t, c] = TIME_SCALE * acc_s + in_res[t, c]
            out_adj[t, c] = in_adj[t, c] - TIME_SCALE * acc_a
        return carry

    lax.fori_loop(0, comp, body, 0)


def _finish(x_st, x_ad, res_p, adj_p, res, adj):
    core = lax.rem(lax.axis_index("tm"), 2)

    @pl.when(core == 0)
    def _():
        _time_terms(res, adj, res_p, adj_p, x_st, x_ad, (x_st, x_ad), None, False, True)

    @pl.when(core == 1)
    def _():
        _time_terms(res, adj, res_p, adj_p, x_st, x_ad, None, (x_st, x_ad), True, True)


def local(state, adjoint, plan, valve):
    n_tm = lax.axis_size("tm")
    inst, comp, beds, nz, nr = state.shape
    block = jax.ShapeDtypeStruct(state.shape, jnp.float32)
    vmem = pl.BlockSpec(memory_space=pltpu.VMEM)
    halo_shape = (inst, comp, beds, 8, nr)

    def kern(*refs):
        _kernel(n_tm, *refs)

    res_p, adj_p, x_st, x_ad = pl.pallas_call(
        kern,
        out_shape=(block,) * 4,
        in_specs=[pl.BlockSpec(memory_space=pltpu.SMEM)] * 2 + [vmem, vmem],
        out_specs=(vmem,) * 4,
        scratch_shapes=[pltpu.VMEM(state.shape, jnp.float32)] * 2
        + [pltpu.VMEM(halo_shape, jnp.float32)] * 2
        + [pltpu.SemaphoreType.DMA((6,)), pltpu.SemaphoreType.DMA((6,))],
        compiler_params=pltpu.CompilerParams(collective_id=0, has_side_effects=True),
    )(plan, valve, state, adjoint)
    core = lax.rem(lax.axis_index("tm"), 2)

    def cross_terms(x):
        rows = []
        for t in range(inst):
            left = None
            right = None
            for k, w in enumerate(STENCIL):
                s = k + 1
                if t - s < 0:
                    term = -w * x[t - s + inst]
                    left = term if left is None else left + term
                if t + s >= inst:
                    term = w * x[t + s - inst]
                    right = term if right is None else right + term
            rows.append(jnp.where(core == 0, left, right))
        return TIME_SCALE * jnp.stack(rows)

    res = res_p + cross_terms(x_st)
    adj = adj_p - cross_terms(x_ad)
    return res, adj


def solution(mesh):
    return jax.shard_map(
        local,
        mesh=mesh,
        in_specs=(
            P("tm", None, None, "sec", None),
            P("tm", None, None, "sec", None),
            P("tm", None),
            P("tm", None),
        ),
        out_specs=(P("tm", None, None, "sec", None), P("tm", None, None, "sec", None)),
        check_vma=False,
    )
```

```python
import jax
import jax.numpy as jnp
from jax import lax
from jax.experimental import pallas as pl
from jax.experimental.pallas import tpu as pltpu
from jax.sharding import PartitionSpec as P

STENCIL = (0.8, -0.2, 4.0 / 105.0, -1.0 / 280.0)
TIME_SCALE = 4.0
FLOW_VELOCITY = 1.0
AXIAL_DISPERSION = 0.3
RADIAL_SPREADING = 0.2
BINDING_STRENGTH = (1.5, 0.6)
HEAT_EXPONENT = (0.5, 0.3)
KINETIC = (1.2, 0.7)
CAPACITY = (2.0, 1.0)
SORPTION_HEAT = (0.4, 0.25)
PURGE_GAIN = 1.5

MESH = pl.DeviceIdType.MESH


def _kernel(n_tm, plan, valve, st, ad, res_out, adj_out, res, adj, rv_st, rv_ad, h_st, h_ad, send, recv, osem):
    inst, comp, beds, nz, nr = st.shape
    me = lax.axis_index("tm")
    sec = lax.axis_index("sec")
    core = lax.rem(me, 2)
    pair = (me + 1 - 2 * core, sec)
    cross = (lax.rem(me + 2 * core - 1 + n_tm, n_tm), sec)
    partner = (me, 1 - sec)

    barrier = pltpu.get_barrier_semaphore()
    for dev in (pair, cross, partner):
        pl.semaphore_signal(barrier, inc=1, device_id=dev, device_id_type=MESH)
    pl.semaphore_wait(barrier, 3)

    def rcopy(src, dst, i, dev):
        cp = pltpu.make_async_remote_copy(
            src_ref=src, dst_ref=dst, send_sem=send.at[i], recv_sem=recv.at[i],
            device_id=dev, device_id_type=MESH,
        )
        cp.start()
        return cp

    row_src = (nz - 1) * (1 - sec)
    halo_copies = [
        rcopy(src.at[:, :, :, pl.ds(row_src, 1), :], dst.at[:, :, :, pl.ds(0, 1), :], 4 + i, partner)
        for i, (src, dst) in enumerate(((st, h_st), (ad, h_ad)))
    ]
    def desc(src, dst, i, dev):
        return pltpu.make_async_remote_copy(
            src_ref=src, dst_ref=dst, send_sem=send.at[i], recv_sem=recv.at[i],
            device_id=dev, device_id_type=MESH,
        )

    def far_descs(c):
        return (
            desc(st.at[:, c], rv_st.at[1 - core, :, c], 6 + c, cross),
            desc(ad.at[:, c], rv_ad.at[1 - core, :, c], 6 + comp + c, cross),
        )

    for c in range(comp):
        for cp in far_descs(c):
            cp.start()
    near_st = rcopy(st, rv_st.at[core], 2, pair)
    near_ad = rcopy(ad, rv_ad.at[core], 3, pair)

    for cp in halo_copies:
        cp.wait_recv()

    sec_f = sec.astype(jnp.float32)
    row = lax.broadcasted_iota(jnp.int32, (nz, nr), 0)
    lane = lax.broadcasted_iota(jnp.int32, (nz, nr), 1)
    first_row = row == 0
    last_row = row == nz - 1
    first_lane = lane == 0
    last_lane = lane == nr - 1

    def radial(x):
        lower = jnp.where(first_lane, 0.0, pltpu.roll(x, 1, 1))
        upper = jnp.where(last_lane, 0.0, pltpu.roll(x, nr - 1, 1))
        return upper - 2.0 * x + lower

    def axial(x, below, above):
        zm = jnp.where(first_row, below, pltpu.roll(x, 1, 0))
        zp = jnp.where(last_row, above, pltpu.roll(x, nz - 1, 0))
        return zm, zp

    def transport(x, below, above):
        zm, zp = axial(x, below, above)
        out = FLOW_VELOCITY * (x - zm) - AXIAL_DISPERSION * (zp - 2.0 * x + zm)
        return out - RADIAL_SPREADING * radial(x)

    def transport_t(lam, below, above):
        lm, lp = axial(lam, below, above)
        out = FLOW_VELOCITY * (lam - lp) - AXIAL_DISPERSION * (lm - 2.0 * lam + lp)
        return out - RADIAL_SPREADING * radial(lam)

    def spatial_body(t, carry):
        for b in range(beds):
            x = [st[t, c, b] for c in range(comp)]
            lam = [ad[t, c, b] for c in range(comp)]
            hs = [h_st[t, c, b, 0:1, :] for c in range(comp)]
            ha = [h_ad[t, c, b, 0:1, :] for c in range(comp)]
            y1, y2, y3, q1, q2, temp = x
            b1 = BINDING_STRENGTH[0] * jnp.exp(HEAT_EXPONENT[0] * temp)
            b2 = BINDING_STRENGTH[1] * jnp.exp(HEAT_EXPONENT[1] * temp)
            den = 1.0 + b1 * y1 + b2 * y2
            p1 = b1 * y1 / den
            p2 = b2 * y2 / den
            rate1 = KINETIC[0] * (CAPACITY[0] * p1 - q1)
            rate2 = KINETIC[1] * (CAPACITY[1] * p2 - q2)
            tr = {}
            trt = {}
            for c in (0, 1, 2, 5):
                below = hs[c] * sec_f
                above = hs[c] * (1.0 - sec_f)
                tr[c] = transport(x[c], below, above)
                lbelow = ha[c] * sec_f
                labove = ha[c] * (1.0 - sec_f)
                trt[c] = transport_t(lam[c], lbelow, labove)
            res[t, 0, b] = tr[0] + rate1
            res[t, 1, b] = tr[1] + rate2
            res[t, 2, b] = tr[2]
            res[t, 3, b] = -rate1
            res[t, 4, b] = -rate2
            res[t, 5, b] = tr[5] - (SORPTION_HEAT[0] * rate1 + SORPTION_HEAT[1] * rate2)
            mu1 = lam[0] - lam[3] - SORPTION_HEAT[0] * lam[5]
            mu2 = lam[1] - lam[4] - SORPTION_HEAT[1] * lam[5]
            n1 = (KINETIC[0] * CAPACITY[0]) * mu1
            n2 = (KINETIC[1] * CAPACITY[1]) * mu2
            cden = -(n1 * p1 + n2 * p2) / den
            cu1 = n1 / den + cden
            cu2 = n2 / den + cden
            adj[t, 0, b] = trt[0] + b1 * cu1
            adj[t, 1, b] = trt[1] + b2 * cu2
            adj[t, 2, b] = trt[2]
            adj[t, 3, b] = -KINETIC[0] * mu1
            adj[t, 4, b] = -KINETIC[1] * mu2
            adj[t, 5, b] = trt[5] + (HEAT_EXPONENT[0] * y1 * b1 * cu1 + HEAT_EXPONENT[1] * y2 * b2 * cu2)
        return carry

    lax.fori_loop(0, inst, spatial_body, 0)

    @pl.when(sec == 1)
    def _():
        def purge_body(t, carry):
            srcs = [lax.rem(b + plan[t, b], beds) for b in range(beds)]
            opens = [jnp.full((1, nr), valve[t, b], jnp.int32) != 0 for b in range(beds)]
            for c in range(3):
                ys = [st[t, c, b, nz - 1 : nz, :] for b in range(beds)]
                ls = [ad[t, c, b, nz - 1 : nz, :] for b in range(beds)]
                for b in range(beds):
                    inc = jnp.zeros((1, nr), jnp.float32)
                    for bp in range(beds):
                        inc = inc + jnp.where(srcs[b] == bp, ys[bp], 0.0)
                    term = jnp.where(opens[b], PURGE_GAIN * (ys[b] - inc), 0.0)
                    res[t, c, b, nz - 1 : nz, :] = res[t, c, b, nz - 1 : nz, :] + term
                    back = jnp.where(opens[b], PURGE_GAIN * ls[b], 0.0)
                    for bb in range(beds):
                        hit = jnp.logical_and(opens[bb], srcs[bb] == b)
                        back = back - jnp.where(hit, PURGE_GAIN * ls[bb], 0.0)
                    adj[t, c, b, nz - 1 : nz, :] = adj[t, c, b, nz - 1 : nz, :] + back
            return carry

        lax.fori_loop(0, inst, purge_body, 0)

    def time_pass(cross_right, use_far, comp_index=None):
        def body(c, carry):
            for t in range(inst):
                acc_s = None
                acc_a = None
                for k, w in enumerate(STENCIL):
                    s = k + 1
                    d_s = None
                    d_a = None
                    for j, sign in ((t + s, 1.0), (t - s, -1.0)):
                        if j >= inst:
                            far = cross_right
                            xs, xa = rv_st[1, j - inst, c], rv_ad[1, j - inst, c]
                        elif j < 0:
                            far = not cross_right
                            xs, xa = rv_st[0, j + inst, c], rv_ad[0, j + inst, c]
                        else:
                            far = False
                            xs, xa = st[j, c], ad[j, c]
                        if far != use_far:
                            continue
                        if sign < 0:
                            xs, xa = -xs, -xa
                        d_s = xs if d_s is None else d_s + xs
                        d_a = xa if d_a is None else d_a + xa
                    if d_s is None:
                        continue
                    acc_s = w * d_s if acc_s is None else acc_s + w * d_s
                    acc_a = w * d_a if acc_a is None else acc_a + w * d_a
                if acc_s is None:
                    continue
                res[t, c] = TIME_SCALE * acc_s + res[t, c]
                adj[t, c] = adj[t, c] - TIME_SCALE * acc_a
            return carry

        if comp_index is None:
            lax.fori_loop(0, comp, body, 0)
        else:
            body(comp_index, 0)

    near_st.wait_recv()
    near_ad.wait_recv()

    @pl.when(core == 0)
    def _():
        time_pass(False, False)

    @pl.when(core == 1)
    def _():
        time_pass(True, False)

    def out_descs(c):
        return (
            pltpu.make_async_copy(res.at[:, c], res_out.at[:, c], osem.at[c]),
            pltpu.make_async_copy(adj.at[:, c], adj_out.at[:, c], osem.at[comp + c]),
        )

    def far_body(c, carry):
        for cp in far_descs(c):
            cp.wait_recv()

        @pl.when(core == 0)
        def _():
            time_pass(False, True, c)

        @pl.when(core == 1)
        def _():
            time_pass(True, True, c)

        for cp in out_descs(c):
            cp.start()
        return carry

    lax.fori_loop(0, comp, far_body, 0)

    def drain(c, carry):
        for cp in out_descs(c):
            cp.wait()
        for cp in far_descs(c):
            cp.wait_send()
        return carry

    lax.fori_loop(0, comp, drain, 0)
    for cp in halo_copies + [near_st, near_ad]:
        cp.wait_send()


def local(state, adjoint, plan, valve):
    n_tm = lax.axis_size("tm")
    inst, comp, beds, nz, nr = state.shape
    block = jax.ShapeDtypeStruct(state.shape, jnp.float32)
    vmem = pl.BlockSpec(memory_space=pltpu.VMEM)
    halo_shape = (inst, comp, beds, 8, nr)

    def kern(*refs):
        _kernel(n_tm, *refs)

    res, adj = pl.pallas_call(
        kern,
        out_shape=(block, block),
        in_specs=[pl.BlockSpec(memory_space=pltpu.SMEM)] * 2 + [vmem, vmem],
        out_specs=(pl.BlockSpec(memory_space=pl.ANY),) * 2,
        scratch_shapes=[pltpu.VMEM(state.shape, jnp.float32)] * 2
        + [pltpu.VMEM((2,) + state.shape, jnp.float32)] * 2
        + [pltpu.VMEM(halo_shape, jnp.float32)] * 2
        + [pltpu.SemaphoreType.DMA((6 + 2 * comp,)), pltpu.SemaphoreType.DMA((6 + 2 * comp,))]
        + [pltpu.SemaphoreType.DMA((2 * comp,))],
        compiler_params=pltpu.CompilerParams(collective_id=0, has_side_effects=True),
    )(plan, valve, state, adjoint)
    return res, adj


def solution(mesh):
    return jax.shard_map(
        local,
        mesh=mesh,
        in_specs=(
            P("tm", None, None, "sec", None),
            P("tm", None, None, "sec", None),
            P("tm", None),
            P("tm", None),
        ),
        out_specs=(P("tm", None, None, "sec", None), P("tm", None, None, "sec", None)),
        check_vma=False,
    )
```

```python
import jax
import jax.numpy as jnp
from jax import lax
from jax.experimental import pallas as pl
from jax.experimental.pallas import tpu as pltpu
from jax.sharding import PartitionSpec as P

STENCIL = (0.8, -0.2, 4.0 / 105.0, -1.0 / 280.0)
TIME_SCALE = 4.0
FLOW_VELOCITY = 1.0
AXIAL_DISPERSION = 0.3
RADIAL_SPREADING = 0.2
BINDING_STRENGTH = (1.5, 0.6)
HEAT_EXPONENT = (0.5, 0.3)
KINETIC = (1.2, 0.7)
CAPACITY = (2.0, 1.0)
SORPTION_HEAT = (0.4, 0.25)
PURGE_GAIN = 1.5

MESH = pl.DeviceIdType.MESH


def _kernel(n_tm, plan, valve, st_hbm, ad_hbm, res_out, adj_out, st, ad, res, adj, rv_st, rv_ad, h_st, h_ad, send, recv, osem, lsem):
    inst, comp, beds, nz, nr = st.shape
    me = lax.axis_index("tm")
    sec = lax.axis_index("sec")
    core = lax.rem(me, 2)
    pair = (me + 1 - 2 * core, sec)
    cross = (lax.rem(me + 2 * core - 1 + n_tm, n_tm), sec)
    partner = (me, 1 - sec)

    loads = [
        pltpu.make_async_copy(st_hbm, st, lsem.at[0]),
        pltpu.make_async_copy(ad_hbm, ad, lsem.at[1]),
    ]
    for cp in loads:
        cp.start()

    barrier = pltpu.get_barrier_semaphore()
    for dev in (pair, cross, partner):
        pl.semaphore_signal(barrier, inc=1, device_id=dev, device_id_type=MESH)
    pl.semaphore_wait(barrier, 3)

    def rcopy(src, dst, i, dev):
        cp = pltpu.make_async_remote_copy(
            src_ref=src, dst_ref=dst, send_sem=send.at[i], recv_sem=recv.at[i],
            device_id=dev, device_id_type=MESH,
        )
        cp.start()
        return cp

    row_src = (nz - 1) * (1 - sec)
    halo_copies = [
        rcopy(src.at[:, :, :, pl.ds(row_src, 1), :], dst.at[:, :, :, pl.ds(0, 1), :], 4 + i, partner)
        for i, (src, dst) in enumerate(((st_hbm, h_st), (ad_hbm, h_ad)))
    ]
    def desc(src, dst, i, dev):
        return pltpu.make_async_remote_copy(
            src_ref=src, dst_ref=dst, send_sem=send.at[i], recv_sem=recv.at[i],
            device_id=dev, device_id_type=MESH,
        )

    def far_descs(c):
        return (
            desc(st_hbm.at[:, c], rv_st.at[1 - core, :, c], 6 + c, cross),
            desc(ad_hbm.at[:, c], rv_ad.at[1 - core, :, c], 6 + comp + c, cross),
        )

    for c in range(comp):
        for cp in far_descs(c):
            cp.start()
    near_st = rcopy(st_hbm, rv_st.at[core], 2, pair)
    near_ad = rcopy(ad_hbm, rv_ad.at[core], 3, pair)
    for cp in loads:
        cp.wait()

    for cp in halo_copies:
        cp.wait_recv()

    sec_f = sec.astype(jnp.float32)
    row = lax.broadcasted_iota(jnp.int32, (nz, nr), 0)
    lane = lax.broadcasted_iota(jnp.int32, (nz, nr), 1)
    first_row = row == 0
    last_row = row == nz - 1
    first_lane = lane == 0
    last_lane = lane == nr - 1

    def radial(x):
        lower = jnp.where(first_lane, 0.0, pltpu.roll(x, 1, 1))
        upper = jnp.where(last_lane, 0.0, pltpu.roll(x, nr - 1, 1))
        return upper - 2.0 * x + lower

    def axial(x, below, above):
        zm = jnp.where(first_row, below, pltpu.roll(x, 1, 0))
        zp = jnp.where(last_row, above, pltpu.roll(x, nz - 1, 0))
        return zm, zp

    def transport(x, below, above):
        zm, zp = axial(x, below, above)
        out = FLOW_VELOCITY * (x - zm) - AXIAL_DISPERSION * (zp - 2.0 * x + zm)
        return out - RADIAL_SPREADING * radial(x)

    def transport_t(lam, below, above):
        lm, lp = axial(lam, below, above)
        out = FLOW_VELOCITY * (lam - lp) - AXIAL_DISPERSION * (lm - 2.0 * lam + lp)
        return out - RADIAL_SPREADING * radial(lam)

    def spatial_body(t, carry):
        for b in range(beds):
            x = [st[t, c, b] for c in range(comp)]
            lam = [ad[t, c, b] for c in range(comp)]
            hs = [h_st[t, c, b, 0:1, :] for c in range(comp)]
            ha = [h_ad[t, c, b, 0:1, :] for c in range(comp)]
            y1, y2, y3, q1, q2, temp = x
            b1 = BINDING_STRENGTH[0] * jnp.exp(HEAT_EXPONENT[0] * temp)
            b2 = BINDING_STRENGTH[1] * jnp.exp(HEAT_EXPONENT[1] * temp)
            den = 1.0 + b1 * y1 + b2 * y2
            p1 = b1 * y1 / den
            p2 = b2 * y2 / den
            rate1 = KINETIC[0] * (CAPACITY[0] * p1 - q1)
            rate2 = KINETIC[1] * (CAPACITY[1] * p2 - q2)
            tr = {}
            trt = {}
            for c in (0, 1, 2, 5):
                below = hs[c] * sec_f
                above = hs[c] * (1.0 - sec_f)
                tr[c] = transport(x[c], below, above)
                lbelow = ha[c] * sec_f
                labove = ha[c] * (1.0 - sec_f)
                trt[c] = transport_t(lam[c], lbelow, labove)
            res[t, 0, b] = tr[0] + rate1
            res[t, 1, b] = tr[1] + rate2
            res[t, 2, b] = tr[2]
            res[t, 3, b] = -rate1
            res[t, 4, b] = -rate2
            res[t, 5, b] = tr[5] - (SORPTION_HEAT[0] * rate1 + SORPTION_HEAT[1] * rate2)
            mu1 = lam[0] - lam[3] - SORPTION_HEAT[0] * lam[5]
            mu2 = lam[1] - lam[4] - SORPTION_HEAT[1] * lam[5]
            n1 = (KINETIC[0] * CAPACITY[0]) * mu1
            n2 = (KINETIC[1] * CAPACITY[1]) * mu2
            cden = -(n1 * p1 + n2 * p2) / den
            cu1 = n1 / den + cden
            cu2 = n2 / den + cden
            adj[t, 0, b] = trt[0] + b1 * cu1
            adj[t, 1, b] = trt[1] + b2 * cu2
            adj[t, 2, b] = trt[2]
            adj[t, 3, b] = -KINETIC[0] * mu1
            adj[t, 4, b] = -KINETIC[1] * mu2
            adj[t, 5, b] = trt[5] + (HEAT_EXPONENT[0] * y1 * b1 * cu1 + HEAT_EXPONENT[1] * y2 * b2 * cu2)
        return carry

    lax.fori_loop(0, inst, spatial_body, 0)

    @pl.when(sec == 1)
    def _():
        def purge_body(t, carry):
            srcs = [lax.rem(b + plan[t, b], beds) for b in range(beds)]
            opens = [jnp.full((1, nr), valve[t, b], jnp.int32) != 0 for b in range(beds)]
            for c in range(3):
                ys = [st[t, c, b, nz - 1 : nz, :] for b in range(beds)]
                ls = [ad[t, c, b, nz - 1 : nz, :] for b in range(beds)]
                for b in range(beds):
                    inc = jnp.zeros((1, nr), jnp.float32)
                    for bp in range(beds):
                        inc = inc + jnp.where(srcs[b] == bp, ys[bp], 0.0)
                    term = jnp.where(opens[b], PURGE_GAIN * (ys[b] - inc), 0.0)
                    res[t, c, b, nz - 1 : nz, :] = res[t, c, b, nz - 1 : nz, :] + term
                    back = jnp.where(opens[b], PURGE_GAIN * ls[b], 0.0)
                    for bb in range(beds):
                        hit = jnp.logical_and(opens[bb], srcs[bb] == b)
                        back = back - jnp.where(hit, PURGE_GAIN * ls[bb], 0.0)
                    adj[t, c, b, nz - 1 : nz, :] = adj[t, c, b, nz - 1 : nz, :] + back
            return carry

        lax.fori_loop(0, inst, purge_body, 0)

    def time_pass(cross_right, use_far, comp_index=None):
        def body(c, carry):
            for t in range(inst):
                acc_s = None
                acc_a = None
                for k, w in enumerate(STENCIL):
                    s = k + 1
                    d_s = None
                    d_a = None
                    for j, sign in ((t + s, 1.0), (t - s, -1.0)):
                        if j >= inst:
                            far = cross_right
                            xs, xa = rv_st[1, j - inst, c], rv_ad[1, j - inst, c]
                        elif j < 0:
                            far = not cross_right
                            xs, xa = rv_st[0, j + inst, c], rv_ad[0, j + inst, c]
                        else:
                            far = False
                            xs, xa = st[j, c], ad[j, c]
                        if far != use_far:
                            continue
                        if sign < 0:
                            xs, xa = -xs, -xa
                        d_s = xs if d_s is None else d_s + xs
                        d_a = xa if d_a is None else d_a + xa
                    if d_s is None:
                        continue
                    acc_s = w * d_s if acc_s is None else acc_s + w * d_s
                    acc_a = w * d_a if acc_a is None else acc_a + w * d_a
                if acc_s is None:
                    continue
                res[t, c] = TIME_SCALE * acc_s + res[t, c]
                adj[t, c] = adj[t, c] - TIME_SCALE * acc_a
            return carry

        if comp_index is None:
            lax.fori_loop(0, comp, body, 0)
        else:
            body(comp_index, 0)

    near_st.wait_recv()
    near_ad.wait_recv()

    @pl.when(core == 0)
    def _():
        time_pass(False, False)

    @pl.when(core == 1)
    def _():
        time_pass(True, False)

    def out_descs(c):
        return (
            pltpu.make_async_copy(res.at[:, c], res_out.at[:, c], osem.at[c]),
            pltpu.make_async_copy(adj.at[:, c], adj_out.at[:, c], osem.at[comp + c]),
        )

    def far_body(c, carry):
        for cp in far_descs(c):
            cp.wait_recv()

        @pl.when(core == 0)
        def _():
            time_pass(False, True, c)

        @pl.when(core == 1)
        def _():
            time_pass(True, True, c)

        for cp in out_descs(c):
            cp.start()
        return carry

    lax.fori_loop(0, comp, far_body, 0)

    def drain(c, carry):
        for cp in out_descs(c):
            cp.wait()
        for cp in far_descs(c):
            cp.wait_send()
        return carry

    lax.fori_loop(0, comp, drain, 0)
    for cp in halo_copies + [near_st, near_ad]:
        cp.wait_send()


def local(state, adjoint, plan, valve):
    n_tm = lax.axis_size("tm")
    inst, comp, beds, nz, nr = state.shape
    block = jax.ShapeDtypeStruct(state.shape, jnp.float32)
    vmem = pl.BlockSpec(memory_space=pltpu.VMEM)
    halo_shape = (inst, comp, beds, 8, nr)

    def kern(*refs):
        _kernel(n_tm, *refs)

    res, adj = pl.pallas_call(
        kern,
        out_shape=(block, block),
        in_specs=[pl.BlockSpec(memory_space=pltpu.SMEM)] * 2 + [pl.BlockSpec(memory_space=pl.ANY)] * 2,
        out_specs=(pl.BlockSpec(memory_space=pl.ANY),) * 2,
        scratch_shapes=[pltpu.VMEM(state.shape, jnp.float32)] * 4
        + [pltpu.VMEM((2,) + state.shape, jnp.float32)] * 2
        + [pltpu.VMEM(halo_shape, jnp.float32)] * 2
        + [pltpu.SemaphoreType.DMA((6 + 2 * comp,)), pltpu.SemaphoreType.DMA((6 + 2 * comp,))]
        + [pltpu.SemaphoreType.DMA((2 * comp,)), pltpu.SemaphoreType.DMA((2,))],
        compiler_params=pltpu.CompilerParams(collective_id=0, has_side_effects=True),
    )(plan, valve, state, adjoint)
    return res, adj


def solution(mesh):
    return jax.shard_map(
        local,
        mesh=mesh,
        in_specs=(
            P("tm", None, None, "sec", None),
            P("tm", None, None, "sec", None),
            P("tm", None),
            P("tm", None),
        ),
        out_specs=(P("tm", None, None, "sec", None), P("tm", None, None, "sec", None)),
        check_vma=False,
    )
```

```python
import jax
import jax.numpy as jnp
from jax import lax
from jax.experimental import pallas as pl
from jax.experimental.pallas import tpu as pltpu
from jax.sharding import PartitionSpec as P

STENCIL = (0.8, -0.2, 4.0 / 105.0, -1.0 / 280.0)
TIME_SCALE = 4.0
FLOW_VELOCITY = 1.0
AXIAL_DISPERSION = 0.3
RADIAL_SPREADING = 0.2
BINDING_STRENGTH = (1.5, 0.6)
HEAT_EXPONENT = (0.5, 0.3)
KINETIC = (1.2, 0.7)
CAPACITY = (2.0, 1.0)
SORPTION_HEAT = (0.4, 0.25)
PURGE_GAIN = 1.5

MESH = pl.DeviceIdType.MESH


def _kernel(n_tm, plan, valve, st_hbm, ad_hbm, res, adj, st, ad, rv_st, rv_ad, h_st, h_ad, send, recv, lsem):
    inst, comp, beds, nz, nr = st.shape
    me = lax.axis_index("tm")
    sec = lax.axis_index("sec")
    core = lax.rem(me, 2)
    pair = (me + 1 - 2 * core, sec)
    cross = (lax.rem(me + 2 * core - 1 + n_tm, n_tm), sec)
    partner = (me, 1 - sec)

    loads = [
        pltpu.make_async_copy(st_hbm, st, lsem.at[0]),
        pltpu.make_async_copy(ad_hbm, ad, lsem.at[1]),
    ]
    for cp in loads:
        cp.start()

    barrier = pltpu.get_barrier_semaphore()
    for dev in (pair, cross, partner):
        pl.semaphore_signal(barrier, inc=1, device_id=dev, device_id_type=MESH)
    pl.semaphore_wait(barrier, 3)

    def rcopy(src, dst, i, dev):
        cp = pltpu.make_async_remote_copy(
            src_ref=src, dst_ref=dst, send_sem=send.at[i], recv_sem=recv.at[i],
            device_id=dev, device_id_type=MESH,
        )
        cp.start()
        return cp

    row_src = (nz - 1) * (1 - sec)
    halo_copies = [
        rcopy(src.at[:, :, :, pl.ds(row_src, 1), :], dst.at[:, :, :, pl.ds(0, 1), :], 4 + i, partner)
        for i, (src, dst) in enumerate(((st_hbm, h_st), (ad_hbm, h_ad)))
    ]
    def desc(src, dst, i, dev):
        return pltpu.make_async_remote_copy(
            src_ref=src, dst_ref=dst, send_sem=send.at[i], recv_sem=recv.at[i],
            device_id=dev, device_id_type=MESH,
        )

    def far_descs(c):
        return (
            desc(st_hbm.at[:, c], rv_st.at[1 - core, :, c], 6 + c, cross),
            desc(ad_hbm.at[:, c], rv_ad.at[1 - core, :, c], 6 + comp + c, cross),
        )

    for c in range(comp):
        for cp in far_descs(c):
            cp.start()
    near_st = rcopy(st_hbm, rv_st.at[core], 2, pair)
    near_ad = rcopy(ad_hbm, rv_ad.at[core], 3, pair)
    for cp in loads:
        cp.wait()

    for cp in halo_copies:
        cp.wait_recv()

    sec_f = sec.astype(jnp.float32)
    row = lax.broadcasted_iota(jnp.int32, (nz, nr), 0)
    lane = lax.broadcasted_iota(jnp.int32, (nz, nr), 1)
    first_row = row == 0
    last_row = row == nz - 1
    first_lane = lane == 0
    last_lane = lane == nr - 1

    def radial(x):
        lower = jnp.where(first_lane, 0.0, pltpu.roll(x, 1, 1))
        upper = jnp.where(last_lane, 0.0, pltpu.roll(x, nr - 1, 1))
        return upper - 2.0 * x + lower

    def axial(x, below, above):
        zm = jnp.where(first_row, below, pltpu.roll(x, 1, 0))
        zp = jnp.where(last_row, above, pltpu.roll(x, nz - 1, 0))
        return zm, zp

    def transport(x, below, above):
        zm, zp = axial(x, below, above)
        out = FLOW_VELOCITY * (x - zm) - AXIAL_DISPERSION * (zp - 2.0 * x + zm)
        return out - RADIAL_SPREADING * radial(x)

    def transport_t(lam, below, above):
        lm, lp = axial(lam, below, above)
        out = FLOW_VELOCITY * (lam - lp) - AXIAL_DISPERSION * (lm - 2.0 * lam + lp)
        return out - RADIAL_SPREADING * radial(lam)

    def spatial_body(t, carry):
        for b in range(beds):
            x = [st[t, c, b] for c in range(comp)]
            lam = [ad[t, c, b] for c in range(comp)]
            hs = [h_st[t, c, b, 0:1, :] for c in range(comp)]
            ha = [h_ad[t, c, b, 0:1, :] for c in range(comp)]
            y1, y2, y3, q1, q2, temp = x
            b1 = BINDING_STRENGTH[0] * jnp.exp(HEAT_EXPONENT[0] * temp)
            b2 = BINDING_STRENGTH[1] * jnp.exp(HEAT_EXPONENT[1] * temp)
            den = 1.0 + b1 * y1 + b2 * y2
            p1 = b1 * y1 / den
            p2 = b2 * y2 / den
            rate1 = KINETIC[0] * (CAPACITY[0] * p1 - q1)
            rate2 = KINETIC[1] * (CAPACITY[1] * p2 - q2)
            tr = {}
            trt = {}
            for c in (0, 1, 2, 5):
                below = hs[c] * sec_f
                above = hs[c] * (1.0 - sec_f)
                tr[c] = transport(x[c], below, above)
                lbelow = ha[c] * sec_f
                labove = ha[c] * (1.0 - sec_f)
                trt[c] = transport_t(lam[c], lbelow, labove)
            res[t, 0, b] = tr[0] + rate1
            res[t, 1, b] = tr[1] + rate2
            res[t, 2, b] = tr[2]
            res[t, 3, b] = -rate1
            res[t, 4, b] = -rate2
            res[t, 5, b] = tr[5] - (SORPTION_HEAT[0] * rate1 + SORPTION_HEAT[1] * rate2)
            mu1 = lam[0] - lam[3] - SORPTION_HEAT[0] * lam[5]
            mu2 = lam[1] - lam[4] - SORPTION_HEAT[1] * lam[5]
            n1 = (KINETIC[0] * CAPACITY[0]) * mu1
            n2 = (KINETIC[1] * CAPACITY[1]) * mu2
            cden = -(n1 * p1 + n2 * p2) / den
            cu1 = n1 / den + cden
            cu2 = n2 / den + cden
            adj[t, 0, b] = trt[0] + b1 * cu1
            adj[t, 1, b] = trt[1] + b2 * cu2
            adj[t, 2, b] = trt[2]
            adj[t, 3, b] = -KINETIC[0] * mu1
            adj[t, 4, b] = -KINETIC[1] * mu2
            adj[t, 5, b] = trt[5] + (HEAT_EXPONENT[0] * y1 * b1 * cu1 + HEAT_EXPONENT[1] * y2 * b2 * cu2)
        return carry

    lax.fori_loop(0, inst, spatial_body, 0)

    @pl.when(sec == 1)
    def _():
        def purge_body(t, carry):
            srcs = [lax.rem(b + plan[t, b], beds) for b in range(beds)]
            opens = [jnp.full((1, nr), valve[t, b], jnp.int32) != 0 for b in range(beds)]
            for c in range(3):
                ys = [st[t, c, b, nz - 1 : nz, :] for b in range(beds)]
                ls = [ad[t, c, b, nz - 1 : nz, :] for b in range(beds)]
                for b in range(beds):
                    inc = jnp.zeros((1, nr), jnp.float32)
                    for bp in range(beds):
                        inc = inc + jnp.where(srcs[b] == bp, ys[bp], 0.0)
                    term = jnp.where(opens[b], PURGE_GAIN * (ys[b] - inc), 0.0)
                    res[t, c, b, nz - 1 : nz, :] = res[t, c, b, nz - 1 : nz, :] + term
                    back = jnp.where(opens[b], PURGE_GAIN * ls[b], 0.0)
                    for bb in range(beds):
                        hit = jnp.logical_and(opens[bb], srcs[bb] == b)
                        back = back - jnp.where(hit, PURGE_GAIN * ls[bb], 0.0)
                    adj[t, c, b, nz - 1 : nz, :] = adj[t, c, b, nz - 1 : nz, :] + back
            return carry

        lax.fori_loop(0, inst, purge_body, 0)

    def time_pass(cross_right, use_far, comp_index=None):
        def body(c, carry):
            for t in range(inst):
                acc_s = None
                acc_a = None
                for k, w in enumerate(STENCIL):
                    s = k + 1
                    d_s = None
                    d_a = None
                    for j, sign in ((t + s, 1.0), (t - s, -1.0)):
                        if j >= inst:
                            far = cross_right
                            xs, xa = rv_st[1, j - inst, c], rv_ad[1, j - inst, c]
                        elif j < 0:
                            far = not cross_right
                            xs, xa = rv_st[0, j + inst, c], rv_ad[0, j + inst, c]
                        else:
                            far = False
                            xs, xa = st[j, c], ad[j, c]
                        if far != use_far:
                            continue
                        if sign < 0:
                            xs, xa = -xs, -xa
                        d_s = xs if d_s is None else d_s + xs
                        d_a = xa if d_a is None else d_a + xa
                    if d_s is None:
                        continue
                    acc_s = w * d_s if acc_s is None else acc_s + w * d_s
                    acc_a = w * d_a if acc_a is None else acc_a + w * d_a
                if acc_s is None:
                    continue
                res[t, c] = TIME_SCALE * acc_s + res[t, c]
                adj[t, c] = adj[t, c] - TIME_SCALE * acc_a
            return carry

        if comp_index is None:
            lax.fori_loop(0, comp, body, 0)
        else:
            body(comp_index, 0)

    near_st.wait_recv()
    near_ad.wait_recv()

    @pl.when(core == 0)
    def _():
        time_pass(False, False)

    @pl.when(core == 1)
    def _():
        time_pass(True, False)

    def far_body(c, carry):
        for cp in far_descs(c):
            cp.wait_recv()

        @pl.when(core == 0)
        def _():
            time_pass(False, True, c)

        @pl.when(core == 1)
        def _():
            time_pass(True, True, c)

        return carry

    lax.fori_loop(0, comp, far_body, 0)

    def drain(c, carry):
        for cp in far_descs(c):
            cp.wait_send()
        return carry

    lax.fori_loop(0, comp, drain, 0)
    for cp in halo_copies + [near_st, near_ad]:
        cp.wait_send()


def local(state, adjoint, plan, valve):
    n_tm = lax.axis_size("tm")
    inst, comp, beds, nz, nr = state.shape
    block = jax.ShapeDtypeStruct(state.shape, jnp.float32)
    vmem = pl.BlockSpec(memory_space=pltpu.VMEM)
    halo_shape = (inst, comp, beds, 8, nr)

    def kern(*refs):
        _kernel(n_tm, *refs)

    res, adj = pl.pallas_call(
        kern,
        out_shape=(pltpu.VMEM(state.shape, jnp.float32),) * 2,
        in_specs=[pl.BlockSpec(memory_space=pltpu.SMEM)] * 2 + [pl.BlockSpec(memory_space=pl.ANY)] * 2,
        out_specs=(vmem, vmem),
        scratch_shapes=[pltpu.VMEM(state.shape, jnp.float32)] * 2
        + [pltpu.VMEM((2,) + state.shape, jnp.float32)] * 2
        + [pltpu.VMEM(halo_shape, jnp.float32)] * 2
        + [pltpu.SemaphoreType.DMA((6 + 2 * comp,)), pltpu.SemaphoreType.DMA((6 + 2 * comp,))]
        + [pltpu.SemaphoreType.DMA((2,))],
        compiler_params=pltpu.CompilerParams(collective_id=0, has_side_effects=True),
    )(plan, valve, state, adjoint)
    return res, adj


def solution(mesh):
    return jax.shard_map(
        local,
        mesh=mesh,
        in_specs=(
            P("tm", None, None, "sec", None),
            P("tm", None, None, "sec", None),
            P("tm", None),
            P("tm", None),
        ),
        out_specs=(P("tm", None, None, "sec", None), P("tm", None, None, "sec", None)),
        check_vma=False,
    )
```

```python
import jax
import jax.numpy as jnp
from jax import lax
from jax.experimental import pallas as pl
from jax.experimental.pallas import tpu as pltpu
from jax.sharding import PartitionSpec as P

STENCIL = (0.8, -0.2, 4.0 / 105.0, -1.0 / 280.0)
TIME_SCALE = 4.0
FLOW_VELOCITY = 1.0
AXIAL_DISPERSION = 0.3
RADIAL_SPREADING = 0.2
BINDING_STRENGTH = (1.5, 0.6)
HEAT_EXPONENT = (0.5, 0.3)
KINETIC = (1.2, 0.7)
CAPACITY = (2.0, 1.0)
SORPTION_HEAT = (0.4, 0.25)
PURGE_GAIN = 1.5

MESH = pl.DeviceIdType.MESH


def _kernel(n_tm, plan, valve, st_hbm, ad_hbm, both, st, ad, rv_st, rv_ad, h_st, h_ad, send, recv, lsem):
    inst, comp, beds, nz, nr = st.shape
    res = both.at[0]
    adj = both.at[1]
    me = lax.axis_index("tm")
    sec = lax.axis_index("sec")
    core = lax.rem(me, 2)
    pair = (me + 1 - 2 * core, sec)
    cross = (lax.rem(me + 2 * core - 1 + n_tm, n_tm), sec)
    partner = (me, 1 - sec)

    loads = [
        pltpu.make_async_copy(st_hbm, st, lsem.at[0]),
        pltpu.make_async_copy(ad_hbm, ad, lsem.at[1]),
    ]
    for cp in loads:
        cp.start()

    barrier = pltpu.get_barrier_semaphore()
    for dev in (pair, cross, partner):
        pl.semaphore_signal(barrier, inc=1, device_id=dev, device_id_type=MESH)
    pl.semaphore_wait(barrier, 3)

    def rcopy(src, dst, i, dev):
        cp = pltpu.make_async_remote_copy(
            src_ref=src, dst_ref=dst, send_sem=send.at[i], recv_sem=recv.at[i],
            device_id=dev, device_id_type=MESH,
        )
        cp.start()
        return cp

    row_src = (nz - 1) * (1 - sec)
    halo_copies = [
        rcopy(src.at[:, :, :, pl.ds(row_src, 1), :], dst.at[:, :, :, pl.ds(0, 1), :], 4 + i, partner)
        for i, (src, dst) in enumerate(((st_hbm, h_st), (ad_hbm, h_ad)))
    ]
    def desc(src, dst, i, dev):
        return pltpu.make_async_remote_copy(
            src_ref=src, dst_ref=dst, send_sem=send.at[i], recv_sem=recv.at[i],
            device_id=dev, device_id_type=MESH,
        )

    def far_descs(c):
        return (
            desc(st_hbm.at[:, c], rv_st.at[1 - core, :, c], 6 + c, cross),
            desc(ad_hbm.at[:, c], rv_ad.at[1 - core, :, c], 6 + comp + c, cross),
        )

    for c in range(comp):
        for cp in far_descs(c):
            cp.start()
    near_st = rcopy(st_hbm, rv_st.at[core], 2, pair)
    near_ad = rcopy(ad_hbm, rv_ad.at[core], 3, pair)
    for cp in loads:
        cp.wait()

    for cp in halo_copies:
        cp.wait_recv()

    sec_f = sec.astype(jnp.float32)
    row = lax.broadcasted_iota(jnp.int32, (nz, nr), 0)
    lane = lax.broadcasted_iota(jnp.int32, (nz, nr), 1)
    first_row = row == 0
    last_row = row == nz - 1
    first_lane = lane == 0
    last_lane = lane == nr - 1

    def radial(x):
        lower = jnp.where(first_lane, 0.0, pltpu.roll(x, 1, 1))
        upper = jnp.where(last_lane, 0.0, pltpu.roll(x, nr - 1, 1))
        return upper - 2.0 * x + lower

    def axial(x, below, above):
        zm = jnp.where(first_row, below, pltpu.roll(x, 1, 0))
        zp = jnp.where(last_row, above, pltpu.roll(x, nz - 1, 0))
        return zm, zp

    def transport(x, below, above):
        zm, zp = axial(x, below, above)
        out = FLOW_VELOCITY * (x - zm) - AXIAL_DISPERSION * (zp - 2.0 * x + zm)
        return out - RADIAL_SPREADING * radial(x)

    def transport_t(lam, below, above):
        lm, lp = axial(lam, below, above)
        out = FLOW_VELOCITY * (lam - lp) - AXIAL_DISPERSION * (lm - 2.0 * lam + lp)
        return out - RADIAL_SPREADING * radial(lam)

    def spatial_body(t, carry):
        for b in range(beds):
            x = [st[t, c, b] for c in range(comp)]
            lam = [ad[t, c, b] for c in range(comp)]
            hs = [h_st[t, c, b, 0:1, :] for c in range(comp)]
            ha = [h_ad[t, c, b, 0:1, :] for c in range(comp)]
            y1, y2, y3, q1, q2, temp = x
            b1 = BINDING_STRENGTH[0] * jnp.exp(HEAT_EXPONENT[0] * temp)
            b2 = BINDING_STRENGTH[1] * jnp.exp(HEAT_EXPONENT[1] * temp)
            den = 1.0 + b1 * y1 + b2 * y2
            p1 = b1 * y1 / den
            p2 = b2 * y2 / den
            rate1 = KINETIC[0] * (CAPACITY[0] * p1 - q1)
            rate2 = KINETIC[1] * (CAPACITY[1] * p2 - q2)
            tr = {}
            trt = {}
            for c in (0, 1, 2, 5):
                below = hs[c] * sec_f
                above = hs[c] * (1.0 - sec_f)
                tr[c] = transport(x[c], below, above)
                lbelow = ha[c] * sec_f
                labove = ha[c] * (1.0 - sec_f)
                trt[c] = transport_t(lam[c], lbelow, labove)
            res[t, 0, b] = tr[0] + rate1
            res[t, 1, b] = tr[1] + rate2
            res[t, 2, b] = tr[2]
            res[t, 3, b] = -rate1
            res[t, 4, b] = -rate2
            res[t, 5, b] = tr[5] - (SORPTION_HEAT[0] * rate1 + SORPTION_HEAT[1] * rate2)
            mu1 = lam[0] - lam[3] - SORPTION_HEAT[0] * lam[5]
            mu2 = lam[1] - lam[4] - SORPTION_HEAT[1] * lam[5]
            n1 = (KINETIC[0] * CAPACITY[0]) * mu1
            n2 = (KINETIC[1] * CAPACITY[1]) * mu2
            cden = -(n1 * p1 + n2 * p2) / den
            cu1 = n1 / den + cden
            cu2 = n2 / den + cden
            adj[t, 0, b] = trt[0] + b1 * cu1
            adj[t, 1, b] = trt[1] + b2 * cu2
            adj[t, 2, b] = trt[2]
            adj[t, 3, b] = -KINETIC[0] * mu1
            adj[t, 4, b] = -KINETIC[1] * mu2
            adj[t, 5, b] = trt[5] + (HEAT_EXPONENT[0] * y1 * b1 * cu1 + HEAT_EXPONENT[1] * y2 * b2 * cu2)
        return carry

    lax.fori_loop(0, inst, spatial_body, 0)

    @pl.when(sec == 1)
    def _():
        def purge_body(t, carry):
            srcs = [lax.rem(b + plan[t, b], beds) for b in range(beds)]
            opens = [jnp.full((1, nr), valve[t, b], jnp.int32) != 0 for b in range(beds)]
            for c in range(3):
                ys = [st[t, c, b, nz - 1 : nz, :] for b in range(beds)]
                ls = [ad[t, c, b, nz - 1 : nz, :] for b in range(beds)]
                for b in range(beds):
                    inc = jnp.zeros((1, nr), jnp.float32)
                    for bp in range(beds):
                        inc = inc + jnp.where(srcs[b] == bp, ys[bp], 0.0)
                    term = jnp.where(opens[b], PURGE_GAIN * (ys[b] - inc), 0.0)
                    res[t, c, b, nz - 1 : nz, :] = res[t, c, b, nz - 1 : nz, :] + term
                    back = jnp.where(opens[b], PURGE_GAIN * ls[b], 0.0)
                    for bb in range(beds):
                        hit = jnp.logical_and(opens[bb], srcs[bb] == b)
                        back = back - jnp.where(hit, PURGE_GAIN * ls[bb], 0.0)
                    adj[t, c, b, nz - 1 : nz, :] = adj[t, c, b, nz - 1 : nz, :] + back
            return carry

        lax.fori_loop(0, inst, purge_body, 0)

    def time_pass(cross_right, use_far, comp_index=None):
        def body(c, carry):
            for t in range(inst):
                acc_s = None
                acc_a = None
                for k, w in enumerate(STENCIL):
                    s = k + 1
                    d_s = None
                    d_a = None
                    for j, sign in ((t + s, 1.0), (t - s, -1.0)):
                        if j >= inst:
                            far = cross_right
                            xs, xa = rv_st[1, j - inst, c], rv_ad[1, j - inst, c]
                        elif j < 0:
                            far = not cross_right
                            xs, xa = rv_st[0, j + inst, c], rv_ad[0, j + inst, c]
                        else:
                            far = False
                            xs, xa = st[j, c], ad[j, c]
                        if far != use_far:
                            continue
                        if sign < 0:
                            xs, xa = -xs, -xa
                        d_s = xs if d_s is None else d_s + xs
                        d_a = xa if d_a is None else d_a + xa
                    if d_s is None:
                        continue
                    acc_s = w * d_s if acc_s is None else acc_s + w * d_s
                    acc_a = w * d_a if acc_a is None else acc_a + w * d_a
                if acc_s is None:
                    continue
                res[t, c] = TIME_SCALE * acc_s + res[t, c]
                adj[t, c] = adj[t, c] - TIME_SCALE * acc_a
            return carry

        if comp_index is None:
            lax.fori_loop(0, comp, body, 0)
        else:
            body(comp_index, 0)

    near_st.wait_recv()
    near_ad.wait_recv()

    @pl.when(core == 0)
    def _():
        time_pass(False, False)

    @pl.when(core == 1)
    def _():
        time_pass(True, False)

    def far_body(c, carry):
        for cp in far_descs(c):
            cp.wait_recv()

        @pl.when(core == 0)
        def _():
            time_pass(False, True, c)

        @pl.when(core == 1)
        def _():
            time_pass(True, True, c)

        return carry

    lax.fori_loop(0, comp, far_body, 0)

    def drain(c, carry):
        for cp in far_descs(c):
            cp.wait_send()
        return carry

    lax.fori_loop(0, comp, drain, 0)
    for cp in halo_copies + [near_st, near_ad]:
        cp.wait_send()


def local(state, adjoint, plan, valve):
    n_tm = lax.axis_size("tm")
    inst, comp, beds, nz, nr = state.shape
    block = jax.ShapeDtypeStruct(state.shape, jnp.float32)
    vmem = pl.BlockSpec(memory_space=pltpu.VMEM)
    halo_shape = (inst, comp, beds, 8, nr)

    def kern(*refs):
        _kernel(n_tm, *refs)

    both = pl.pallas_call(
        kern,
        out_shape=pltpu.VMEM((2,) + state.shape, jnp.float32),
        in_specs=[pl.BlockSpec(memory_space=pltpu.SMEM)] * 2 + [pl.BlockSpec(memory_space=pl.ANY)] * 2,
        out_specs=vmem,
        scratch_shapes=[pltpu.VMEM(state.shape, jnp.float32)] * 2
        + [pltpu.VMEM((2,) + state.shape, jnp.float32)] * 2
        + [pltpu.VMEM(halo_shape, jnp.float32)] * 2
        + [pltpu.SemaphoreType.DMA((6 + 2 * comp,)), pltpu.SemaphoreType.DMA((6 + 2 * comp,))]
        + [pltpu.SemaphoreType.DMA((2,))],
        compiler_params=pltpu.CompilerParams(collective_id=0, has_side_effects=True),
    )(plan, valve, state, adjoint)
    return both[0], both[1]


def solution(mesh):
    return jax.shard_map(
        local,
        mesh=mesh,
        in_specs=(
            P("tm", None, None, "sec", None),
            P("tm", None, None, "sec", None),
            P("tm", None),
            P("tm", None),
        ),
        out_specs=(P("tm", None, None, "sec", None), P("tm", None, None, "sec", None)),
        check_vma=False,
    )
```

```python
import jax
import jax.numpy as jnp
from jax import lax
from jax.experimental import pallas as pl
from jax.experimental.pallas import tpu as pltpu
from jax.sharding import PartitionSpec as P

STENCIL = (0.8, -0.2, 4.0 / 105.0, -1.0 / 280.0)
TIME_SCALE = 4.0
FLOW_VELOCITY = 1.0
AXIAL_DISPERSION = 0.3
RADIAL_SPREADING = 0.2
BINDING_STRENGTH = (1.5, 0.6)
HEAT_EXPONENT = (0.5, 0.3)
KINETIC = (1.2, 0.7)
CAPACITY = (2.0, 1.0)
SORPTION_HEAT = (0.4, 0.25)
PURGE_GAIN = 1.5

MESH = pl.DeviceIdType.MESH


def _kernel(n_tm, plan, valve, st_hbm, ad_hbm, both, st, ad, rv_st, rv_ad, h_st, h_ad, send, recv, lsem):
    inst, comp, beds, nz, nr = st.shape
    res = both.at[0]
    adj = both.at[1]
    me = lax.axis_index("tm")
    sec = lax.axis_index("sec")
    core = lax.rem(me, 2)
    pair = (me + 1 - 2 * core, sec)
    cross = (lax.rem(me + 2 * core - 1 + n_tm, n_tm), sec)
    partner = (me, 1 - sec)

    loads = [
        pltpu.make_async_copy(st_hbm, st, lsem.at[0]),
        pltpu.make_async_copy(ad_hbm, ad, lsem.at[1]),
    ]
    for cp in loads:
        cp.start()

    barrier = pltpu.get_barrier_semaphore()
    for dev in (pair, cross, partner):
        pl.semaphore_signal(barrier, inc=1, device_id=dev, device_id_type=MESH)
    pl.semaphore_wait(barrier, 3)

    def rcopy(src, dst, i, dev):
        cp = pltpu.make_async_remote_copy(
            src_ref=src, dst_ref=dst, send_sem=send.at[i], recv_sem=recv.at[i],
            device_id=dev, device_id_type=MESH,
        )
        cp.start()
        return cp

    row_src = (nz - 1) * (1 - sec)
    halo_copies = [
        rcopy(src.at[:, :, :, pl.ds(row_src, 1), :], dst.at[:, :, :, pl.ds(0, 1), :], 4 + i, partner)
        for i, (src, dst) in enumerate(((st_hbm, h_st), (ad_hbm, h_ad)))
    ]
    def desc(src, dst, i, dev):
        return pltpu.make_async_remote_copy(
            src_ref=src, dst_ref=dst, send_sem=send.at[i], recv_sem=recv.at[i],
            device_id=dev, device_id_type=MESH,
        )

    def far_descs(c):
        return (
            desc(st_hbm.at[:, c], rv_st.at[1 - core, :, c], 6 + c, cross),
            desc(ad_hbm.at[:, c], rv_ad.at[1 - core, :, c], 6 + comp + c, cross),
        )

    for i in range(2):
        for c in range(comp):
            far_descs(c)[i].start()
    near_st = rcopy(st_hbm, rv_st.at[core], 2, pair)
    near_ad = rcopy(ad_hbm, rv_ad.at[core], 3, pair)
    for cp in loads:
        cp.wait()

    for cp in halo_copies:
        cp.wait_recv()

    sec_f = sec.astype(jnp.float32)
    row = lax.broadcasted_iota(jnp.int32, (nz, nr), 0)
    lane = lax.broadcasted_iota(jnp.int32, (nz, nr), 1)
    first_row = row == 0
    last_row = row == nz - 1
    first_lane = lane == 0
    last_lane = lane == nr - 1

    def radial(x):
        lower = jnp.where(first_lane, 0.0, pltpu.roll(x, 1, 1))
        upper = jnp.where(last_lane, 0.0, pltpu.roll(x, nr - 1, 1))
        return upper - 2.0 * x + lower

    def axial(x, below, above):
        zm = jnp.where(first_row, below, pltpu.roll(x, 1, 0))
        zp = jnp.where(last_row, above, pltpu.roll(x, nz - 1, 0))
        return zm, zp

    def transport(x, below, above):
        zm, zp = axial(x, below, above)
        out = FLOW_VELOCITY * (x - zm) - AXIAL_DISPERSION * (zp - 2.0 * x + zm)
        return out - RADIAL_SPREADING * radial(x)

    def transport_t(lam, below, above):
        lm, lp = axial(lam, below, above)
        out = FLOW_VELOCITY * (lam - lp) - AXIAL_DISPERSION * (lm - 2.0 * lam + lp)
        return out - RADIAL_SPREADING * radial(lam)

    def spatial_body(t, carry):
        for b in range(beds):
            x = [st[t, c, b] for c in range(comp)]
            lam = [ad[t, c, b] for c in range(comp)]
            hs = [h_st[t, c, b, 0:1, :] for c in range(comp)]
            ha = [h_ad[t, c, b, 0:1, :] for c in range(comp)]
            y1, y2, y3, q1, q2, temp = x
            b1 = BINDING_STRENGTH[0] * jnp.exp(HEAT_EXPONENT[0] * temp)
            b2 = BINDING_STRENGTH[1] * jnp.exp(HEAT_EXPONENT[1] * temp)
            den = 1.0 + b1 * y1 + b2 * y2
            p1 = b1 * y1 / den
            p2 = b2 * y2 / den
            rate1 = KINETIC[0] * (CAPACITY[0] * p1 - q1)
            rate2 = KINETIC[1] * (CAPACITY[1] * p2 - q2)
            tr = {}
            trt = {}
            for c in (0, 1, 2, 5):
                below = hs[c] * sec_f
                above = hs[c] * (1.0 - sec_f)
                tr[c] = transport(x[c], below, above)
                lbelow = ha[c] * sec_f
                labove = ha[c] * (1.0 - sec_f)
                trt[c] = transport_t(lam[c], lbelow, labove)
            res[t, 0, b] = tr[0] + rate1
            res[t, 1, b] = tr[1] + rate2
            res[t, 2, b] = tr[2]
            res[t, 3, b] = -rate1
            res[t, 4, b] = -rate2
            res[t, 5, b] = tr[5] - (SORPTION_HEAT[0] * rate1 + SORPTION_HEAT[1] * rate2)
            mu1 = lam[0] - lam[3] - SORPTION_HEAT[0] * lam[5]
            mu2 = lam[1] - lam[4] - SORPTION_HEAT[1] * lam[5]
            n1 = (KINETIC[0] * CAPACITY[0]) * mu1
            n2 = (KINETIC[1] * CAPACITY[1]) * mu2
            cden = -(n1 * p1 + n2 * p2) / den
            cu1 = n1 / den + cden
            cu2 = n2 / den + cden
            adj[t, 0, b] = trt[0] + b1 * cu1
            adj[t, 1, b] = trt[1] + b2 * cu2
            adj[t, 2, b] = trt[2]
            adj[t, 3, b] = -KINETIC[0] * mu1
            adj[t, 4, b] = -KINETIC[1] * mu2
            adj[t, 5, b] = trt[5] + (HEAT_EXPONENT[0] * y1 * b1 * cu1 + HEAT_EXPONENT[1] * y2 * b2 * cu2)
        return carry

    lax.fori_loop(0, inst, spatial_body, 0)

    @pl.when(sec == 1)
    def _():
        def purge_body(t, carry):
            srcs = [lax.rem(b + plan[t, b], beds) for b in range(beds)]
            opens = [jnp.full((1, nr), valve[t, b], jnp.int32) != 0 for b in range(beds)]
            for c in range(3):
                ys = [st[t, c, b, nz - 1 : nz, :] for b in range(beds)]
                ls = [ad[t, c, b, nz - 1 : nz, :] for b in range(beds)]
                for b in range(beds):
                    inc = jnp.zeros((1, nr), jnp.float32)
                    for bp in range(beds):
                        inc = inc + jnp.where(srcs[b] == bp, ys[bp], 0.0)
                    term = jnp.where(opens[b], PURGE_GAIN * (ys[b] - inc), 0.0)
                    res[t, c, b, nz - 1 : nz, :] = res[t, c, b, nz - 1 : nz, :] + term
                    back = jnp.where(opens[b], PURGE_GAIN * ls[b], 0.0)
                    for bb in range(beds):
                        hit = jnp.logical_and(opens[bb], srcs[bb] == b)
                        back = back - jnp.where(hit, PURGE_GAIN * ls[bb], 0.0)
                    adj[t, c, b, nz - 1 : nz, :] = adj[t, c, b, nz - 1 : nz, :] + back
            return carry

        lax.fori_loop(0, inst, purge_body, 0)

    def time_pass(cross_right, use_far, comp_index=None, arrays=(0, 1)):
        srcs = ((st, rv_st, res, 1.0), (ad, rv_ad, adj, -1.0))

        def body(c, carry):
            for which in arrays:
                own, recvd, out, scale = srcs[which]
                for t in range(inst):
                    acc = None
                    for k, w in enumerate(STENCIL):
                        s = k + 1
                        d = None
                        for j, sign in ((t + s, 1.0), (t - s, -1.0)):
                            if j >= inst:
                                far = cross_right
                            elif j < 0:
                                far = not cross_right
                            else:
                                far = False
                            if far != use_far:
                                continue
                            if j >= inst:
                                x = recvd[1, j - inst, c]
                            elif j < 0:
                                x = recvd[0, j + inst, c]
                            else:
                                x = own[j, c]
                            if sign < 0:
                                x = -x
                            d = x if d is None else d + x
                        if d is None:
                            continue
                        acc = w * d if acc is None else acc + w * d
                    if acc is None:
                        continue
                    if scale > 0:
                        out[t, c] = TIME_SCALE * acc + out[t, c]
                    else:
                        out[t, c] = out[t, c] - TIME_SCALE * acc
            return carry

        if comp_index is None:
            lax.fori_loop(0, comp, body, 0)
        else:
            body(comp_index, 0)

    near_st.wait_recv()
    near_ad.wait_recv()

    @pl.when(core == 0)
    def _():
        time_pass(False, False)

    @pl.when(core == 1)
    def _():
        time_pass(True, False)

    for i in range(2):
        def far_body(c, carry, i=i):
            far_descs(c)[i].wait_recv()

            @pl.when(core == 0)
            def _():
                time_pass(False, True, c, (i,))

            @pl.when(core == 1)
            def _():
                time_pass(True, True, c, (i,))

            return carry

        lax.fori_loop(0, comp, far_body, 0)

    def drain(c, carry):
        for cp in far_descs(c):
            cp.wait_send()
        return carry

    lax.fori_loop(0, comp, drain, 0)
    for cp in halo_copies + [near_st, near_ad]:
        cp.wait_send()


def local(state, adjoint, plan, valve):
    n_tm = lax.axis_size("tm")
    inst, comp, beds, nz, nr = state.shape
    block = jax.ShapeDtypeStruct(state.shape, jnp.float32)
    vmem = pl.BlockSpec(memory_space=pltpu.VMEM)
    halo_shape = (inst, comp, beds, 8, nr)

    def kern(*refs):
        _kernel(n_tm, *refs)

    both = pl.pallas_call(
        kern,
        out_shape=pltpu.VMEM((2,) + state.shape, jnp.float32),
        in_specs=[pl.BlockSpec(memory_space=pltpu.SMEM)] * 2 + [pl.BlockSpec(memory_space=pl.ANY)] * 2,
        out_specs=vmem,
        scratch_shapes=[pltpu.VMEM(state.shape, jnp.float32)] * 2
        + [pltpu.VMEM((2,) + state.shape, jnp.float32)] * 2
        + [pltpu.VMEM(halo_shape, jnp.float32)] * 2
        + [pltpu.SemaphoreType.DMA((6 + 2 * comp,)), pltpu.SemaphoreType.DMA((6 + 2 * comp,))]
        + [pltpu.SemaphoreType.DMA((2,))],
        compiler_params=pltpu.CompilerParams(collective_id=0, has_side_effects=True),
    )(plan, valve, state, adjoint)
    return both[0], both[1]


def solution(mesh):
    return jax.shard_map(
        local,
        mesh=mesh,
        in_specs=(
            P("tm", None, None, "sec", None),
            P("tm", None, None, "sec", None),
            P("tm", None),
            P("tm", None),
        ),
        out_specs=(P("tm", None, None, "sec", None), P("tm", None, None, "sec", None)),
        check_vma=False,
    )
```

```python
import jax
import jax.numpy as jnp
from jax import lax
from jax.experimental import pallas as pl
from jax.experimental.pallas import tpu as pltpu
from jax.sharding import PartitionSpec as P

STENCIL = (0.8, -0.2, 4.0 / 105.0, -1.0 / 280.0)
TIME_SCALE = 4.0
FLOW_VELOCITY = 1.0
AXIAL_DISPERSION = 0.3
RADIAL_SPREADING = 0.2
BINDING_STRENGTH = (1.5, 0.6)
HEAT_EXPONENT = (0.5, 0.3)
KINETIC = (1.2, 0.7)
CAPACITY = (2.0, 1.0)
SORPTION_HEAT = (0.4, 0.25)
PURGE_GAIN = 1.5

MESH = pl.DeviceIdType.MESH


def _kernel(n_tm, plan, valve, st_hbm, ad_hbm, both, st, ad, rv_st, rv_ad, h_st, h_ad, send, recv, lsem):
    inst, comp, beds, nz, nr = st.shape
    res = both.at[0]
    adj = both.at[1]
    me = lax.axis_index("tm")
    sec = lax.axis_index("sec")
    core = lax.rem(me, 2)
    pair = (me + 1 - 2 * core, sec)
    cross = (lax.rem(me + 2 * core - 1 + n_tm, n_tm), sec)
    partner = (me, 1 - sec)

    loads = [
        pltpu.make_async_copy(st_hbm, st, lsem.at[0]),
        pltpu.make_async_copy(ad_hbm, ad, lsem.at[1]),
    ]
    for cp in loads:
        cp.start()

    barrier = pltpu.get_barrier_semaphore()
    for dev in (pair, cross, partner):
        pl.semaphore_signal(barrier, inc=1, device_id=dev, device_id_type=MESH)
    pl.semaphore_wait(barrier, 3)

    def rcopy(src, dst, i, dev):
        cp = pltpu.make_async_remote_copy(
            src_ref=src, dst_ref=dst, send_sem=send.at[i], recv_sem=recv.at[i],
            device_id=dev, device_id_type=MESH,
        )
        cp.start()
        return cp

    row_src = (nz - 1) * (1 - sec)
    halo_copies = [
        rcopy(src.at[:, :, :, pl.ds(row_src, 1), :], dst.at[:, :, :, pl.ds(0, 1), :], 4 + i, partner)
        for i, (src, dst) in enumerate(((st_hbm, h_st), (ad_hbm, h_ad)))
    ]
    def desc(src, dst, i, dev):
        return pltpu.make_async_remote_copy(
            src_ref=src, dst_ref=dst, send_sem=send.at[i], recv_sem=recv.at[i],
            device_id=dev, device_id_type=MESH,
        )

    def far_descs(c):
        return (
            desc(st_hbm.at[:, c], rv_st.at[1 - core, :, c], 6 + c, cross),
            desc(ad_hbm.at[:, c], rv_ad.at[1 - core, :, c], 6 + comp + c, cross),
        )

    for i in range(2):
        for c in range(comp):
            far_descs(c)[i].start()
    near_st = rcopy(st_hbm, rv_st.at[core], 2, pair)
    near_ad = rcopy(ad_hbm, rv_ad.at[core], 3, pair)
    for cp in loads:
        cp.wait()

    for cp in halo_copies:
        cp.wait_recv()

    sec_f = sec.astype(jnp.float32)
    row = lax.broadcasted_iota(jnp.int32, (nz, nr), 0)
    lane = lax.broadcasted_iota(jnp.int32, (nz, nr), 1)
    first_row = row == 0
    last_row = row == nz - 1
    first_lane = lane == 0
    last_lane = lane == nr - 1

    def radial(x):
        lower = jnp.where(first_lane, 0.0, pltpu.roll(x, 1, 1))
        upper = jnp.where(last_lane, 0.0, pltpu.roll(x, nr - 1, 1))
        return upper - 2.0 * x + lower

    def axial(x, below, above):
        zm = jnp.where(first_row, below, pltpu.roll(x, 1, 0))
        zp = jnp.where(last_row, above, pltpu.roll(x, nz - 1, 0))
        return zm, zp

    def transport(x, below, above):
        zm, zp = axial(x, below, above)
        out = FLOW_VELOCITY * (x - zm) - AXIAL_DISPERSION * (zp - 2.0 * x + zm)
        return out - RADIAL_SPREADING * radial(x)

    def transport_t(lam, below, above):
        lm, lp = axial(lam, below, above)
        out = FLOW_VELOCITY * (lam - lp) - AXIAL_DISPERSION * (lm - 2.0 * lam + lp)
        return out - RADIAL_SPREADING * radial(lam)

    def spatial_body(t, carry):
        for b in range(beds):
            x = [st[t, c, b] for c in range(comp)]
            lam = [ad[t, c, b] for c in range(comp)]
            hs = [h_st[t, c, b, 0:1, :] for c in range(comp)]
            ha = [h_ad[t, c, b, 0:1, :] for c in range(comp)]
            y1, y2, y3, q1, q2, temp = x
            b1 = BINDING_STRENGTH[0] * jnp.exp(HEAT_EXPONENT[0] * temp)
            b2 = BINDING_STRENGTH[1] * jnp.exp(HEAT_EXPONENT[1] * temp)
            den = 1.0 + b1 * y1 + b2 * y2
            p1 = b1 * y1 / den
            p2 = b2 * y2 / den
            rate1 = KINETIC[0] * (CAPACITY[0] * p1 - q1)
            rate2 = KINETIC[1] * (CAPACITY[1] * p2 - q2)
            tr = {}
            trt = {}
            for c in (0, 1, 2, 5):
                below = hs[c] * sec_f
                above = hs[c] * (1.0 - sec_f)
                tr[c] = transport(x[c], below, above)
                lbelow = ha[c] * sec_f
                labove = ha[c] * (1.0 - sec_f)
                trt[c] = transport_t(lam[c], lbelow, labove)
            res[t, 0, b] = tr[0] + rate1
            res[t, 1, b] = tr[1] + rate2
            res[t, 2, b] = tr[2]
            res[t, 3, b] = -rate1
            res[t, 4, b] = -rate2
            res[t, 5, b] = tr[5] - (SORPTION_HEAT[0] * rate1 + SORPTION_HEAT[1] * rate2)
            mu1 = lam[0] - lam[3] - SORPTION_HEAT[0] * lam[5]
            mu2 = lam[1] - lam[4] - SORPTION_HEAT[1] * lam[5]
            n1 = (KINETIC[0] * CAPACITY[0]) * mu1
            n2 = (KINETIC[1] * CAPACITY[1]) * mu2
            cden = -(n1 * p1 + n2 * p2) / den
            cu1 = n1 / den + cden
            cu2 = n2 / den + cden
            adj[t, 0, b] = trt[0] + b1 * cu1
            adj[t, 1, b] = trt[1] + b2 * cu2
            adj[t, 2, b] = trt[2]
            adj[t, 3, b] = -KINETIC[0] * mu1
            adj[t, 4, b] = -KINETIC[1] * mu2
            adj[t, 5, b] = trt[5] + (HEAT_EXPONENT[0] * y1 * b1 * cu1 + HEAT_EXPONENT[1] * y2 * b2 * cu2)
        return carry

    lax.fori_loop(0, inst, spatial_body, 0)

    @pl.when(sec == 1)
    def _():
        def purge_body(t, carry):
            srcs = [lax.rem(b + plan[t, b], beds) for b in range(beds)]
            opens = [jnp.full((1, nr), valve[t, b], jnp.int32) != 0 for b in range(beds)]
            for c in range(3):
                ys = [st[t, c, b, nz - 1 : nz, :] for b in range(beds)]
                ls = [ad[t, c, b, nz - 1 : nz, :] for b in range(beds)]
                for b in range(beds):
                    inc = jnp.zeros((1, nr), jnp.float32)
                    for bp in range(beds):
                        inc = inc + jnp.where(srcs[b] == bp, ys[bp], 0.0)
                    term = jnp.where(opens[b], PURGE_GAIN * (ys[b] - inc), 0.0)
                    res[t, c, b, nz - 1 : nz, :] = res[t, c, b, nz - 1 : nz, :] + term
                    back = jnp.where(opens[b], PURGE_GAIN * ls[b], 0.0)
                    for bb in range(beds):
                        hit = jnp.logical_and(opens[bb], srcs[bb] == b)
                        back = back - jnp.where(hit, PURGE_GAIN * ls[bb], 0.0)
                    adj[t, c, b, nz - 1 : nz, :] = adj[t, c, b, nz - 1 : nz, :] + back
            return carry

        lax.fori_loop(0, inst, purge_body, 0)

    def time_pass(cross_right, use_far, comp_index=None, arrays=(0, 1)):
        srcs = ((st, rv_st, res, 1.0), (ad, rv_ad, adj, -1.0))

        def body(c, carry):
            for which in arrays:
                own, recvd, out, scale = srcs[which]
                for t in range(inst):
                    acc = None
                    for k, w in enumerate(STENCIL):
                        s = k + 1
                        d = None
                        for j, sign in ((t + s, 1.0), (t - s, -1.0)):
                            if j >= inst:
                                far = cross_right
                            elif j < 0:
                                far = not cross_right
                            else:
                                far = False
                            if far != use_far:
                                continue
                            if j >= inst:
                                x = recvd[1, j - inst, c]
                            elif j < 0:
                                x = recvd[0, j + inst, c]
                            else:
                                x = own[j, c]
                            if sign < 0:
                                x = -x
                            d = x if d is None else d + x
                        if d is None:
                            continue
                        acc = w * d if acc is None else acc + w * d
                    if acc is None:
                        continue
                    if scale > 0:
                        out[t, c] = TIME_SCALE * acc + out[t, c]
                    else:
                        out[t, c] = out[t, c] - TIME_SCALE * acc
            return carry

        if comp_index is None:
            lax.fori_loop(0, comp, body, 0)
        else:
            body(comp_index, 0)

    near_st.wait_recv()
    near_ad.wait_recv()

    @pl.when(core == 0)
    def _():
        time_pass(False, False)

    @pl.when(core == 1)
    def _():
        time_pass(True, False)

    for i in range(2):
        def far_body(c, carry, i=i):
            far_descs(c)[i].wait_recv()

            @pl.when(core == 0)
            def _():
                time_pass(False, True, c, (i,))

            @pl.when(core == 1)
            def _():
                time_pass(True, True, c, (i,))

            return carry

        lax.fori_loop(0, comp, far_body, 0)

    def drain(c, carry):
        for cp in far_descs(c):
            cp.wait_send()
        return carry

    lax.fori_loop(0, comp, drain, 0)
    for cp in halo_copies + [near_st, near_ad]:
        cp.wait_send()


def _store(both, res_out, adj_out, sem):
    copies = [
        pltpu.make_async_copy(both.at[0], res_out, sem.at[0]),
        pltpu.make_async_copy(both.at[1], adj_out, sem.at[1]),
    ]
    for cp in copies:
        cp.start()
    for cp in copies:
        cp.wait()


def local(state, adjoint, plan, valve):
    n_tm = lax.axis_size("tm")
    inst, comp, beds, nz, nr = state.shape
    block = jax.ShapeDtypeStruct(state.shape, jnp.float32)
    vmem = pl.BlockSpec(memory_space=pltpu.VMEM)
    halo_shape = (inst, comp, beds, 8, nr)

    def kern(*refs):
        _kernel(n_tm, *refs)

    both = pl.pallas_call(
        kern,
        out_shape=pltpu.VMEM((2,) + state.shape, jnp.float32),
        in_specs=[pl.BlockSpec(memory_space=pltpu.SMEM)] * 2 + [pl.BlockSpec(memory_space=pl.ANY)] * 2,
        out_specs=vmem,
        scratch_shapes=[pltpu.VMEM(state.shape, jnp.float32)] * 2
        + [pltpu.VMEM((2,) + state.shape, jnp.float32)] * 2
        + [pltpu.VMEM(halo_shape, jnp.float32)] * 2
        + [pltpu.SemaphoreType.DMA((6 + 2 * comp,)), pltpu.SemaphoreType.DMA((6 + 2 * comp,))]
        + [pltpu.SemaphoreType.DMA((2,))],
        compiler_params=pltpu.CompilerParams(collective_id=0, has_side_effects=True),
    )(plan, valve, state, adjoint)
    hbm = pl.BlockSpec(memory_space=pl.ANY)
    return pl.pallas_call(
        _store,
        out_shape=(block, block),
        in_specs=[vmem],
        out_specs=(hbm, hbm),
        scratch_shapes=[pltpu.SemaphoreType.DMA((2,))],
    )(pltpu.with_memory_space_constraint(both, pltpu.VMEM))


def solution(mesh):
    return jax.shard_map(
        local,
        mesh=mesh,
        in_specs=(
            P("tm", None, None, "sec", None),
            P("tm", None, None, "sec", None),
            P("tm", None),
            P("tm", None),
        ),
        out_specs=(P("tm", None, None, "sec", None), P("tm", None, None, "sec", None)),
        check_vma=False,
    )
```

```python
import jax
import jax.numpy as jnp
from jax import lax
from jax.experimental import pallas as pl
from jax.experimental.pallas import tpu as pltpu
from jax.sharding import PartitionSpec as P

STENCIL = (0.8, -0.2, 4.0 / 105.0, -1.0 / 280.0)
TIME_SCALE = 4.0
FLOW_VELOCITY = 1.0
AXIAL_DISPERSION = 0.3
RADIAL_SPREADING = 0.2
BINDING_STRENGTH = (1.5, 0.6)
HEAT_EXPONENT = (0.5, 0.3)
KINETIC = (1.2, 0.7)
CAPACITY = (2.0, 1.0)
SORPTION_HEAT = (0.4, 0.25)
PURGE_GAIN = 1.5

MESH = pl.DeviceIdType.MESH


def _kernel(n_tm, plan, valve, st_hbm, ad_hbm, both, st, ad, rv_st, rv_ad, h_st, h_ad, send, recv, lsem):
    inst, comp, beds, nz, nr = st.shape
    res = both.at[0]
    adj = both.at[1]
    me = lax.axis_index("tm")
    sec = lax.axis_index("sec")
    core = lax.rem(me, 2)
    pair = (me + 1 - 2 * core, sec)
    cross = (lax.rem(me + 2 * core - 1 + n_tm, n_tm), sec)
    partner = (me, 1 - sec)

    loads = [
        pltpu.make_async_copy(st_hbm, st, lsem.at[0]),
        pltpu.make_async_copy(ad_hbm, ad, lsem.at[1]),
    ]
    for cp in loads:
        cp.start()

    barrier = pltpu.get_barrier_semaphore()
    for dev in (pair, cross, partner):
        pl.semaphore_signal(barrier, inc=1, device_id=dev, device_id_type=MESH)
    pl.semaphore_wait(barrier, 3)

    def rcopy(src, dst, i, dev):
        cp = pltpu.make_async_remote_copy(
            src_ref=src, dst_ref=dst, send_sem=send.at[i], recv_sem=recv.at[i],
            device_id=dev, device_id_type=MESH,
        )
        cp.start()
        return cp

    row_src = (nz - 1) * (1 - sec)
    halo_copies = [
        rcopy(src.at[:, :, :, pl.ds(row_src, 1), :], dst.at[:, :, :, pl.ds(0, 1), :], 4 + i, partner)
        for i, (src, dst) in enumerate(((st_hbm, h_st), (ad_hbm, h_ad)))
    ]
    def desc(src, dst, i, dev):
        return pltpu.make_async_remote_copy(
            src_ref=src, dst_ref=dst, send_sem=send.at[i], recv_sem=recv.at[i],
            device_id=dev, device_id_type=MESH,
        )

    def far_descs(c):
        return (
            desc(st_hbm.at[:, c], rv_st.at[1 - core, :, c], 6 + c, cross),
            desc(ad_hbm.at[:, c], rv_ad.at[1 - core, :, c], 6 + comp + c, cross),
        )

    for i in range(2):
        for c in range(comp):
            far_descs(c)[i].start()
    near_st = rcopy(st_hbm, rv_st.at[core], 2, pair)
    near_ad = rcopy(ad_hbm, rv_ad.at[core], 3, pair)
    for cp in loads:
        cp.wait()

    for cp in halo_copies:
        cp.wait_recv()

    sec_f = sec.astype(jnp.float32)
    row = lax.broadcasted_iota(jnp.int32, (nz, nr), 0)
    lane = lax.broadcasted_iota(jnp.int32, (nz, nr), 1)
    first_row = row == 0
    last_row = row == nz - 1
    first_lane = lane == 0
    last_lane = lane == nr - 1

    def radial(x):
        lower = jnp.where(first_lane, 0.0, pltpu.roll(x, 1, 1))
        upper = jnp.where(last_lane, 0.0, pltpu.roll(x, nr - 1, 1))
        return upper - 2.0 * x + lower

    def axial(x, below, above):
        zm = jnp.where(first_row, below, pltpu.roll(x, 1, 0))
        zp = jnp.where(last_row, above, pltpu.roll(x, nz - 1, 0))
        return zm, zp

    def transport(x, below, above):
        zm, zp = axial(x, below, above)
        out = FLOW_VELOCITY * (x - zm) - AXIAL_DISPERSION * (zp - 2.0 * x + zm)
        return out - RADIAL_SPREADING * radial(x)

    def transport_t(lam, below, above):
        lm, lp = axial(lam, below, above)
        out = FLOW_VELOCITY * (lam - lp) - AXIAL_DISPERSION * (lm - 2.0 * lam + lp)
        return out - RADIAL_SPREADING * radial(lam)

    def spatial_body(t, carry):
        for b in range(beds):
            x = [st[t, c, b] for c in range(comp)]
            lam = [ad[t, c, b] for c in range(comp)]
            hs = [h_st[t, c, b, 0:1, :] for c in range(comp)]
            ha = [h_ad[t, c, b, 0:1, :] for c in range(comp)]
            y1, y2, y3, q1, q2, temp = x
            b1 = BINDING_STRENGTH[0] * jnp.exp(HEAT_EXPONENT[0] * temp)
            b2 = BINDING_STRENGTH[1] * jnp.exp(HEAT_EXPONENT[1] * temp)
            den = 1.0 + b1 * y1 + b2 * y2
            p1 = b1 * y1 / den
            p2 = b2 * y2 / den
            rate1 = KINETIC[0] * (CAPACITY[0] * p1 - q1)
            rate2 = KINETIC[1] * (CAPACITY[1] * p2 - q2)
            tr = {}
            trt = {}
            for c in (0, 1, 2, 5):
                below = hs[c] * sec_f
                above = hs[c] * (1.0 - sec_f)
                tr[c] = transport(x[c], below, above)
                lbelow = ha[c] * sec_f
                labove = ha[c] * (1.0 - sec_f)
                trt[c] = transport_t(lam[c], lbelow, labove)
            res[t, 0, b] = tr[0] + rate1
            res[t, 1, b] = tr[1] + rate2
            res[t, 2, b] = tr[2]
            res[t, 3, b] = -rate1
            res[t, 4, b] = -rate2
            res[t, 5, b] = tr[5] - (SORPTION_HEAT[0] * rate1 + SORPTION_HEAT[1] * rate2)
            mu1 = lam[0] - lam[3] - SORPTION_HEAT[0] * lam[5]
            mu2 = lam[1] - lam[4] - SORPTION_HEAT[1] * lam[5]
            n1 = (KINETIC[0] * CAPACITY[0]) * mu1
            n2 = (KINETIC[1] * CAPACITY[1]) * mu2
            cden = -(n1 * p1 + n2 * p2) / den
            cu1 = n1 / den + cden
            cu2 = n2 / den + cden
            adj[t, 0, b] = trt[0] + b1 * cu1
            adj[t, 1, b] = trt[1] + b2 * cu2
            adj[t, 2, b] = trt[2]
            adj[t, 3, b] = -KINETIC[0] * mu1
            adj[t, 4, b] = -KINETIC[1] * mu2
            adj[t, 5, b] = trt[5] + (HEAT_EXPONENT[0] * y1 * b1 * cu1 + HEAT_EXPONENT[1] * y2 * b2 * cu2)
        return carry

    lax.fori_loop(0, inst, spatial_body, 0)

    @pl.when(sec == 1)
    def _():
        def purge_body(t, carry):
            srcs = [lax.rem(b + plan[t, b], beds) for b in range(beds)]
            opens = [jnp.full((1, nr), valve[t, b], jnp.int32) != 0 for b in range(beds)]
            for c in range(3):
                ys = [st[t, c, b, nz - 1 : nz, :] for b in range(beds)]
                ls = [ad[t, c, b, nz - 1 : nz, :] for b in range(beds)]
                for b in range(beds):
                    inc = jnp.zeros((1, nr), jnp.float32)
                    for bp in range(beds):
                        inc = inc + jnp.where(srcs[b] == bp, ys[bp], 0.0)
                    term = jnp.where(opens[b], PURGE_GAIN * (ys[b] - inc), 0.0)
                    res[t, c, b, nz - 1 : nz, :] = res[t, c, b, nz - 1 : nz, :] + term
                    back = jnp.where(opens[b], PURGE_GAIN * ls[b], 0.0)
                    for bb in range(beds):
                        hit = jnp.logical_and(opens[bb], srcs[bb] == b)
                        back = back - jnp.where(hit, PURGE_GAIN * ls[bb], 0.0)
                    adj[t, c, b, nz - 1 : nz, :] = adj[t, c, b, nz - 1 : nz, :] + back
            return carry

        lax.fori_loop(0, inst, purge_body, 0)

    def time_pass(cross_right, use_far, comp_index=None, arrays=(0, 1)):
        srcs = ((st, rv_st, res, 1.0), (ad, rv_ad, adj, -1.0))

        def body(c, carry):
            for which in arrays:
                own, recvd, out, scale = srcs[which]
                for t in range(inst):
                    acc = None
                    for k, w in enumerate(STENCIL):
                        s = k + 1
                        d = None
                        for j, sign in ((t + s, 1.0), (t - s, -1.0)):
                            if j >= inst:
                                far = cross_right
                            elif j < 0:
                                far = not cross_right
                            else:
                                far = False
                            if far != use_far:
                                continue
                            if j >= inst:
                                x = recvd[1, j - inst, c]
                            elif j < 0:
                                x = recvd[0, j + inst, c]
                            else:
                                x = own[j, c]
                            if sign < 0:
                                x = -x
                            d = x if d is None else d + x
                        if d is None:
                            continue
                        acc = w * d if acc is None else acc + w * d
                    if acc is None:
                        continue
                    if scale > 0:
                        out[t, c] = TIME_SCALE * acc + out[t, c]
                    else:
                        out[t, c] = out[t, c] - TIME_SCALE * acc
            return carry

        if comp_index is None:
            lax.fori_loop(0, comp, body, 0)
        else:
            body(comp_index, 0)

    near_st.wait_recv()
    near_ad.wait_recv()

    @pl.when(core == 0)
    def _():
        time_pass(False, False)

    @pl.when(core == 1)
    def _():
        time_pass(True, False)

    for i in range(2):
        def far_body(c, carry, i=i):
            far_descs(c)[i].wait_recv()

            @pl.when(core == 0)
            def _():
                time_pass(False, True, c, (i,))

            @pl.when(core == 1)
            def _():
                time_pass(True, True, c, (i,))

            return carry

        lax.fori_loop(0, comp, far_body, 0)

    def drain(c, carry):
        for cp in far_descs(c):
            cp.wait_send()
        return carry

    lax.fori_loop(0, comp, drain, 0)
    for cp in halo_copies + [near_st, near_ad]:
        cp.wait_send()


def _store(both, res_out, adj_out, sem):
    inst = res_out.shape[0]
    copies = [
        pltpu.make_async_copy(both.at[i, t], out.at[t], sem.at[i * inst + t])
        for i, out in enumerate((res_out, adj_out))
        for t in range(inst)
    ]
    for cp in copies:
        cp.start()
    for cp in copies:
        cp.wait()


def local(state, adjoint, plan, valve):
    n_tm = lax.axis_size("tm")
    inst, comp, beds, nz, nr = state.shape
    block = jax.ShapeDtypeStruct(state.shape, jnp.float32)
    vmem = pl.BlockSpec(memory_space=pltpu.VMEM)
    halo_shape = (inst, comp, beds, 8, nr)

    def kern(*refs):
        _kernel(n_tm, *refs)

    both = pl.pallas_call(
        kern,
        out_shape=pltpu.VMEM((2,) + state.shape, jnp.float32),
        in_specs=[pl.BlockSpec(memory_space=pltpu.SMEM)] * 2 + [pl.BlockSpec(memory_space=pl.ANY)] * 2,
        out_specs=vmem,
        scratch_shapes=[pltpu.VMEM(state.shape, jnp.float32)] * 2
        + [pltpu.VMEM((2,) + state.shape, jnp.float32)] * 2
        + [pltpu.VMEM(halo_shape, jnp.float32)] * 2
        + [pltpu.SemaphoreType.DMA((6 + 2 * comp,)), pltpu.SemaphoreType.DMA((6 + 2 * comp,))]
        + [pltpu.SemaphoreType.DMA((2,))],
        compiler_params=pltpu.CompilerParams(collective_id=0, has_side_effects=True),
    )(plan, valve, state, adjoint)
    hbm = pl.BlockSpec(memory_space=pl.ANY)
    return pl.pallas_call(
        _store,
        out_shape=(block, block),
        in_specs=[vmem],
        out_specs=(hbm, hbm),
        scratch_shapes=[pltpu.SemaphoreType.DMA((2 * inst,))],
    )(pltpu.with_memory_space_constraint(both, pltpu.VMEM))


def solution(mesh):
    return jax.shard_map(
        local,
        mesh=mesh,
        in_specs=(
            P("tm", None, None, "sec", None),
            P("tm", None, None, "sec", None),
            P("tm", None),
            P("tm", None),
        ),
        out_specs=(P("tm", None, None, "sec", None), P("tm", None, None, "sec", None)),
        check_vma=False,
    )
```

```python
import jax
import jax.numpy as jnp
from jax import lax
from jax.experimental import pallas as pl
from jax.experimental.pallas import tpu as pltpu
from jax.sharding import PartitionSpec as P

STENCIL = (0.8, -0.2, 4.0 / 105.0, -1.0 / 280.0)
TIME_SCALE = 4.0
FLOW_VELOCITY = 1.0
AXIAL_DISPERSION = 0.3
RADIAL_SPREADING = 0.2
BINDING_STRENGTH = (1.5, 0.6)
HEAT_EXPONENT = (0.5, 0.3)
KINETIC = (1.2, 0.7)
CAPACITY = (2.0, 1.0)
SORPTION_HEAT = (0.4, 0.25)
PURGE_GAIN = 1.5

MESH = pl.DeviceIdType.MESH


def _kernel(n_tm, plan, valve, st_hbm, ad_hbm, both, st, ad, rv_st, rv_ad, h_st, h_ad, send, recv, lsem):
    inst, comp, beds, nz, nr = st.shape
    res = both.at[0]
    adj = both.at[1]
    me = lax.axis_index("tm")
    sec = lax.axis_index("sec")
    core = lax.rem(me, 2)
    pair = (me + 1 - 2 * core, sec)
    cross = (lax.rem(me + 2 * core - 1 + n_tm, n_tm), sec)
    partner = (me, 1 - sec)

    barrier = pltpu.get_barrier_semaphore()
    for dev in (pair, cross, partner):
        pl.semaphore_signal(barrier, inc=1, device_id=dev, device_id_type=MESH)
    pl.semaphore_wait(barrier, 3)

    def rcopy(src, dst, i, dev):
        cp = pltpu.make_async_remote_copy(
            src_ref=src, dst_ref=dst, send_sem=send.at[i], recv_sem=recv.at[i],
            device_id=dev, device_id_type=MESH,
        )
        cp.start()
        return cp

    def desc(src, dst, i, dev):
        return pltpu.make_async_remote_copy(
            src_ref=src, dst_ref=dst, send_sem=send.at[i], recv_sem=recv.at[i],
            device_id=dev, device_id_type=MESH,
        )

    def far_descs(c):
        return (
            desc(st_hbm.at[:, c], rv_st.at[1 - core, :, c], 6 + c, cross),
            desc(ad_hbm.at[:, c], rv_ad.at[1 - core, :, c], 6 + comp + c, cross),
        )

    for i in range(2):
        for c in range(comp):
            far_descs(c)[i].start()
    row_src = (nz - 1) * (1 - sec)
    halo_copies = [
        rcopy(src.at[:, :, :, pl.ds(row_src, 1), :], dst.at[:, :, :, pl.ds(0, 1), :], 4 + i, partner)
        for i, (src, dst) in enumerate(((st_hbm, h_st), (ad_hbm, h_ad)))
    ]
    loads = [
        pltpu.make_async_copy(st_hbm, st, lsem.at[0]),
        pltpu.make_async_copy(ad_hbm, ad, lsem.at[1]),
    ]
    for cp in loads:
        cp.start()
    near_st = rcopy(st_hbm, rv_st.at[core], 2, pair)
    near_ad = rcopy(ad_hbm, rv_ad.at[core], 3, pair)
    for cp in loads:
        cp.wait()

    for cp in halo_copies:
        cp.wait_recv()

    sec_f = sec.astype(jnp.float32)
    row = lax.broadcasted_iota(jnp.int32, (nz, nr), 0)
    lane = lax.broadcasted_iota(jnp.int32, (nz, nr), 1)
    first_row = row == 0
    last_row = row == nz - 1
    first_lane = lane == 0
    last_lane = lane == nr - 1

    def radial(x):
        lower = jnp.where(first_lane, 0.0, pltpu.roll(x, 1, 1))
        upper = jnp.where(last_lane, 0.0, pltpu.roll(x, nr - 1, 1))
        return upper - 2.0 * x + lower

    def axial(x, below, above):
        zm = jnp.where(first_row, below, pltpu.roll(x, 1, 0))
        zp = jnp.where(last_row, above, pltpu.roll(x, nz - 1, 0))
        return zm, zp

    def transport(x, below, above):
        zm, zp = axial(x, below, above)
        out = FLOW_VELOCITY * (x - zm) - AXIAL_DISPERSION * (zp - 2.0 * x + zm)
        return out - RADIAL_SPREADING * radial(x)

    def transport_t(lam, below, above):
        lm, lp = axial(lam, below, above)
        out = FLOW_VELOCITY * (lam - lp) - AXIAL_DISPERSION * (lm - 2.0 * lam + lp)
        return out - RADIAL_SPREADING * radial(lam)

    def spatial_body(t, carry):
        for b in range(beds):
            x = [st[t, c, b] for c in range(comp)]
            lam = [ad[t, c, b] for c in range(comp)]
            hs = [h_st[t, c, b, 0:1, :] for c in range(comp)]
            ha = [h_ad[t, c, b, 0:1, :] for c in range(comp)]
            y1, y2, y3, q1, q2, temp = x
            b1 = BINDING_STRENGTH[0] * jnp.exp(HEAT_EXPONENT[0] * temp)
            b2 = BINDING_STRENGTH[1] * jnp.exp(HEAT_EXPONENT[1] * temp)
            den = 1.0 + b1 * y1 + b2 * y2
            p1 = b1 * y1 / den
            p2 = b2 * y2 / den
            rate1 = KINETIC[0] * (CAPACITY[0] * p1 - q1)
            rate2 = KINETIC[1] * (CAPACITY[1] * p2 - q2)
            tr = {}
            trt = {}
            for c in (0, 1, 2, 5):
                below = hs[c] * sec_f
                above = hs[c] * (1.0 - sec_f)
                tr[c] = transport(x[c], below, above)
                lbelow = ha[c] * sec_f
                labove = ha[c] * (1.0 - sec_f)
                trt[c] = transport_t(lam[c], lbelow, labove)
            res[t, 0, b] = tr[0] + rate1
            res[t, 1, b] = tr[1] + rate2
            res[t, 2, b] = tr[2]
            res[t, 3, b] = -rate1
            res[t, 4, b] = -rate2
            res[t, 5, b] = tr[5] - (SORPTION_HEAT[0] * rate1 + SORPTION_HEAT[1] * rate2)
            mu1 = lam[0] - lam[3] - SORPTION_HEAT[0] * lam[5]
            mu2 = lam[1] - lam[4] - SORPTION_HEAT[1] * lam[5]
            n1 = (KINETIC[0] * CAPACITY[0]) * mu1
            n2 = (KINETIC[1] * CAPACITY[1]) * mu2
            cden = -(n1 * p1 + n2 * p2) / den
            cu1 = n1 / den + cden
            cu2 = n2 / den + cden
            adj[t, 0, b] = trt[0] + b1 * cu1
            adj[t, 1, b] = trt[1] + b2 * cu2
            adj[t, 2, b] = trt[2]
            adj[t, 3, b] = -KINETIC[0] * mu1
            adj[t, 4, b] = -KINETIC[1] * mu2
            adj[t, 5, b] = trt[5] + (HEAT_EXPONENT[0] * y1 * b1 * cu1 + HEAT_EXPONENT[1] * y2 * b2 * cu2)
        return carry

    lax.fori_loop(0, inst, spatial_body, 0)

    @pl.when(sec == 1)
    def _():
        def purge_body(t, carry):
            srcs = [lax.rem(b + plan[t, b], beds) for b in range(beds)]
            opens = [jnp.full((1, nr), valve[t, b], jnp.int32) != 0 for b in range(beds)]
            for c in range(3):
                ys = [st[t, c, b, nz - 1 : nz, :] for b in range(beds)]
                ls = [ad[t, c, b, nz - 1 : nz, :] for b in range(beds)]
                for b in range(beds):
                    inc = jnp.zeros((1, nr), jnp.float32)
                    for bp in range(beds):
                        inc = inc + jnp.where(srcs[b] == bp, ys[bp], 0.0)
                    term = jnp.where(opens[b], PURGE_GAIN * (ys[b] - inc), 0.0)
                    res[t, c, b, nz - 1 : nz, :] = res[t, c, b, nz - 1 : nz, :] + term
                    back = jnp.where(opens[b], PURGE_GAIN * ls[b], 0.0)
                    for bb in range(beds):
                        hit = jnp.logical_and(opens[bb], srcs[bb] == b)
                        back = back - jnp.where(hit, PURGE_GAIN * ls[bb], 0.0)
                    adj[t, c, b, nz - 1 : nz, :] = adj[t, c, b, nz - 1 : nz, :] + back
            return carry

        lax.fori_loop(0, inst, purge_body, 0)

    def time_pass(cross_right, use_far, comp_index=None, arrays=(0, 1)):
        srcs = ((st, rv_st, res, 1.0), (ad, rv_ad, adj, -1.0))

        def body(c, carry):
            for which in arrays:
                own, recvd, out, scale = srcs[which]
                for t in range(inst):
                    acc = None
                    for k, w in enumerate(STENCIL):
                        s = k + 1
                        d = None
                        for j, sign in ((t + s, 1.0), (t - s, -1.0)):
                            if j >= inst:
                                far = cross_right
                            elif j < 0:
                                far = not cross_right
                            else:
                                far = False
                            if far != use_far:
                                continue
                            if j >= inst:
                                x = recvd[1, j - inst, c]
                            elif j < 0:
                                x = recvd[0, j + inst, c]
                            else:
                                x = own[j, c]
                            if sign < 0:
                                x = -x
                            d = x if d is None else d + x
                        if d is None:
                            continue
                        acc = w * d if acc is None else acc + w * d
                    if acc is None:
                        continue
                    if scale > 0:
                        out[t, c] = TIME_SCALE * acc + out[t, c]
                    else:
                        out[t, c] = out[t, c] - TIME_SCALE * acc
            return carry

        if comp_index is None:
            lax.fori_loop(0, comp, body, 0)
        else:
            body(comp_index, 0)

    near_st.wait_recv()
    near_ad.wait_recv()

    @pl.when(core == 0)
    def _():
        time_pass(False, False)

    @pl.when(core == 1)
    def _():
        time_pass(True, False)

    for i in range(2):
        def far_body(c, carry, i=i):
            far_descs(c)[i].wait_recv()

            @pl.when(core == 0)
            def _():
                time_pass(False, True, c, (i,))

            @pl.when(core == 1)
            def _():
                time_pass(True, True, c, (i,))

            return carry

        lax.fori_loop(0, comp, far_body, 0)

    def drain(c, carry):
        for cp in far_descs(c):
            cp.wait_send()
        return carry

    lax.fori_loop(0, comp, drain, 0)
    for cp in halo_copies + [near_st, near_ad]:
        cp.wait_send()


def local(state, adjoint, plan, valve):
    n_tm = lax.axis_size("tm")
    inst, comp, beds, nz, nr = state.shape
    block = jax.ShapeDtypeStruct(state.shape, jnp.float32)
    vmem = pl.BlockSpec(memory_space=pltpu.VMEM)
    halo_shape = (inst, comp, beds, 8, nr)

    def kern(*refs):
        _kernel(n_tm, *refs)

    both = pl.pallas_call(
        kern,
        out_shape=pltpu.VMEM((2,) + state.shape, jnp.float32),
        in_specs=[pl.BlockSpec(memory_space=pltpu.SMEM)] * 2 + [pl.BlockSpec(memory_space=pl.ANY)] * 2,
        out_specs=vmem,
        scratch_shapes=[pltpu.VMEM(state.shape, jnp.float32)] * 2
        + [pltpu.VMEM((2,) + state.shape, jnp.float32)] * 2
        + [pltpu.VMEM(halo_shape, jnp.float32)] * 2
        + [pltpu.SemaphoreType.DMA((6 + 2 * comp,)), pltpu.SemaphoreType.DMA((6 + 2 * comp,))]
        + [pltpu.SemaphoreType.DMA((2,))],
        compiler_params=pltpu.CompilerParams(collective_id=0, has_side_effects=True),
    )(plan, valve, state, adjoint)
    return both[0], both[1]


def solution(mesh):
    return jax.shard_map(
        local,
        mesh=mesh,
        in_specs=(
            P("tm", None, None, "sec", None),
            P("tm", None, None, "sec", None),
            P("tm", None),
            P("tm", None),
        ),
        out_specs=(P("tm", None, None, "sec", None), P("tm", None, None, "sec", None)),
        check_vma=False,
    )
```
